32 devices in a mesh: dp: 2 (over x), row: 4 (over y, core), col: 4 (over z).
Axes of the slice: x: 2, y: 2, z: 4, core: 2. Of those that a mesh axis runs over, the one named last changes fastest.
Arguments:
- images: bfloat16 [2, 2, 64, 64, 768], P(None, 'dp', 'row', 'col'), may hold values from -6 to 6
- qkv_weight: bfloat16 [768, 2304], P(('dp', 'row', 'col')), may hold values from -0.21875 to 0.21875
- qv_bias: bfloat16 [1536], P(('dp', 'row', 'col')), may hold values from -1.5 to 1.5
- proj_weight: bfloat16 [768, 768], P(('dp', 'row', 'col')), may hold values from -1.5 to 1.5
- proj_bias: bfloat16 [768], P(('dp', 'row', 'col')), may hold values from -1.5 to 1.5
- pre_gain: bfloat16 [768], P(('dp', 'row', 'col')), may hold values from 0.5 to 1.5
- pre_shift: bfloat16 [768], P(('dp', 'row', 'col')), may hold values from -1.5 to 1.5
- mid_gain: bfloat16 [768], P(('dp', 'row', 'col')), may hold values from 0.5 to 1.5
- mid_shift: bfloat16 [768], P(('dp', 'row', 'col')), may hold values from -1.5 to 1.5
- up_weight: bfloat16 [768, 3072], P(('dp', 'row', 'col')), may hold values from -0.21875 to 0.21875
- up_bias: bfloat16 [3072], P(('dp', 'row', 'col')), may hold values from -1.5 to 1.5
- down_weight: bfloat16 [3072, 768], P(('dp', 'row', 'col')), may hold values from -0.109375 to 0.109375
- down_bias: bfloat16 [768], P(('dp', 'row', 'col')), may hold values from -1.5 to 1.5
- rel_rows: bfloat16 [27, 64], replicated, may hold values from -0.5 to 0.5
- rel_cols: bfloat16 [27, 64], replicated, may hold values from -0.5 to 0.5
- cotangent: bfloat16 [2, 2, 64, 64, 768], P(None, 'dp', 'row', 'col'), may hold values from -6 to 6
Outputs:
- out: bfloat16 [2, 2, 64, 64, 768], P(None, 'dp', 'row', 'col')
- images_grad: float32 [2, 2, 64, 64, 768], P(None, 'dp', 'row', 'col')
- qkv_weight_grad: float32 [768, 2304], P(('dp', 'row', 'col'))
- qv_bias_grad: float32 [1536], P(('dp', 'row', 'col'))
- proj_weight_grad: float32 [768, 768], P(('dp', 'row', 'col'))
- proj_bias_grad: float32 [768], P(('dp', 'row', 'col'))
- pre_gain_grad: float32 [768], P(('dp', 'row', 'col'))
- pre_shift_grad: float32 [768], P(('dp', 'row', 'col'))
- mid_gain_grad: float32 [768], P(('dp', 'row', 'col'))
- mid_shift_grad: float32 [768], P(('dp', 'row', 'col'))
- up_weight_grad: float32 [768, 3072], P(('dp', 'row', 'col'))
- up_bias_grad: float32 [3072], P(('dp', 'row', 'col'))
- down_weight_grad: float32 [3072, 768], P(('dp', 'row', 'col'))
- down_bias_grad: float32 [768], P(('dp', 'row', 'col'))
- rel_rows_grad: float32 [27, 64], replicated
- rel_cols_grad: float32 [27, 64], replicated
The draws below stay inside these ranges and needn't reach their ends.
All inputs are finite; a program needn't handle non-finite values.
Results may differ from the reference program's by a relative error of at most 0.013.
Values may be sent and summed in bfloat16 or wider, within the bound.
No kernel may reach another device: no remote copies, remote signals or barrier semaphores. Data moves between devices by JAX's collectives and lax.ppermute only.
A program may use at most 384 MiB of HBM per device.

```python
import jax
import jax.numpy as jnp
from jax import lax

D = 768
HEADS = 12
HEAD = 64
FF = 3072
GRID = 64
WIN = 14
MICRO = 2
IMAGES = 2
NWIN = 5
RELN = 27


def block_scale(key, dims, split, smallest, largest):
    gain = 1.0
    for axis_at, blocks in split:
        draws = jax.random.uniform(jax.random.fold_in(jax.random.fold_in(key, 6), axis_at), (blocks,), jnp.float32, smallest / len(split), largest / len(split))
        gain = gain * jnp.repeat(jnp.exp(draws), dims[axis_at] // blocks).reshape((-1,) + (1,) * (len(dims) - 1 - axis_at))
    return gain


def normal_values(key, dims, spread, limit, shards=(), held_as=jnp.bfloat16):
    array = spread * jax.random.normal(key, dims, jnp.float32)
    if shards:
        array = array * block_scale(key, dims, shards, -0.22, 0.18)
    return jnp.clip(array, -limit, limit).astype(held_as)


def setup_inputs(seed: int = 0) -> dict:
    arg_keys = jax.random.split(jax.random.key(seed), 17)
    images = normal_values(arg_keys[0], (MICRO, IMAGES, GRID, GRID, D), 1.0, 6.0, ((1, 2), (2, 4), (3, 4)))
    qkv_weight = normal_values(arg_keys[1], (D, 3 * D), D ** -0.5, 0.21875, ((0, 32),))
    qv_bias = normal_values(arg_keys[2], (2 * D,), 0.3, 1.5, ((0, 32),))
    proj_weight = normal_values(arg_keys[3], (D, D), (D // 48) ** -0.5, 1.5, ((0, 32),))
    proj_bias = normal_values(arg_keys[4], (D,), 0.3, 1.5, ((0, 32),))
    pre_gain = jnp.clip(1.0 + 0.1 * jax.random.normal(arg_keys[5], (D,), jnp.float32), 0.5, 1.5).astype(jnp.bfloat16)
    pre_shift = normal_values(arg_keys[6], (D,), 0.3, 1.5, ((0, 32),))
    mid_gain = jnp.clip(1.0 + 0.1 * jax.random.normal(arg_keys[7], (D,), jnp.float32), 0.5, 1.5).astype(jnp.bfloat16)
    mid_shift = normal_values(arg_keys[8], (D,), 0.3, 1.5, ((0, 32),))
    up_weight = normal_values(arg_keys[9], (D, FF), D ** -0.5, 0.21875, ((0, 32),))
    up_bias = normal_values(arg_keys[10], (FF,), 0.3, 1.5, ((0, 32),))
    down_weight = normal_values(arg_keys[11], (FF, D), FF ** -0.5, 0.109375, ((0, 32),))
    down_bias = normal_values(arg_keys[12], (D,), 0.3, 1.5, ((0, 32),))
    rel_rows = normal_values(arg_keys[13], (RELN, HEAD), 0.08, 0.5)
    rel_cols = normal_values(arg_keys[14], (RELN, HEAD), 0.08, 0.5)
    cotangent = normal_values(arg_keys[15], (MICRO, IMAGES, GRID, GRID, D), 1.0, 6.0, ((1, 2), (2, 4), (3, 4)))
    return {"images": images, "qkv_weight": qkv_weight, "qv_bias": qv_bias, "proj_weight": proj_weight, "proj_bias": proj_bias, "pre_gain": pre_gain, "pre_shift": pre_shift, "mid_gain": mid_gain, "mid_shift": mid_shift, "up_weight": up_weight, "up_bias": up_bias, "down_weight": down_weight, "down_bias": down_bias, "rel_rows": rel_rows, "rel_cols": rel_cols, "cotangent": cotangent}


@jax.custom_vjp
def low(v):
    return lax.optimization_barrier(v.astype(jnp.bfloat16)).astype(jnp.float32)

@jax.custom_vjp
def low_back(v):
    return v

def low_keep(v):
    return (low(v), None)

def low_pass(kept, grad):
    return (grad,)

def back_keep(v):
    return (v, None)

def back_low(kept, grad):
    return (low(grad),)
low.defvjp(low_keep, low_pass)
low_back.defvjp(back_keep, back_low)
exact_prec = lax.Precision.HIGHEST
epsilon = 1e-06

def layer_norm(values, gain_vec, shift_vec):
    center = values - lax.optimization_barrier(jnp.mean(values, axis=-1, keepdims=True))
    inverse = lax.rsqrt(lax.optimization_barrier(jnp.mean(center * center, axis=-1, keepdims=True)) + epsilon)
    return center * inverse * gain_vec + shift_vec

def rel_table(table_rows):
    places = jnp.arange(WIN)
    offsets = places[:, None] - places[None, :] + WIN - 1
    return table_rows[offsets]

def forward_image(pixels, params):
    qkv_weight, qv_bias, proj_weight, proj_bias, pre_gain, pre_shift, mid_gain, mid_shift, up_weight, up_bias, down_weight, down_bias, rel_rows, rel_cols = params
    hidden = low_back(low(layer_norm(pixels, pre_gain, pre_shift)))
    pad_extra = NWIN * WIN - GRID
    padded_side = NWIN * WIN
    window_count = NWIN * NWIN
    padded = jnp.pad(hidden, ((0, pad_extra), (0, pad_extra), (0, 0)))
    windows = padded.reshape(NWIN, WIN, NWIN, WIN, D).transpose(0, 2, 1, 3, 4).reshape(window_count, WIN * WIN, D)
    full_bias = jnp.concatenate([qv_bias[:D], jnp.zeros((D,), jnp.float32), qv_bias[D:]])
    qkv_rows = low_back(low(jnp.matmul(windows, qkv_weight, precision=exact_prec) + full_bias))
    qkv_rows = qkv_rows.reshape(window_count, WIN * WIN, 3, HEADS, HEAD)
    queries = qkv_rows[:, :, 0]
    key_rows = qkv_rows[:, :, 1]
    value_rows = qkv_rows[:, :, 2]
    scores = jnp.einsum('nqhc,nkhc->nhqk', queries, key_rows, precision=exact_prec) * HEAD ** (-0.5)
    grid_queries = queries.reshape(window_count, WIN, WIN, HEADS, HEAD)
    along_rows = jnp.einsum('nxyhc,xkc->nhxyk', grid_queries, rel_table(rel_rows), precision=exact_prec)
    along_cols = jnp.einsum('nxyhc,ykc->nhxyk', grid_queries, rel_table(rel_cols), precision=exact_prec)
    scores = scores.reshape(window_count, HEADS, WIN, WIN, WIN, WIN) + along_rows[..., :, None] + along_cols[..., None, :]
    scores = low_back(scores.reshape(window_count, HEADS, WIN * WIN, WIN * WIN))
    attention = low(jax.nn.softmax(scores, axis=-1))
    attended = jnp.einsum('nhqk,nkhc->nqhc', attention, value_rows, precision=exact_prec).reshape(window_count, WIN * WIN, D)
    attended = low_back(low(attended))
    attended = attended.reshape(NWIN, NWIN, WIN, WIN, D).transpose(0, 2, 1, 3, 4).reshape(padded_side, padded_side, D)
    attended = attended[:GRID, :GRID]
    branch = low_back(jnp.matmul(attended, proj_weight, precision=exact_prec) + proj_bias)
    middle = pixels + branch
    second = low(layer_norm(middle, mid_gain, mid_shift))
    inner_act = low_back(jnp.matmul(second, up_weight, precision=exact_prec) + up_bias)
    active = low(jax.nn.gelu(inner_act, approximate=False))
    return middle + jnp.matmul(active, down_weight, precision=exact_prec) + down_bias

def reference(images, qkv_weight, qv_bias, proj_weight, proj_bias, pre_gain, pre_shift, mid_gain, mid_shift, up_weight, up_bias, down_weight, down_bias, rel_rows, rel_cols, cotangent):
    params = (qkv_weight.astype(jnp.float32), qv_bias.astype(jnp.float32), proj_weight.astype(jnp.float32), proj_bias.astype(jnp.float32), pre_gain.astype(jnp.float32), pre_shift.astype(jnp.float32), mid_gain.astype(jnp.float32), mid_shift.astype(jnp.float32), up_weight.astype(jnp.float32), up_bias.astype(jnp.float32), down_weight.astype(jnp.float32), down_bias.astype(jnp.float32), rel_rows.astype(jnp.float32), rel_cols.astype(jnp.float32))
    flat_images = images.reshape(-1, GRID, GRID, D)
    flat_cotangent = cotangent.reshape(-1, GRID, GRID, D)
    zero_grads = jax.tree.map(jnp.zeros_like, params)

    def per_image(totals, paired):
        pixels, incoming = paired
        result, pull = jax.vjp(forward_image, pixels.astype(jnp.float32), params)
        pixel_grad, param_grads = pull(incoming.astype(jnp.float32))
        return (jax.tree.map(jnp.add, totals, param_grads), (result.astype(jnp.bfloat16), pixel_grad))
    totals, (outputs, pixel_grads) = lax.scan(per_image, zero_grads, (flat_images, flat_cotangent))
    return (outputs.reshape(images.shape), pixel_grads.reshape(images.shape), totals[0], totals[1], totals[2], totals[3], totals[4], totals[5], totals[6], totals[7], totals[8], totals[9], totals[10], totals[11], totals[12], totals[13])
```

```python
import math

import jax
import jax.numpy as jnp
import numpy as np
from jax import lax
from jax.experimental import pallas as pl
from jax.experimental.pallas import tpu as pltpu
from jax.sharding import PartitionSpec as P

HEAD = 64
WIN = 14
GRID = 64
NWIN = 5
PITCH = 16
KEYS = WIN * PITCH
LANES = 128
ROWFIELD, COLFIELD, LOWFIELD, MASKLANE = 0, 14, 28, 56
COLTABLE = 32
NEG = -1e30
EDGE = GRID - WIN * (NWIN - 1)
epsilon = 1e-06
bf16 = jnp.bfloat16
f32 = jnp.float32


def dot_nn(a, b):
    return lax.dot_general(a, b, (((1,), (0,)), ((), ())), preferred_element_type=f32)


def dot_nt(a, b):
    return lax.dot_general(a, b, (((1,), (1,)), ((), ())), preferred_element_type=f32)


def dot_tn(a, b):
    return lax.dot_general(a, b, (((0,), (0,)), ((), ())), preferred_element_type=f32)


def key_fields():
    ahead = np.zeros((KEYS, HEAD), np.float32)
    back = np.zeros((KEYS, HEAD), np.float32)
    for a in range(WIN):
        for b in range(PITCH):
            t = PITCH * a + b
            if b < WIN:
                for low in (0, LOWFIELD):
                    ahead[t, low + ROWFIELD + a] = 1
                    ahead[t, low + COLFIELD + b] = 1
                back[t, ROWFIELD + WIN - 1 - a] = 1
                back[t, COLFIELD + WIN - 1 - b] = 1
            else:
                ahead[t, MASKLANE] = NEG
    both = lambda x: jnp.asarray(np.concatenate([x, x], 1), bf16)
    return both(ahead), both(back)


def table_matrix(row_tab, col_tab, reverse):
    half = jnp.zeros((HEAD, HEAD), bf16)
    a, b = (row_tab[::-1], col_tab[::-1]) if reverse else (row_tab, col_tab)
    half = half.at[:, : 2 * WIN - 1].set(a.T).at[:, COLTABLE : COLTABLE + 2 * WIN - 1].set(b.T)
    none = jnp.zeros_like(half)
    return jnp.concatenate(
        [jnp.concatenate([none, half], 1), jnp.concatenate([half, none], 1)], 0
    )


def lane_in(shape, start, count):
    lane = lax.broadcasted_iota(jnp.int32, shape, 1) % HEAD
    return (lane >= start) & (lane < start + count)


def query_fields(q2, table):
    turned = dot_nn(q2, table)
    parts = []
    shape = (PITCH, LANES)
    in_rows = lane_in(shape, ROWFIELD, WIN)
    in_cols = lane_in(shape, COLFIELD, WIN)
    for a in range(q2.shape[0] // PITCH):
        t = turned[PITCH * a : PITCH * (a + 1)]
        r = pltpu.roll(t, (a - WIN + 1) % LANES, 1)
        c = pltpu.roll(t, LANES - (COLTABLE + 2 * WIN - 2 - (WIN - 1) - COLFIELD), 1, stride=1, stride_axis=0)
        parts.append(jnp.where(in_rows, r, jnp.where(in_cols, c, 0.0)))
    full = jnp.concatenate(parts, 0)
    high = full.astype(bf16).astype(f32)
    low = pltpu.roll(full - high, LOWFIELD, 1)
    one = jnp.where(lane_in(full.shape, MASKLANE, 1), 1.0, 0.0)
    return (high + low + one).astype(bf16)


def field_tables(fields):
    parts = []
    shape = (PITCH, LANES)
    in_rows = lane_in(shape, ROWFIELD, WIN)
    in_cols = lane_in(shape, COLFIELD, WIN)
    for a in range(fields.shape[0] // PITCH):
        t = fields[PITCH * a : PITCH * (a + 1)]
        r = jnp.where(in_rows, t, 0.0)
        c = jnp.where(in_cols, t, 0.0)
        r = pltpu.roll(r, a, 1) if a else r
        c = pltpu.roll(c, COLTABLE - COLFIELD, 1, stride=1, stride_axis=0)
        parts.append(r + c)
    return jnp.concatenate(parts, 0)


def first_half(shape, axis):
    return lax.broadcasted_iota(jnp.int32, shape, axis) < HEAD


def padded_rows(block, fill):
    if block.shape[0] == KEYS:
        return block
    rest = (KEYS - block.shape[0], LANES)
    return jnp.concatenate([block, jnp.broadcast_to(fill, rest).astype(block.dtype)], 0)


def attend_kernel(slots, q_ref, k_ref, v_ref, vb_ref, tab_ref, kf_ref, att_ref, lse_ref):
    kf = kf_ref[...]
    for s, (row, count, lane0) in enumerate(slots):
        rows = pl.ds(row, count)
        q2 = q_ref[rows, :]
        k2 = padded_rows(k_ref[rows, :] * bf16(HEAD ** -0.5), jnp.zeros((1, LANES), bf16))
        v2 = padded_rows(v_ref[rows, :], vb_ref[0:1, :])
        x2 = query_fields(q2, tab_ref[s])
        left = first_half((count, LANES), 1)
        leftk = first_half((KEYS, LANES), 1)
        outs = []
        for e in range(2):
            qa = jnp.where(left, q2, x2) if e == 0 else jnp.where(left, x2, q2)
            ka = jnp.where(leftk, k2, kf) if e == 0 else jnp.where(leftk, kf, k2)
            one = jnp.ones((KEYS, LANES), bf16)
            va = jnp.where(leftk, v2, one) if e == 0 else jnp.where(leftk, one, v2)
            st = dot_nt(ka, qa)
            peak = jnp.max(st, axis=0, keepdims=True)
            pt = jnp.exp(st - peak).astype(bf16)
            ot = dot_tn(va, pt)
            mass = ot[HEAD : HEAD + 1] if e == 0 else ot[0:1]
            lse_ref[0, e : e + 1, lane0 : lane0 + count] = peak + jnp.log(mass)
            outs.append(ot * (1.0 / mass))
        both = jnp.where(first_half((LANES, count), 0), outs[0], outs[1])
        att_ref[rows, :] = both.T.astype(bf16)


def attend_back_kernel(
    slots, q_ref, k_ref, v_ref, do_ref, lse_ref, vb_ref, tab_ref, tabb_ref, kf_ref, kb_ref,
    dqkv_ref, dtab_ref, dvb_ref,
):
    kf = kf_ref[...]
    kb = kb_ref[...]
    extra = jnp.zeros((1, LANES), f32)

    @pl.when(pl.program_id(0) == 0)
    def _():
        dtab_ref[...] = jnp.zeros_like(dtab_ref)

    for s, (row, count, lane0) in enumerate(slots):
        rows = pl.ds(row, count)
        q2 = q_ref[rows, :]
        do2 = do_ref[rows, :]
        k2 = padded_rows(k_ref[rows, :] * bf16(HEAD ** -0.5), jnp.zeros((1, LANES), bf16))
        v2 = padded_rows(v_ref[rows, :], vb_ref[0:1, :])
        x2 = query_fields(q2, tab_ref[s])
        left = first_half((count, LANES), 1)
        leftk = first_half((KEYS, LANES), 1)
        zero = jnp.zeros((KEYS, LANES), bf16)
        dq, dk, dv = [], [], []
        for e in range(2):
            qa = jnp.where(left, q2, x2) if e == 0 else jnp.where(left, x2, q2)
            ka = jnp.where(leftk, k2, kf) if e == 0 else jnp.where(leftk, kf, k2)
            kr = jnp.where(leftk, k2, kb) if e == 0 else jnp.where(leftk, kb, k2)
            va = jnp.where(leftk, v2, zero) if e == 0 else jnp.where(leftk, zero, v2)
            st = dot_nt(ka, qa)
            pt = jnp.exp(st - lse_ref[0, e : e + 1, lane0 : lane0 + count])
            dpt = dot_nt(va, do2)
            mean = jnp.sum(pt * dpt, axis=0, keepdims=True)
            dst = (pt * (dpt - mean)).astype(bf16)
            dv.append(dot_nn(pt.astype(bf16), do2))
            dk.append(dot_nn(dst, qa))
            dq.append(dot_tn(dst, kr))
        fields = jnp.where(left, dq[1], dq[0])
        dt = field_tables(fields)
        high = dt.astype(bf16)
        low = (dt - high.astype(f32)).astype(bf16)
        tabb = tabb_ref[s]
        dq2 = jnp.where(left, dq[0], dq[1]) + dot_nt(high, tabb) + dot_nt(low, tabb)
        dk2 = jnp.where(leftk, dk[0], dk[1]) * (HEAD ** -0.5)
        dv2 = jnp.where(leftk, dv[0], dv[1])
        dqkv_ref[0, rows, :] = dq2.astype(bf16)
        dqkv_ref[1, rows, :] = dk2[:count].astype(bf16)
        dqkv_ref[2, rows, :] = dv2[:count].astype(bf16)
        if count < KEYS:
            extra = extra + jnp.sum(dv2[count:], axis=0, keepdims=True)
        dtab_ref[s] += dot_tn(q2, high) + dot_tn(q2, low)
    dvb_ref[0] = jnp.broadcast_to(extra, (8, LANES))


def slot_places(counts):
    places, row, lane = [], 0, 0
    for count in counts:
        places.append((row, count, lane))
        row += count
        lane += -(-count // LANES) * LANES
    return tuple(places), row, lane


def attend(projected, bias_v, tables, counts):
    slots, rows, lanes = slot_places(counts)
    width = projected.shape[1] // 3
    pairs = width // LANES
    kf, _ = key_fields()
    col = lambda off: pl.BlockSpec((rows, LANES), lambda p: (0, off * pairs + p))
    return pl.pallas_call(
        lambda *refs: attend_kernel(slots, *refs),
        grid=(pairs,),
        in_specs=[
            col(0), col(1), col(2),
            pl.BlockSpec((8, LANES), lambda p: (0, p)),
            pl.BlockSpec((len(counts), LANES, LANES), lambda p: (0, 0, 0)),
            pl.BlockSpec((KEYS, LANES), lambda p: (0, 0)),
        ],
        out_specs=[
            pl.BlockSpec((rows, LANES), lambda p: (0, p)),
            pl.BlockSpec((1, 8, lanes), lambda p: (p, 0, 0)),
        ],
        out_shape=[
            jax.ShapeDtypeStruct((rows, width), bf16),
            jax.ShapeDtypeStruct((pairs, 8, lanes), f32),
        ],
        compiler_params=pltpu.CompilerParams(vmem_limit_bytes=48 << 20),
        name="attend",
    )(projected, projected, projected, bias_v, tables, kf)


def attend_back(projected, upstream, lse, bias_v, tables, tables_back, counts):
    slots, rows, lanes = slot_places(counts)
    width = projected.shape[1] // 3
    pairs = width // LANES
    kf, kb = key_fields()
    col = lambda off: pl.BlockSpec((rows, LANES), lambda p: (0, off * pairs + p))
    n = len(counts)
    return pl.pallas_call(
        lambda *refs: attend_back_kernel(slots, *refs),
        grid=(pairs,),
        in_specs=[
            col(0), col(1), col(2), col(0),
            pl.BlockSpec((1, 8, lanes), lambda p: (p, 0, 0)),
            pl.BlockSpec((8, LANES), lambda p: (0, p)),
            pl.BlockSpec((n, LANES, LANES), lambda p: (0, 0, 0)),
            pl.BlockSpec((n, LANES, LANES), lambda p: (0, 0, 0)),
            pl.BlockSpec((KEYS, LANES), lambda p: (0, 0)),
            pl.BlockSpec((KEYS, LANES), lambda p: (0, 0)),
        ],
        out_specs=[
            pl.BlockSpec((3, rows, LANES), lambda p: (0, 0, p)),
            pl.BlockSpec((n, LANES, LANES), lambda p: (0, 0, 0)),
            pl.BlockSpec((1, 8, LANES), lambda p: (p, 0, 0)),
        ],
        out_shape=[
            jax.ShapeDtypeStruct((3, rows, width), bf16),
            jax.ShapeDtypeStruct((n, LANES, LANES), f32),
            jax.ShapeDtypeStruct((pairs, 8, LANES), f32),
        ],
        compiler_params=pltpu.CompilerParams(vmem_limit_bytes=48 << 20),
        name="attend_back",
    )(projected, projected, projected, upstream, lse, bias_v, tables, tables_back, kf, kb)


def sides(index):
    return WIN * index, min(WIN * index + WIN, GRID)


class Plan:
    def __init__(self, rows, cols, images):
        self.rows, self.cols, self.images = rows, cols, images
        self.devices = rows * cols
        self.tile_rows, self.tile_cols = GRID // rows, GRID // cols
        self.tokens = images * self.tile_rows * self.tile_cols
        kinds = ([], [], [])
        for n in range(images):
            for i in range(NWIN):
                for j in range(NWIN):
                    kinds[(i == NWIN - 1) + (j == NWIN - 1)].append((n, i, j))
        self.caps = tuple(-(-len(kind) // self.devices) for kind in kinds)
        self.parts = {w: self._sources(w) for kind in kinds for w in kind}
        owner = self._assign(kinds)
        self.counts = (KEYS,) * self.caps[0] + (EDGE * PITCH,) * (self.caps[1] + self.caps[2])
        _, self.window_rows, _ = slot_places(self.counts)
        self._tables(kinds, owner)

    def _distance(self, one, two):
        r, c = divmod(one, self.cols)
        q, e = divmod(two, self.cols)
        return abs(c - e) + abs(r // 2 - q // 2) + (0.125 if r % 2 != q % 2 else 0.0)

    def _sources(self, window):
        _, i, j = window
        (r0, r1), (c0, c1) = sides(i), sides(j)
        tr, tc = self.tile_rows, self.tile_cols
        found = {}
        for r in range(r0 // tr, (r1 - 1) // tr + 1):
            for c in range(c0 // tc, (c1 - 1) // tc + 1):
                high = min(r1, (r + 1) * tr) - max(r0, r * tr)
                wide = min(c1, (c + 1) * tc) - max(c0, c * tc)
                found[r * self.cols + c] = high * wide
        return found

    def _rounds(self, owner):
        pairs = {}
        for window, dev in owner.items():
            for source, amount in self.parts[window].items():
                if source != dev:
                    pairs[source, dev] = pairs.get((source, dev), 0) + amount
        rounds = []
        for pair, amount in sorted(pairs.items(), key=lambda p: (-p[1], p[0])):
            for senders, takers, members in rounds:
                if pair[0] not in senders and pair[1] not in takers:
                    break
            else:
                senders, takers, members = set(), set(), []
                rounds.append((senders, takers, members))
            senders.add(pair[0])
            takers.add(pair[1])
            members.append(pair)
        return pairs, [members for _, _, members in rounds]

    def _cost(self, owner):
        pairs, rounds = self._rounds(owner)
        moved = sum(amount * self._distance(*pair) for pair, amount in pairs.items())
        return moved / 4 + sum(64 + max(pairs[p] for p in members) for members in rounds)

    def _assign(self, kinds):
        owner = {}
        room = {}
        for kind, windows in enumerate(kinds):
            room[kind] = [self.caps[kind]] * self.devices
            for window in sorted(windows, key=lambda w: (-(w[1] + w[2]), w)):
                far = lambda d: sum(t * self._distance(s, d) for s, t in self.parts[window].items())
                dev = min((d for d in range(self.devices) if room[kind][d]), key=lambda d: (far(d), d))
                owner[window] = dev
                room[kind][dev] -= 1
        best = self._cost(owner)
        for _ in range(4):
            before = best
            for kind in (1, 2, 0):
                for one in kinds[kind]:
                    for dev in range(self.devices):
                        if dev == owner[one]:
                            continue
                        trials = []
                        if room[kind][dev]:
                            trials.append({**owner, one: dev})
                        for two in kinds[kind]:
                            if owner[two] == dev:
                                trials.append({**owner, one: dev, two: owner[one]})
                        for trial in trials:
                            price = self._cost(trial)
                            if price < best - 1e-9:
                                if sum(trial[w] != owner[w] for w in kinds[kind]) == 1:
                                    room[kind][owner[one]] += 1
                                    room[kind][dev] -= 1
                                owner, best = trial, price
                                break
            if best >= before:
                break
        return owner

    def _tables(self, kinds, owner):
        places, _, _ = slot_places(self.counts)
        starts = (0, self.caps[0], self.caps[0] + self.caps[1])
        self.swapped = np.zeros((self.devices, len(self.counts)), np.int32)
        taken = {}
        moves = {}
        for kind, windows in enumerate(kinds):
            for window in windows:
                n, i, j = window
                dev = owner[window]
                slot = starts[kind] + taken.get((dev, kind), 0)
                taken[dev, kind] = taken.get((dev, kind), 0) + 1
                swap = kind == 1 and j == NWIN - 1
                self.swapped[dev, slot] = swap
                (r0, r1), (c0, c1) = sides(i), sides(j)
                for r in range(r0, r1):
                    for c in range(c0, c1):
                        a, b = (c - c0, r - r0) if swap else (r - r0, c - c0)
                        row = places[slot][0] + PITCH * a + b
                        source = (r // self.tile_rows) * self.cols + c // self.tile_cols
                        token = (n * self.tile_rows + r % self.tile_rows) * self.tile_cols
                        token += c % self.tile_cols
                        moves.setdefault((source, dev), []).append((token, row))
        _, rounds = self._rounds(owner)
        self.perms = rounds
        self.sizes = [-(-max(len(moves[p]) for p in members) // PITCH) * PITCH for members in rounds]
        total = sum(self.sizes)
        self.pack = np.full((self.devices, total), -1, np.int32)
        self.take = np.full((self.devices, self.window_rows), -1, np.int32)
        self.pack_back = np.full((self.devices, total), -1, np.int32)
        self.take_back = np.full((self.devices, self.tokens), -1, np.int32)
        for dev in range(self.devices):
            for token, row in moves.get((dev, dev), ()):
                self.take[dev, row] = token
                self.take_back[dev, token] = row
        at = 0
        for members, size in zip(rounds, self.sizes):
            for source, dev in members:
                for k, (token, row) in enumerate(moves[source, dev]):
                    self.pack[source, at + k] = token
                    self.take[dev, row] = self.tokens + at + k
                    self.pack_back[dev, at + k] = row
                    self.take_back[source, token] = self.window_rows + at + k
            at += size


def chosen(index, start, count):
    spot = lax.broadcasted_iota(jnp.int32, (count, index.shape[1]), 0) + start
    return jnp.where(spot == index, 1.0, 0.0).astype(bf16)


def pack_kernel(sizes, index_ref, tokens_ref, *out_refs):
    at = 0
    tokens = tokens_ref[...].astype(bf16)
    for size, out_ref in zip(sizes, out_refs):
        index = index_ref[0:1, at : at + size]
        out_ref[...] = dot_tn(chosen(index, 0, tokens.shape[0]), tokens).astype(bf16)
        at += size


def pack(index, tokens, sizes):
    return pl.pallas_call(
        lambda *refs: pack_kernel(sizes, *refs),
        out_shape=[jax.ShapeDtypeStruct((size, tokens.shape[1]), bf16) for size in sizes],
        compiler_params=pltpu.CompilerParams(vmem_limit_bytes=40 << 20),
        name="pack",
    )(index[None], tokens)


def take_kernel(index_ref, local_ref, *refs):
    out_ref = refs[-1]
    index = index_ref[...]
    local = local_ref[...]
    hot = chosen(index, 0, local.shape[0])
    total = dot_tn(hot, local.astype(bf16))
    if local.dtype == f32:
        total = total + dot_tn(hot, (local - local.astype(bf16).astype(f32)).astype(bf16))
    at = local.shape[0]
    for ref in refs[:-1]:
        total = total + dot_tn(chosen(index, at, ref.shape[0]), ref[...])
        at += ref.shape[0]
    out_ref[...] = total.astype(out_ref.dtype)


def take(index, local, arrived):
    return pl.pallas_call(
        take_kernel,
        out_shape=jax.ShapeDtypeStruct((index.shape[0], local.shape[1]), local.dtype),
        compiler_params=pltpu.CompilerParams(vmem_limit_bytes=40 << 20),
        name="take",
    )(index[None], local, *arrived)


class Mover:
    def __init__(self, plan):
        self.plan = plan
        here = lax.axis_index("row") * plan.cols + lax.axis_index("col")
        mine = lambda table: lax.dynamic_index_in_dim(jnp.asarray(table), here, 0, keepdims=False)
        self.index = {name: mine(getattr(plan, name)) for name in ("pack", "take", "pack_back", "take_back")}
        self.swapped = mine(plan.swapped)

    def to_windows(self, tokens):
        sent = pack(self.index["pack"], tokens, self.plan.sizes)
        arrived = [lax.ppermute(s, ("row", "col"), perm) for s, perm in zip(sent, self.plan.perms)]
        return take(self.index["take"], tokens, arrived)

    def to_tile(self, rows):
        sent = pack(self.index["pack_back"], rows, self.plan.sizes)
        arrived = [
            lax.ppermute(s, ("row", "col"), [(d, s2) for s2, d in perm])
            for s, perm in zip(sent, self.plan.perms)
        ]
        return take(self.index["take_back"], rows, arrived)


AXES = ("dp", "row", "col")
TORUS = (2, 4, 4)


def over_dp(v):
    return lax.ppermute(v, "dp", [(0, 1), (1, 0)])


def over_y(v):
    return lax.ppermute(v, "row", [(r, (r + 2) % 4) for r in range(4)])


def over_core(v):
    return lax.ppermute(v, "row", [(r, r ^ 1) for r in range(4)])


def over_col(v, steps):
    return lax.ppermute(v, "col", [(c, (c + steps) % 4) for c in range(4)])


def block_at(flip_dp, flip_y, flip_core):
    dp, row = lax.axis_index("dp"), lax.axis_index("row")
    return (
        ((dp + flip_dp) % 2) * 4 + ((row // 2 + flip_y) % 2) * 2 + (row % 2 + flip_core) % 2
    )


def gather_pieces(shard):
    place = lax.axis_index("col")
    seen = [shard] + [over_col(shard, k) for k in (1, 2, 3)]
    column = []
    for j in range(4):
        block = seen[0]
        for k in (1, 2, 3):
            block = jnp.where((place - j) % 4 == k, seen[k], block)
        column.append(block)
    own = jnp.concatenate(column, 0)
    half = shard.shape[1] // 2
    by_dp, by_y = over_dp(own), over_y(own)
    diag_low, diag_high = over_dp(by_y[:, :half]), over_y(by_dp[:, half:])
    pieces = [own, by_dp, by_y, diag_low, diag_high]
    return pieces + [over_core(p) for p in pieces]


def place_kernel(half, *refs):
    pieces, out_ref, sems = refs[:10], refs[10], refs[11]
    copies = []
    for k, piece in enumerate(pieces):
        core, kind = divmod(k, 5)
        block = block_at(kind in (1, 3, 4), kind in (2, 3, 4), core)
        target = out_ref.at[block]
        if kind == 3:
            target = out_ref.at[block, :, pl.ds(0, half)]
        if kind == 4:
            target = out_ref.at[block, :, pl.ds(half, half)]
        copies.append(pltpu.make_async_copy(piece, target, sems.at[k]))
    for copy in copies:
        copy.start()
    for copy in copies:
        copy.wait()


def gather_rows(shard):
    pieces = gather_pieces(shard)
    rows, width = pieces[0].shape
    whole = pl.pallas_call(
        lambda *refs: place_kernel(width // 2, *refs),
        out_specs=pl.BlockSpec(memory_space=pl.ANY),
        out_shape=jax.ShapeDtypeStruct((8, rows, width), shard.dtype),
        scratch_shapes=[pltpu.SemaphoreType.DMA((10,))],
        compiler_params=pltpu.CompilerParams(vmem_limit_bytes=40 << 20),
        name="place",
    )(*pieces)
    return whole.reshape(8 * rows, width)


def scatter_sum(grad):
    rows, width = grad.shape[0] // 8, grad.shape[1]
    half = width // 2
    blocks = grad.reshape(8, rows, width)
    kinds = ((0, 0), (1, 0), (0, 1), (1, 1))
    pick = lambda kind, core: lax.dynamic_index_in_dim(blocks, block_at(*kind, core), 0, False)
    other = over_core(jnp.stack([pick(kind, 1) for kind in kinds]))
    own, to_dp, to_y, diag = [
        pick(kind, 0).astype(f32) + other[k].astype(f32) for k, kind in enumerate(kinds)
    ]
    diag = diag.astype(bf16)
    low, high = over_dp(diag[:, :half]), over_y(diag[:, half:])
    to_dp = jnp.concatenate([to_dp[:, :half], to_dp[:, half:] + high.astype(f32)], 1).astype(bf16)
    to_y = jnp.concatenate([to_y[:, :half] + low.astype(f32), to_y[:, half:]], 1).astype(bf16)
    column = own + over_dp(to_dp).astype(f32) + over_y(to_y).astype(f32)
    column = column.reshape(4, rows // 4, width)
    sent = column.astype(bf16)
    place = lax.axis_index("col")
    total = lax.dynamic_index_in_dim(column, place, 0, False)
    for k in (1, 2, 3):
        step = over_col(lax.dynamic_index_in_dim(sent, (place + k) % 4, 0, False), k)
        total = total + step.astype(f32)
    return total


def tree_sum(value):
    value = value + over_col(value, 1) + over_col(value, 2) + over_col(value, 3)
    value = value + over_dp(value)
    value = value + over_y(value)
    return value + over_core(value)


def on_torus():
    return tuple(lax.axis_size(a) for a in AXES) == TORUS


def device_number():
    return (lax.axis_index("dp") * lax.axis_size("row") + lax.axis_index("row")) * lax.axis_size(
        "col"
    ) + lax.axis_index("col")


def whole_weight(shard):
    if on_torus():
        return gather_rows(shard)
    return lax.all_gather(shard, AXES, axis=0, tiled=True)


def shared_sum(grad):
    if on_torus():
        return scatter_sum(grad.astype(bf16))
    return lax.psum_scatter(grad, AXES, scatter_dimension=0, tiled=True)


def sum_everywhere(value):
    if on_torus():
        return tree_sum(value)
    return lax.psum(value, AXES)


def whole_vectors(shards):
    count = lax.axis_size("dp") * lax.axis_size("row") * lax.axis_size("col")
    packed = jnp.concatenate(shards)
    spot = lax.broadcasted_iota(jnp.int32, (count, packed.shape[0]), 0) == device_number()
    table = sum_everywhere(jnp.where(spot, packed[None], jnp.zeros((), bf16)))
    vectors, at = [], 0
    for shard in shards:
        vectors.append(table[:, at : at + shard.shape[0]].reshape(-1))
        at += shard.shape[0]
    return vectors


def shared_vectors(vectors, tables):
    count = lax.axis_size("dp") * lax.axis_size("row") * lax.axis_size("col")
    flat = jnp.concatenate([v.reshape(-1) for v in (*vectors, *tables)])
    total = sum_everywhere(flat)
    mine, at = [], 0
    for vector in vectors:
        share = vector.shape[0] // count
        mine.append(lax.dynamic_slice(total, (at + device_number() * share,), (share,)))
        at += vector.shape[0]
    full = []
    for table in tables:
        full.append(total[at : at + table.size].reshape(table.shape))
        at += table.size
    return mine, full


def normalize(values):
    center = values - jnp.mean(values, axis=-1, keepdims=True)
    inverse = lax.rsqrt(jnp.mean(center * center, axis=-1, keepdims=True) + epsilon)
    return center * inverse, inverse


def norm_back(upstream, normed, inverse, gain):
    scaled = upstream * gain
    inner = jnp.mean(scaled, axis=-1, keepdims=True)
    cross = jnp.mean(scaled * normed, axis=-1, keepdims=True)
    result = inverse * (scaled - inner - normed * cross)
    return result, jnp.sum(upstream * normed, axis=0), jnp.sum(upstream, axis=0)


def body(
    images, qkv_weight, qv_bias, proj_weight, proj_bias, pre_gain, pre_shift, mid_gain, mid_shift,
    up_weight, up_bias, down_weight, down_bias, rel_rows, rel_cols, cotangent,
):
    width = images.shape[-1]
    plan = plan_for(lax.axis_size("row"), lax.axis_size("col"), images.shape[0] * images.shape[1])
    move = Mover(plan)
    counts = plan.counts
    x_low = move.to_windows(images.reshape(-1, width))
    qkv = whole_weight(qkv_weight)
    vectors = whole_vectors(
        [qv_bias, proj_bias, pre_gain, pre_shift, mid_gain, mid_shift, up_bias, down_bias]
    )
    qv, proj_add, gain_one, shift_one, gain_two, shift_two, up_add, down_add = [
        v.astype(f32) for v in vectors
    ]
    upstream = move.to_windows(cotangent.reshape(-1, width))
    proj = whole_weight(proj_weight)
    up = whole_weight(up_weight)
    down = whole_weight(down_weight)

    swapped = move.swapped[:, None, None] > 0
    ahead = [table_matrix(rel_rows, rel_cols, True), table_matrix(rel_cols, rel_rows, True)]
    back = [table_matrix(rel_rows, rel_cols, False), table_matrix(rel_cols, rel_rows, False)]
    tables = jnp.where(swapped, ahead[1][None], ahead[0][None])
    tables_back = jnp.where(swapped, back[1][None], back[0][None])

    real = (move.index["take"] >= 0)[:, None]
    x = x_low.astype(f32)
    plain_one, inverse_one = normalize(x)
    hidden = jnp.where(real, plain_one * gain_one + shift_one, 0.0).astype(bf16)
    full_bias = jnp.concatenate([qv[:width], jnp.zeros((width,), f32), qv[width:]])
    projected = (jnp.dot(hidden, qkv, preferred_element_type=f32) + full_bias).astype(bf16)
    bias_v = jnp.broadcast_to(qv[None, width:], (8, width)).astype(bf16)
    attended, logsum = attend(projected, bias_v, tables, counts)
    middle = x + jnp.dot(attended, proj, preferred_element_type=f32) + proj_add
    plain_two, inverse_two = normalize(middle)
    second = (plain_two * gain_two + shift_two).astype(bf16)
    inner = jnp.dot(second, up, preferred_element_type=f32) + up_add
    cdf = 0.5 * (1.0 + lax.erf(inner * 2.0 ** (-0.5)))
    pdf = jnp.exp(-0.5 * inner * inner) * (2.0 * math.pi) ** (-0.5)
    active = (inner * cdf).astype(bf16)
    slope = cdf + inner * pdf
    result = middle + jnp.dot(active, down, preferred_element_type=f32) + down_add
    out = move.to_tile(result.astype(bf16))

    flow = upstream.astype(f32)
    down_grad = shared_sum(dot_tn(active, upstream))
    inner_grad = (dot_nt(upstream, down) * slope).astype(bf16)
    up_grad = shared_sum(dot_tn(second, inner_grad))
    second_grad = dot_nt(inner_grad, up)
    part, mid_gain_grad, mid_shift_grad = norm_back(second_grad, plain_two, inverse_two, gain_two)
    middle_grad = flow + part
    branch = middle_grad.astype(bf16)
    proj_grad = shared_sum(dot_tn(attended, branch))
    attended_grad = dot_nt(branch, proj).astype(bf16)
    pieces, table_grads, bias_v_grad = attend_back(
        projected, attended_grad, logsum, bias_v, tables, tables_back, counts
    )
    projected_grad = jnp.concatenate([pieces[0], pieces[1], pieces[2]], 1)
    qkv_grad = shared_sum(dot_tn(hidden, projected_grad))
    hidden_grad = dot_nt(projected_grad, qkv).astype(bf16).astype(f32)
    hidden_grad = jnp.where(real, hidden_grad, 0.0)
    part, pre_gain_grad, pre_shift_grad = norm_back(hidden_grad, plain_one, inverse_one, gain_one)
    images_grad = move.to_tile(middle_grad + part)

    sums = jnp.sum(projected_grad, axis=0, dtype=f32)
    qv_grad = jnp.concatenate(
        [sums[:width], sums[2 * width :] + bias_v_grad[:, 0].reshape(-1)]
    )
    row_part, col_part = table_sums(table_grads)
    swap = move.swapped[:, None, None] > 0
    rows_grad = jnp.sum(jnp.where(swap, col_part, row_part), axis=0)
    cols_grad = jnp.sum(jnp.where(swap, row_part, col_part), axis=0)
    mine, full = shared_vectors(
        [
            qv_grad,
            jnp.sum(branch, axis=0, dtype=f32),
            pre_gain_grad,
            pre_shift_grad,
            mid_gain_grad,
            mid_shift_grad,
            jnp.sum(inner_grad, axis=0, dtype=f32),
            jnp.sum(flow, axis=0),
        ],
        [rows_grad, cols_grad],
    )
    return (
        out.reshape(images.shape),
        images_grad.reshape(images.shape),
        qkv_grad,
        mine[0],
        proj_grad,
        mine[1],
        mine[2],
        mine[3],
        mine[4],
        mine[5],
        up_grad,
        mine[6],
        down_grad,
        mine[7],
        full[0],
        full[1],
    )


def table_sums(grads):
    count = 2 * WIN - 1
    left, right = grads[:, :HEAD, HEAD:], grads[:, HEAD:, :HEAD]
    both = jnp.swapaxes(left + right, 1, 2)
    return both[:, :count], both[:, COLTABLE : COLTABLE + count]


PLANS = {}


def plan_for(rows, cols, images):
    key = (rows, cols, images)
    if key not in PLANS:
        PLANS[key] = Plan(*key)
    return PLANS[key]


def solution(mesh):
    tokens = P(None, "dp", "row", "col", None)
    rows = P(AXES, None)
    vector = P(AXES)
    placed = (
        tokens, rows, vector, rows, vector, vector, vector, vector, vector,
        rows, vector, rows, vector, P(), P(), tokens,
    )
    given = (tokens, tokens, rows, vector, rows, vector, vector, vector, vector, vector,
             rows, vector, rows, vector, P(), P())
    return jax.shard_map(body, mesh=mesh, in_specs=placed, out_specs=given, check_vma=False)
```

```python
import math

import jax
import jax.numpy as jnp
import numpy as np
from jax import lax
from jax.experimental import pallas as pl
from jax.experimental.pallas import tpu as pltpu
from jax.sharding import PartitionSpec as P

HEAD = 64
WIN = 14
GRID = 64
NWIN = 5
PITCH = 16
KEYS = WIN * PITCH
LANES = 128
ROWFIELD, COLFIELD, LOWFIELD, MASKLANE = 0, 14, 28, 56
COLTABLE = 32
NEG = -1e30
COST = 1024
EDGE = GRID - WIN * (NWIN - 1)
epsilon = 1e-06
bf16 = jnp.bfloat16
f32 = jnp.float32


def dot_nn(a, b):
    return lax.dot_general(a, b, (((1,), (0,)), ((), ())), preferred_element_type=f32)


def dot_nt(a, b):
    return lax.dot_general(a, b, (((1,), (1,)), ((), ())), preferred_element_type=f32)


def dot_tn(a, b):
    return lax.dot_general(a, b, (((0,), (0,)), ((), ())), preferred_element_type=f32)


def key_fields(reverse):
    shape = (KEYS, LANES)
    t = lax.broadcasted_iota(jnp.int32, shape, 0)
    a, b = t // PITCH, t % PITCH
    lane = lax.broadcasted_iota(jnp.int32, shape, 1) % HEAD
    if reverse:
        one = (lane == ROWFIELD + WIN - 1 - a) | (lane == COLFIELD + WIN - 1 - b)
        return jnp.where(one & (b < WIN), 1.0, 0.0).astype(bf16)
    one = (lane == ROWFIELD + a) | (lane == LOWFIELD + ROWFIELD + a)
    one = one | (lane == COLFIELD + b) | (lane == LOWFIELD + COLFIELD + b)
    out = jnp.where(one & (b < WIN), 1.0, 0.0)
    return jnp.where((lane == MASKLANE) & (b >= WIN), NEG, out).astype(bf16)


def tables_kernel(swapped_ref, rows_ref, cols_ref, ahead_ref, back_ref):
    shape = (2 * WIN - 1, HEAD)
    index = lax.broadcasted_iota(jnp.int32, shape, 0)
    lane = lax.broadcasted_iota(jnp.int32, shape, 1)
    empty = jnp.zeros((HEAD, HEAD), f32)
    for ref, place in ((ahead_ref, 2 * WIN - 2 - index), (back_ref, index)):
        spots = [jnp.where(lane == place + start, 1.0, 0.0).astype(bf16) for start in (0, COLTABLE)]
        both = []
        for one, two in ((rows_ref, cols_ref), (cols_ref, rows_ref)):
            half = dot_tn(one[...], spots[0]) + dot_tn(two[...], spots[1])
            full = [jnp.concatenate(pair, 1) for pair in ((empty, half), (half, empty))]
            both.append(jnp.concatenate(full, 0).astype(bf16))
        for s in range(ref.shape[0]):

            @pl.when(swapped_ref[s] == 0)
            def _():
                ref[s] = both[0]

            @pl.when(swapped_ref[s] != 0)
            def _():
                ref[s] = both[1]


def position_tables(swapped, rel_rows, rel_cols):
    one = jax.ShapeDtypeStruct((swapped.shape[0], LANES, LANES), bf16)
    return pl.pallas_call(
        tables_kernel,
        grid_spec=pltpu.PrefetchScalarGridSpec(
            num_scalar_prefetch=1,
            grid=(1,),
            in_specs=[pl.BlockSpec(rel_rows.shape, lambda s, w: (0, 0))] * 2,
            out_specs=[pl.BlockSpec(one.shape, lambda s, w: (0, 0, 0))] * 2,
        ),
        out_shape=[one, one],
        name="position_tables",
    )(swapped, rel_rows, rel_cols)


def lane_in(shape, start, count):
    lane = lax.broadcasted_iota(jnp.int32, shape, 1) % HEAD
    return (lane >= start) & (lane < start + count)


def query_fields(q2, table):
    turned = dot_nn(q2, table)
    parts = []
    shape = (PITCH, LANES)
    in_rows = lane_in(shape, ROWFIELD, WIN)
    in_cols = lane_in(shape, COLFIELD, WIN)
    for a in range(q2.shape[0] // PITCH):
        t = turned[PITCH * a : PITCH * (a + 1)]
        r = pltpu.roll(t, (a - WIN + 1) % LANES, 1)
        c = pltpu.roll(t, LANES - (COLTABLE + 2 * WIN - 2 - (WIN - 1) - COLFIELD), 1, stride=1, stride_axis=0)
        parts.append(jnp.where(in_rows, r, jnp.where(in_cols, c, 0.0)))
    full = jnp.concatenate(parts, 0)
    high = full.astype(bf16).astype(f32)
    low = pltpu.roll(full - high, LOWFIELD, 1)
    one = jnp.where(lane_in(full.shape, MASKLANE, 1), 1.0, 0.0)
    return (high + low + one).astype(bf16)


def field_tables(fields):
    parts = []
    shape = (PITCH, LANES)
    in_rows = lane_in(shape, ROWFIELD, WIN)
    in_cols = lane_in(shape, COLFIELD, WIN)
    for a in range(fields.shape[0] // PITCH):
        t = fields[PITCH * a : PITCH * (a + 1)]
        r = jnp.where(in_rows, t, 0.0)
        c = jnp.where(in_cols, t, 0.0)
        r = pltpu.roll(r, a, 1) if a else r
        c = pltpu.roll(c, COLTABLE - COLFIELD, 1, stride=1, stride_axis=0)
        parts.append(r + c)
    return jnp.concatenate(parts, 0)


def first_half(shape, axis):
    return lax.broadcasted_iota(jnp.int32, shape, axis) < HEAD


def padded_rows(block, fill):
    if block.shape[0] == KEYS:
        return block
    rest = (KEYS - block.shape[0], LANES)
    return jnp.concatenate([block, jnp.broadcast_to(fill, rest).astype(block.dtype)], 0)


def attend_kernel(slots, q_ref, k_ref, v_ref, vb_ref, tab_ref, att_ref, lse_ref):
    kf = key_fields(False)
    for s, (row, count, lane0) in enumerate(slots):
        rows = pl.ds(row, count)
        q2 = q_ref[rows, :]
        k2 = padded_rows(k_ref[rows, :] * bf16(HEAD ** -0.5), jnp.zeros((1, LANES), bf16))
        v2 = padded_rows(v_ref[rows, :], vb_ref[0:1, :])
        x2 = query_fields(q2, tab_ref[s])
        left = first_half((count, LANES), 1)
        leftk = first_half((KEYS, LANES), 1)
        outs = []
        for e in range(2):
            qa = jnp.where(left, q2, x2) if e == 0 else jnp.where(left, x2, q2)
            ka = jnp.where(leftk, k2, kf) if e == 0 else jnp.where(leftk, kf, k2)
            one = jnp.ones((KEYS, LANES), bf16)
            va = jnp.where(leftk, v2, one) if e == 0 else jnp.where(leftk, one, v2)
            st = dot_nt(ka, qa)
            peak = jnp.max(st, axis=0, keepdims=True)
            pt = jnp.exp(st - peak).astype(bf16)
            ot = dot_tn(va, pt)
            mass = ot[HEAD : HEAD + 1] if e == 0 else ot[0:1]
            lse_ref[0, e : e + 1, lane0 : lane0 + count] = peak + jnp.log(mass)
            outs.append(ot * (1.0 / mass))
        both = jnp.where(first_half((LANES, count), 0), outs[0], outs[1])
        att_ref[rows, :] = both.T.astype(bf16)


def attend_back_kernel(
    slots, q_ref, k_ref, v_ref, do_ref, lse_ref, vb_ref, tab_ref, tabb_ref,
    dqkv_ref, dtab_ref, dvb_ref,
):
    kf = key_fields(False)
    kb = key_fields(True)
    extra = jnp.zeros((1, LANES), f32)

    @pl.when(pl.program_id(0) == 0)
    def _():
        dtab_ref[...] = jnp.zeros_like(dtab_ref)

    for s, (row, count, lane0) in enumerate(slots):
        rows = pl.ds(row, count)
        q2 = q_ref[rows, :]
        do2 = do_ref[rows, :]
        k2 = padded_rows(k_ref[rows, :] * bf16(HEAD ** -0.5), jnp.zeros((1, LANES), bf16))
        v2 = padded_rows(v_ref[rows, :], vb_ref[0:1, :])
        x2 = query_fields(q2, tab_ref[s])
        left = first_half((count, LANES), 1)
        leftk = first_half((KEYS, LANES), 1)
        zero = jnp.zeros((KEYS, LANES), bf16)
        dq, dk, dv = [], [], []
        for e in range(2):
            qa = jnp.where(left, q2, x2) if e == 0 else jnp.where(left, x2, q2)
            ka = jnp.where(leftk, k2, kf) if e == 0 else jnp.where(leftk, kf, k2)
            kr = jnp.where(leftk, k2, kb) if e == 0 else jnp.where(leftk, kb, k2)
            va = jnp.where(leftk, v2, zero) if e == 0 else jnp.where(leftk, zero, v2)
            st = dot_nt(ka, qa)
            pt = jnp.exp(st - lse_ref[0, e : e + 1, lane0 : lane0 + count])
            dpt = dot_nt(va, do2)
            mean = jnp.sum(pt * dpt, axis=0, keepdims=True)
            dst = (pt * (dpt - mean)).astype(bf16)
            dv.append(dot_nn(pt.astype(bf16), do2))
            dk.append(dot_nn(dst, qa))
            dq.append(dot_tn(dst, kr))
        fields = jnp.where(left, dq[1], dq[0])
        dt = field_tables(fields)
        high = dt.astype(bf16)
        low = (dt - high.astype(f32)).astype(bf16)
        tabb = tabb_ref[s]
        dq2 = jnp.where(left, dq[0], dq[1]) + dot_nt(high, tabb) + dot_nt(low, tabb)
        dk2 = jnp.where(leftk, dk[0], dk[1]) * (HEAD ** -0.5)
        dv2 = jnp.where(leftk, dv[0], dv[1])
        dqkv_ref[0, rows, :] = dq2.astype(bf16)
        dqkv_ref[1, rows, :] = dk2[:count].astype(bf16)
        dqkv_ref[2, rows, :] = dv2[:count].astype(bf16)
        if count < KEYS:
            extra = extra + jnp.sum(dv2[count:], axis=0, keepdims=True)
        dtab_ref[s] += dot_tn(q2, high) + dot_tn(q2, low)
    dvb_ref[0] = jnp.broadcast_to(extra, (8, LANES))


def slot_places(counts):
    places, row, lane = [], 0, 0
    for count in counts:
        places.append((row, count, lane))
        row += count
        lane += -(-count // LANES) * LANES
    return tuple(places), row, lane


def attend(projected, bias_v, tables, counts, first, count):
    slots, rows, lanes = slot_places(counts)
    width = projected.shape[1] // 3
    pairs = width // LANES
    col = lambda off: pl.BlockSpec((rows, LANES), lambda p: (0, off * pairs + first + p))
    return pl.pallas_call(
        lambda *refs: attend_kernel(slots, *refs),
        grid=(count,),
        in_specs=[
            col(0), col(1), col(2),
            pl.BlockSpec((8, LANES), lambda p: (0, first + p)),
            pl.BlockSpec((len(counts), LANES, LANES), lambda p: (0, 0, 0)),
        ],
        out_specs=[
            pl.BlockSpec((rows, LANES), lambda p: (0, p)),
            pl.BlockSpec((1, 8, lanes), lambda p: (p, 0, 0)),
        ],
        out_shape=[
            jax.ShapeDtypeStruct((rows, count * LANES), bf16),
            jax.ShapeDtypeStruct((count, 8, lanes), f32),
        ],
        compiler_params=pltpu.CompilerParams(vmem_limit_bytes=48 << 20),
        cost_estimate=pl.CostEstimate(flops=COST, bytes_accessed=1024, transcendentals=0),
        name="attend",
    )(projected, projected, projected, bias_v, tables)


def attend_back(projected, upstream, lse, bias_v, tables, tables_back, counts, first):
    count = lse.shape[0]
    slots, rows, lanes = slot_places(counts)
    width = projected.shape[1] // 3
    pairs = width // LANES
    col = lambda off: pl.BlockSpec((rows, LANES), lambda p: (0, off * pairs + first + p))
    n = len(counts)
    return pl.pallas_call(
        lambda *refs: attend_back_kernel(slots, *refs),
        grid=(count,),
        in_specs=[
            col(0), col(1), col(2), col(0),
            pl.BlockSpec((1, 8, lanes), lambda p: (p, 0, 0)),
            pl.BlockSpec((8, LANES), lambda p: (0, first + p)),
            pl.BlockSpec((n, LANES, LANES), lambda p: (0, 0, 0)),
            pl.BlockSpec((n, LANES, LANES), lambda p: (0, 0, 0)),
        ],
        out_specs=[
            pl.BlockSpec((3, rows, LANES), lambda p: (0, 0, p)),
            pl.BlockSpec((n, LANES, LANES), lambda p: (0, 0, 0)),
            pl.BlockSpec((1, 8, LANES), lambda p: (p, 0, 0)),
        ],
        out_shape=[
            jax.ShapeDtypeStruct((3, rows, count * LANES), bf16),
            jax.ShapeDtypeStruct((n, LANES, LANES), f32),
            jax.ShapeDtypeStruct((count, 8, LANES), f32),
        ],
        compiler_params=pltpu.CompilerParams(vmem_limit_bytes=48 << 20),
        cost_estimate=pl.CostEstimate(flops=COST, bytes_accessed=1024, transcendentals=0),
        name="attend_back",
    )(projected, projected, projected, upstream, lse, bias_v, tables, tables_back)


def sides(index):
    return WIN * index, min(WIN * index + WIN, GRID)


class Plan:
    def __init__(self, rows, cols, images):
        self.rows, self.cols, self.images = rows, cols, images
        self.devices = rows * cols
        self.tile_rows, self.tile_cols = GRID // rows, GRID // cols
        self.tokens = images * self.tile_rows * self.tile_cols
        kinds = ([], [], [])
        for n in range(images):
            for i in range(NWIN):
                for j in range(NWIN):
                    kinds[(i == NWIN - 1) + (j == NWIN - 1)].append((n, i, j))
        self.caps = tuple(-(-len(kind) // self.devices) for kind in kinds)
        self.parts = {w: self._sources(w) for kind in kinds for w in kind}
        owner = self._assign(kinds)
        self.counts = (KEYS,) * self.caps[0] + (EDGE * PITCH,) * (self.caps[1] + self.caps[2])
        _, self.window_rows, _ = slot_places(self.counts)
        self._tables(kinds, owner)

    def _distance(self, one, two):
        r, c = divmod(one, self.cols)
        q, e = divmod(two, self.cols)
        return abs(c - e) + abs(r // 2 - q // 2) + (0.125 if r % 2 != q % 2 else 0.0)

    def _sources(self, window):
        _, i, j = window
        (r0, r1), (c0, c1) = sides(i), sides(j)
        tr, tc = self.tile_rows, self.tile_cols
        found = {}
        for r in range(r0 // tr, (r1 - 1) // tr + 1):
            for c in range(c0 // tc, (c1 - 1) // tc + 1):
                high = min(r1, (r + 1) * tr) - max(r0, r * tr)
                wide = min(c1, (c + 1) * tc) - max(c0, c * tc)
                found[r * self.cols + c] = high * wide
        return found

    def _rounds(self, owner):
        pairs = {}
        for window, dev in owner.items():
            for source, amount in self.parts[window].items():
                if source != dev:
                    pairs[source, dev] = pairs.get((source, dev), 0) + amount
        rounds = []
        for pair, amount in sorted(pairs.items(), key=lambda p: (-p[1], p[0])):
            for senders, takers, members in rounds:
                if pair[0] not in senders and pair[1] not in takers:
                    break
            else:
                senders, takers, members = set(), set(), []
                rounds.append((senders, takers, members))
            senders.add(pair[0])
            takers.add(pair[1])
            members.append(pair)
        return pairs, [members for _, _, members in rounds]

    def _cost(self, owner):
        pairs, rounds = self._rounds(owner)
        moved = sum(amount * self._distance(*pair) for pair, amount in pairs.items())
        return moved / 4 + sum(64 + max(pairs[p] for p in members) for members in rounds)

    def _assign(self, kinds):
        owner = {}
        room = {}
        for kind, windows in enumerate(kinds):
            room[kind] = [self.caps[kind]] * self.devices
            for window in sorted(windows, key=lambda w: (-(w[1] + w[2]), w)):
                far = lambda d: sum(t * self._distance(s, d) for s, t in self.parts[window].items())
                dev = min((d for d in range(self.devices) if room[kind][d]), key=lambda d: (far(d), d))
                owner[window] = dev
                room[kind][dev] -= 1
        best = self._cost(owner)
        for _ in range(4):
            before = best
            for kind in (1, 2, 0):
                for one in kinds[kind]:
                    for dev in range(self.devices):
                        if dev == owner[one]:
                            continue
                        trials = []
                        if room[kind][dev]:
                            trials.append({**owner, one: dev})
                        for two in kinds[kind]:
                            if owner[two] == dev:
                                trials.append({**owner, one: dev, two: owner[one]})
                        for trial in trials:
                            price = self._cost(trial)
                            if price < best - 1e-9:
                                if sum(trial[w] != owner[w] for w in kinds[kind]) == 1:
                                    room[kind][owner[one]] += 1
                                    room[kind][dev] -= 1
                                owner, best = trial, price
                                break
            if best >= before:
                break
        return owner

    def _tables(self, kinds, owner):
        places, _, _ = slot_places(self.counts)
        starts = (0, self.caps[0], self.caps[0] + self.caps[1])
        self.swapped = np.zeros((self.devices, len(self.counts)), np.int32)
        taken = {}
        moves = {}
        for kind, windows in enumerate(kinds):
            for window in windows:
                n, i, j = window
                dev = owner[window]
                slot = starts[kind] + taken.get((dev, kind), 0)
                taken[dev, kind] = taken.get((dev, kind), 0) + 1
                swap = kind == 1 and j == NWIN - 1
                self.swapped[dev, slot] = swap
                (r0, r1), (c0, c1) = sides(i), sides(j)
                for r in range(r0, r1):
                    for c in range(c0, c1):
                        a, b = (c - c0, r - r0) if swap else (r - r0, c - c0)
                        row = places[slot][0] + PITCH * a + b
                        source = (r // self.tile_rows) * self.cols + c // self.tile_cols
                        token = (n * self.tile_rows + r % self.tile_rows) * self.tile_cols
                        token += c % self.tile_cols
                        moves.setdefault((source, dev), []).append((token, row))
        _, rounds = self._rounds(owner)
        self.perms = rounds
        self.sizes = [-(-max(len(moves[p]) for p in members) // PITCH) * PITCH for members in rounds]
        total = sum(self.sizes)
        self.pack = np.full((self.devices, total), -1, np.int32)
        self.take = np.full((self.devices, self.window_rows), -1, np.int32)
        self.pack_back = np.full((self.devices, total), -1, np.int32)
        self.take_back = np.full((self.devices, self.tokens), -1, np.int32)
        for dev in range(self.devices):
            for token, row in moves.get((dev, dev), ()):
                self.take[dev, row] = token
                self.take_back[dev, token] = row
        at = 0
        for members, size in zip(rounds, self.sizes):
            for source, dev in members:
                for k, (token, row) in enumerate(moves[source, dev]):
                    self.pack[source, at + k] = token
                    self.take[dev, row] = self.tokens + at + k
                    self.pack_back[dev, at + k] = row
                    self.take_back[source, token] = self.window_rows + at + k
            at += size


def chosen(index, start, count):
    spot = lax.broadcasted_iota(jnp.int32, (count, index.shape[1]), 0) + start
    return jnp.where(spot == index, 1.0, 0.0).astype(bf16)


def pack_kernel(sizes, index_ref, *refs):
    token_refs, out_refs = refs[: len(refs) - len(sizes)], refs[len(refs) - len(sizes) :]
    at = 0
    for size, out_ref in zip(sizes, out_refs):
        hot = chosen(index_ref[0:1, at : at + size], 0, token_refs[0].shape[0])
        for k, ref in enumerate(token_refs):
            width = ref.shape[1]
            moved = dot_tn(hot, ref[...].astype(bf16)).astype(bf16)
            out_ref[:, width * k : width * (k + 1)] = moved
        at += size


def pack(index, tokens, sizes):
    width = sum(t.shape[1] for t in tokens)
    return pl.pallas_call(
        lambda *refs: pack_kernel(sizes, *refs),
        out_shape=[jax.ShapeDtypeStruct((size, width), bf16) for size in sizes],
        compiler_params=pltpu.CompilerParams(vmem_limit_bytes=40 << 20),
        name="pack",
    )(index[None], *tokens)


def take_kernel(count, masked, index_ref, *refs):
    local_refs, arrived, out_refs = refs[:count], refs[count : -count - masked], refs[-count - masked :]
    index = index_ref[...]
    at = local_refs[0].shape[0]
    hot = chosen(index, 0, at)
    totals = []
    for ref in local_refs:
        local = ref[...]
        total = dot_tn(hot, local.astype(bf16))
        if local.dtype == f32:
            total = total + dot_tn(hot, (local - local.astype(bf16).astype(f32)).astype(bf16))
        totals.append(total)
    for ref in arrived:
        hot = chosen(index, at, ref.shape[0])
        width = ref.shape[1] // count
        totals = [
            t + dot_tn(hot, ref[:, width * k : width * (k + 1)]) for k, t in enumerate(totals)
        ]
        at += ref.shape[0]
    for ref, total in zip(out_refs, totals):
        ref[...] = total.astype(ref.dtype)
    if masked:
        row = jnp.where(index >= 0, 1.0, 0.0)
        out_refs[-1][...] = jnp.broadcast_to(row, (LANES, row.shape[1])).T


def take(index, locals_, arrived, masked=False):
    shapes = [((index.shape[0], local.shape[1]), local.dtype) for local in locals_]
    if masked:
        shapes.append(((index.shape[0], LANES), f32))
    return pl.pallas_call(
        lambda *refs: take_kernel(len(locals_), int(masked), *refs),
        out_shape=[jax.ShapeDtypeStruct(*shape) for shape in shapes],
        compiler_params=pltpu.CompilerParams(vmem_limit_bytes=40 << 20),
        name="take",
    )(index[None], *locals_, *arrived)


class Mover:
    def __init__(self, plan):
        self.plan = plan
        here = lax.axis_index("row") * plan.cols + lax.axis_index("col")
        mine = lambda table: lax.dynamic_index_in_dim(jnp.asarray(table), here, 0, keepdims=False)
        self.index = {name: mine(getattr(plan, name)) for name in ("pack", "take", "pack_back", "take_back")}
        self.swapped = mine(plan.swapped)

    def pack(self, *tokens):
        return pack(self.index["pack"], tokens, self.plan.sizes)

    def send(self, packed):
        return [lax.ppermute(s, ("row", "col"), perm) for s, perm in zip(packed, self.plan.perms)]

    def receive(self, *tokens, arrived, masked=False):
        return take(self.index["take"], tokens, arrived, masked)

    def pack_back(self, *rows):
        return pack(self.index["pack_back"], rows, self.plan.sizes)

    def send_back(self, packed):
        back = [[(two, one) for one, two in perm] for perm in self.plan.perms]
        return [lax.ppermute(s, ("row", "col"), perm) for s, perm in zip(packed, back)]

    def receive_back(self, *rows, arrived):
        return take(self.index["take_back"], rows, arrived)


AXES = ("dp", "row", "col")
TORUS = (2, 4, 4)


def after(values, *first):
    return lax.optimization_barrier((tuple(values), first))[0]


def over_dp(v):
    return lax.ppermute(v, "dp", [(0, 1), (1, 0)])


def over_y(v):
    return lax.ppermute(v, "row", [(r, (r + 2) % 4) for r in range(4)])


def over_both(v):
    return lax.ppermute(v, ("dp", "row"), [(k, (k // 4 + 1) % 2 * 4 + (k % 4 + 2) % 4) for k in range(8)])


def over_core(v):
    return lax.ppermute(v, "row", [(r, r ^ 1) for r in range(4)])


def over_col(v, steps):
    return lax.ppermute(v, "col", [(c, (c + steps) % 4) for c in range(4)])


def block_at(flip_dp, flip_y, flip_core):
    dp, row = lax.axis_index("dp"), lax.axis_index("row")
    return (
        ((dp + flip_dp) % 2) * 4 + ((row // 2 + flip_y) % 2) * 2 + (row % 2 + flip_core) % 2
    )


KINDS = ((0, 0), (1, 0), (0, 1), (1, 1))


def column_kernel(store, *refs):
    seen, out_ref = refs[:4], refs[4]
    place = lax.axis_index("col")
    for j in range(4):
        for k in range(4):

            @pl.when((place - j) % 4 == k)
            def _():
                store(out_ref, j, seen[k])


def in_column(shard, store, shape):
    seen = [shard] + [over_col(shard, k) for k in (1, 2, 3)]
    return pl.pallas_call(
        lambda *refs: column_kernel(store, *refs),
        out_shape=jax.ShapeDtypeStruct(shape, bf16),
        name="in_column",
    )(*seen)


def planes_of(weight):
    return jnp.swapaxes(weight.reshape(weight.shape[0], -1, weight.shape[0] * 32), 0, 1)


SMALL = 8


def first_shard_kernel(w_ref, *refs):
    out_ref = refs[-1]
    rows, width = w_ref.shape[0], out_ref.shape[1]
    for plane in range(3):
        out_ref[rows * plane : rows * (plane + 1), :] = w_ref[:, width * plane : width * (plane + 1)]
    out_ref[3 * rows :, :] = jnp.zeros((SMALL, width), bf16)
    for k, ref in enumerate(refs[:-1]):
        out_ref[3 * rows + k : 3 * rows + k + 1, 0 : ref.shape[1]] = ref[...]


def first_weights(qkv_weight, small):
    rows, width = qkv_weight.shape[0], qkv_weight.shape[1] // 3
    shard = pl.pallas_call(
        first_shard_kernel,
        out_shape=jax.ShapeDtypeStruct((3 * rows + SMALL, width), bf16),
        name="first_shard",
    )(qkv_weight, *[v[None] for v in small])
    (shard,) = yield (shard,)

    def store(ref, j, shard):
        for plane in range(3):
            at = rows * (4 * plane + j)
            ref[at : at + rows, :] = shard[rows * plane : rows * (plane + 1), :]
        at = 12 * rows + SMALL * j
        ref[at : at + SMALL, :] = shard[3 * rows :, :]

    own = in_column(shard, store, (12 * rows + 4 * SMALL, width))
    (own,) = yield (own,)
    pieces = [own, over_dp(own), over_y(own), over_both(own)]
    pieces = yield pieces
    pieces = [*pieces, *[over_core(p) for p in pieces]]
    yield pieces


def gathered_planes(up_weight, down_weight, proj_weight):
    rows, width = proj_weight.shape
    planes = [planes_of(up_weight), down_weight.reshape(-1, rows, width), proj_weight[None]]
    return lax.all_gather(jnp.concatenate(planes, 0)[None], AXES, axis=0, tiled=True)


def scatter_sum(mine, other, whole):
    (other,) = yield (other,)
    came = over_core(other)
    (came,) = yield (came,)
    own, to_dp, to_y, diag = [mine[k].astype(f32) + came[k].astype(f32) for k in range(4)]
    to_dp, to_y, diag = yield [v.astype(bf16) for v in (to_dp, to_y, diag)]
    came = yield (over_dp(to_dp), over_y(to_y), over_both(diag))
    column = own
    for part in came:
        column = column + part.astype(f32)
    planes, rows, width = column.shape
    column = column.reshape(planes, 4, rows // 4, width)
    sent = column.astype(bf16)
    place = lax.axis_index("col")
    at = lambda values, k: lax.dynamic_index_in_dim(values, (place + k) % 4, 1 - whole, False)
    total = at(column, 0)
    steps = yield [at(sent, k) for k in (1, 2, 3)]
    steps = yield [over_col(step, k) for k, step in zip((1, 2, 3), steps)]
    for step in steps:
        total = total + step.astype(f32)
    yield (total,)


class Steps:
    def __init__(self, steps):
        self.steps = steps
        self.arrays = tuple(next(steps))

    def __call__(self, *values):
        values, arrays = lax.optimization_barrier((values, self.arrays))
        self.arrays = tuple(self.steps.send(arrays))
        return values if len(values) != 1 else values[0]


def tree_sum(value):
    value = value + over_col(value, 1) + over_col(value, 2) + over_col(value, 3)
    value = value + over_dp(value) + over_y(value) + over_both(value)
    return value + over_core(value)


def on_torus():
    return tuple(lax.axis_size(a) for a in AXES) == TORUS


def device_number():
    return (lax.axis_index("dp") * lax.axis_size("row") + lax.axis_index("row")) * lax.axis_size(
        "col"
    ) + lax.axis_index("col")


def sum_everywhere(value):
    if on_torus():
        return tree_sum(value)
    return lax.psum(value, AXES)


def gather_at_once(*shards):
    return tuple(lax.all_gather(s, AXES, axis=0, tiled=True) for s in shards)


def sum_at_once(grad):
    return lax.psum_scatter(grad, AXES, scatter_dimension=0, tiled=True)


SPREAD = 0.3275911
TAIL_COEFFICIENTS = (0.1850680112838745, 0.18050004541873932, 0.20733030140399933, 0.020621487870812416, 0.46248844265937805, -0.41615772247314453, 0.5027683973312378, -0.14261901378631592)


def normal_parts(u):
    z = jnp.abs(u) * (2.0 ** -0.5)
    t = 1.0 / (1.0 + SPREAD * z)
    bell = jnp.exp(-0.5 * u * u)
    total = jnp.full_like(t, TAIL_COEFFICIENTS[-1])
    for coefficient in TAIL_COEFFICIENTS[-2::-1]:
        total = total * t + coefficient
    tail = 0.5 * total * t * bell
    return jnp.where(u < 0, tail, 1.0 - tail), bell * (2.0 * math.pi) ** -0.5


def normalize(values):
    center = values - jnp.mean(values, axis=-1, keepdims=True)
    inverse = lax.rsqrt(jnp.mean(center * center, axis=-1, keepdims=True) + epsilon)
    return center * inverse, inverse


def norm_back(upstream, normed, inverse, gain):
    scaled = upstream * gain
    inner = jnp.mean(scaled, axis=-1, keepdims=True)
    cross = jnp.mean(scaled * normed, axis=-1, keepdims=True)
    result = inverse * (scaled - inner - normed * cross)
    sums = [jnp.sum(v, axis=0, keepdims=True) for v in (upstream * normed, upstream)]
    return result, sums


def store_blocks(grad, kept, refs):
    kept[...] = grad
    rows = grad.shape[0] // 8
    for core, ref in enumerate(refs):
        for k, kind in enumerate(KINDS):
            at = pl.multiple_of(block_at(*kind, core) * rows, rows)
            ref[k, 0] = kept[pl.ds(at, rows), :].astype(bf16)


def stacked_rows(rows):
    spare = jnp.zeros((8 - len(rows), rows[0].shape[1]), f32)
    return jnp.concatenate([*rows, spare], 0)


def spread(count, width):
    return jnp.asarray(np.arange(width)[None] % count == np.arange(LANES)[:, None], bf16)


QV, PROJ_ADD, GAIN_ONE, SHIFT_ONE, GAIN_TWO, SHIFT_TWO, UP_ADD, DOWN_ADD = range(8)
HELD = (48, 24, 24, 24, 24, 24, 96, 24)


def row(ref, k):
    return ref[k : k + 1, :]


def vectors_kernel(*refs):
    pieces, spreads = refs[:8], refs[8:11]
    vecs_ref, up_add_ref, bias_ref, bias_v_ref = refs[11:]
    rows = jnp.concatenate([piece[:, 0:LANES] for piece in pieces], 0)
    whole = []
    for count, spread_ref in zip((24, 48, 96), spreads):
        wide = dot_nn(rows, spread_ref[...])
        total = jnp.zeros((SMALL, wide.shape[1]), f32)
        group = lax.broadcasted_iota(jnp.int32, total.shape, 1) // count
        for k in range(8):
            block = block_at(*KINDS[k % 4], k // 4)
            for col in range(4):
                at = SMALL * (4 * k + col)
                total = total + jnp.where(group == 4 * block + col, wide[at : at + SMALL], 0.0)
        whole.append(total)
    vecs_ref[...] = whole[0]
    up_add_ref[...] = whole[2]
    qv = whole[1][QV : QV + 1]
    width = vecs_ref.shape[1]
    bias_ref[...] = jnp.concatenate([qv[:, :width], jnp.zeros((1, width), f32), qv[:, width:]], 1)
    bias_v_ref[...] = jnp.broadcast_to(qv[:, width:], bias_v_ref.shape).astype(bf16)


def vectors(pieces):
    rows, width = pieces[0].shape
    spreads = [spread(count, 32 * count) for count in (24, 48, 96)]
    tail = pl.BlockSpec((4 * SMALL, width), lambda s: (rows // (4 * SMALL) - 1, 0))
    shapes = [((SMALL, width), f32), ((SMALL, 4 * width), f32), ((1, 3 * width), f32), ((8, width), bf16)]
    return pl.pallas_call(
        vectors_kernel,
        grid=(1,),
        in_specs=[tail] * 8 + [whole_spec(s) for s in spreads],
        out_specs=[pl.BlockSpec(shape, lambda s: (0, 0)) for shape, _ in shapes],
        out_shape=[jax.ShapeDtypeStruct(*shape) for shape in shapes],
        name="vectors",
    )(*pieces, *spreads)


def gathered_vectors(small):
    whole = [v.astype(f32) for v in gather_at_once(*small)]
    width = whole[PROJ_ADD].shape[0]
    none = jnp.zeros((width,), f32)
    vecs = jnp.stack([v if v.shape[0] == width else none for v in whole])
    up_add = jnp.broadcast_to(whole[UP_ADD][None], (SMALL, 4 * width))
    query, value = whole[QV][:width], whole[QV][width:]
    bias = jnp.concatenate([query, none, value])[None]
    return vecs, up_add, bias, jnp.broadcast_to(value[None], (8, width)).astype(bf16)


def assemble(target, pieces):
    for k, piece in enumerate(pieces):
        if piece is None:
            continue
        rows = piece.shape[-2]
        at = pl.multiple_of(block_at(*KINDS[k % 4], k // 4) * rows, rows)
        target[pl.ds(at, rows), :] = piece[...].reshape(rows, piece.shape[-1])


def qkv_ahead_kernel(x_ref, real_ref, vecs_ref, bias_ref, *refs):
    weight_refs, (hidden_ref, out_ref, w_ref) = refs[:-3], refs[-3:]

    @pl.when(pl.program_id(0) == 0)
    def _():
        plain, _ = normalize(x_ref[...].astype(f32))
        hidden = plain * row(vecs_ref, GAIN_ONE) + row(vecs_ref, SHIFT_ONE)
        hidden = hidden * real_ref[:, 0:1]
        hidden_ref[...] = hidden.astype(bf16)

    if len(weight_refs) == 1:
        w_ref[...] = weight_refs[0][...]
    else:
        assemble(w_ref, weight_refs)
    out_ref[...] = (dot_nn(hidden_ref[...], w_ref[...]) + bias_ref[...]).astype(bf16)


def join_rows(target, source, planes):
    rows = source.shape[2]
    at = 0
    for device in range(source.shape[0]):
        for plane in range(planes):
            target[at : at + rows, :] = source[device, plane]
            at += rows


def up_kernel(x_ref, a0_ref, a1_ref, a2_ref, vecs_ref, up_add_ref, w_ref, p_ref, *refs):
    middle_ref, second_ref, active_ref, slope_ref, up_ref, proj_ref = refs
    pieced = len(w_ref.shape) > 2

    @pl.when(pl.program_id(0) == 0)
    def _():
        if pieced:
            join_rows(proj_ref, p_ref, 1)
        else:
            proj_ref[...] = p_ref[...]
        middle = x_ref[...].astype(f32) + row(vecs_ref, PROJ_ADD)
        for k, ref in enumerate((a0_ref, a1_ref, a2_ref)):
            size = ref.shape[1]
            middle = middle + dot_nn(ref[...], proj_ref[size * k : size * (k + 1), :])
        plain, _ = normalize(middle)
        middle_ref[...] = middle
        second = plain * row(vecs_ref, GAIN_TWO) + row(vecs_ref, SHIFT_TWO)
        second_ref[...] = second.astype(bf16)

    if pieced:
        join_rows(up_ref, w_ref, 1)
    else:
        up_ref[...] = w_ref[...]
    inner = dot_nn(second_ref[...], up_ref[...]) + row(up_add_ref, UP_ADD)
    below, density = normal_parts(inner)
    active_ref[...] = (inner * below).astype(bf16)
    slope_ref[...] = below + inner * density


def down_kernel(active_ref, slope_ref, middle_ref, g_ref, vecs_ref, w_ref, *refs):
    out_ref, grad_ref, inner_grad_ref, up_add_grad_ref, total = refs[:5]
    step = pl.program_id(0)

    @pl.when(step == 0)
    def _():
        total[...] = middle_ref[...] + row(vecs_ref, DOWN_ADD)

    if len(w_ref.shape) > 2:
        join_rows(refs[5], w_ref, 4)
        down = refs[5][...]
    else:
        down = w_ref[...]
    active = active_ref[...]
    g = g_ref[...]
    inner_grad = (dot_nt(g, down) * slope_ref[...]).astype(bf16)
    inner_grad_ref[...] = inner_grad
    up_add_grad_ref[...] = jnp.broadcast_to(
        jnp.sum(inner_grad.astype(f32), axis=0, keepdims=True), up_add_grad_ref.shape
    )
    total[...] += dot_nn(active, down)
    grad_ref[...] = dot_tn(active, g).astype(bf16)

    @pl.when(step == pl.num_programs(0) - 1)
    def _():
        out_ref[...] = total[...].astype(bf16)


def mlp_back_kernel(
    pieced, second_ref, inner_grad_ref, up_ref, middle_ref, g_ref, a0_ref, a1_ref, a2_ref, proj_ref,
    vecs_ref, mine_ref, other_ref, middle_grad_ref, attended_grad_ref, sums_ref, total, kept,
):
    step = pl.program_id(0)
    last = pl.num_programs(0) - 1

    def store(grad):
        if pieced:
            store_blocks(grad, kept, (mine_ref, other_ref))
        else:
            blocks = grad.astype(bf16).reshape(8, 1, grad.shape[0] // 8, grad.shape[1])
            mine_ref[...] = blocks[:4]
            other_ref[...] = blocks[4:]

    @pl.when(step == 0)
    def _():
        total[...] = jnp.zeros_like(total)

    @pl.when(step < last)
    def _():
        inner_grad = inner_grad_ref[...]
        total[...] += dot_nt(inner_grad, up_ref[...])
        store(dot_tn(second_ref[...], inner_grad))

    @pl.when(step == last)
    def _():
        plain, inverse = normalize(middle_ref[...])
        flow = g_ref[...].astype(f32)
        part, sums = norm_back(total[...], plain, inverse, row(vecs_ref, GAIN_TWO))
        middle_grad = flow + part
        middle_grad_ref[...] = middle_grad
        branch = middle_grad.astype(bf16)
        attended_grad_ref[...] = dot_nt(branch, proj_ref[...]).astype(bf16)
        store(jnp.concatenate([dot_tn(ref[...], branch) for ref in (a0_ref, a1_ref, a2_ref)], 0))
        column = lambda v: jnp.sum(v, axis=0, keepdims=True)
        sums_ref[...] = stacked_rows([*sums, column(branch.astype(f32)), column(flow)])


def qkv_back_kernel(
    pieced, hidden_ref, d0_ref, d1_ref, d2_ref, w_ref, middle_grad_ref, x_ref, real_ref, vecs_ref,
    mine_ref, other_ref, column_ref, images_grad_ref, sums_ref, total, kept,
):
    step = pl.program_id(0)

    @pl.when(step == 0)
    def _():
        total[...] = jnp.zeros_like(total)

    back = jnp.concatenate([ref[0] for ref in (d0_ref, d1_ref, d2_ref)], 1)
    total[...] += dot_nt(back, w_ref[...])
    grad = dot_tn(hidden_ref[...], back)
    if pieced:
        store_blocks(grad, kept, (mine_ref, other_ref))
    else:
        blocks = grad.astype(bf16).reshape(8, 1, grad.shape[0] // 8, grad.shape[1])
        mine_ref[...] = blocks[:4]
        other_ref[...] = blocks[4:]
    column_ref[0] = jnp.broadcast_to(
        jnp.sum(back.astype(f32), axis=0, keepdims=True), column_ref.shape[1:]
    )

    @pl.when(step == pl.num_programs(0) - 1)
    def _():
        hidden_grad = total[...].astype(bf16).astype(f32) * real_ref[:, 0:1]
        plain, inverse = normalize(x_ref[...].astype(f32))
        part, sums = norm_back(hidden_grad, plain, inverse, row(vecs_ref, GAIN_ONE))
        images_grad_ref[...] = middle_grad_ref[...] + part
        sums_ref[...] = stacked_rows(sums)


def whole_spec(array):
    return pl.BlockSpec(array.shape, lambda s: (0,) * array.ndim)


def across(rows, width):
    return pl.BlockSpec((rows, width), lambda s: (0, s))


def cost(flops):
    return pl.CostEstimate(flops=COST, bytes_accessed=1024, transcendentals=0)


BIG = pltpu.CompilerParams(vmem_limit_bytes=56 << 20)


def qkv_ahead(x, real, vecs, bias, weights):
    rows, width = x.shape
    shard = width // 8
    if len(weights) == 1:
        specs = [across(width, width)]
    else:
        specs = [pl.BlockSpec((shard, width), lambda s: (s, 0))] * 8
    return pl.pallas_call(
        qkv_ahead_kernel,
        grid=(3,),
        in_specs=[
            whole_spec(x), whole_spec(real), whole_spec(vecs), across(1, width), *specs,
        ],
        out_specs=[whole_spec(x), across(rows, width), across(width, width)],
        out_shape=[
            jax.ShapeDtypeStruct((rows, width), bf16),
            jax.ShapeDtypeStruct((rows, 3 * width), bf16),
            jax.ShapeDtypeStruct((width, 3 * width), bf16),
        ],
        compiler_params=BIG,
        cost_estimate=cost(5 * 10**9),
        name="qkv_ahead",
    )(x, real, vecs, bias, *weights)


def up_ahead(x, attended, vecs, up_add, weights):
    rows, width = x.shape
    if len(weights) == 2:
        specs = [across(width, width), whole_spec(weights[1])]
    else:
        (planes,) = weights
        one = (planes.shape[0], 1, *planes.shape[2:])
        specs = [pl.BlockSpec(one, lambda s: (0, s, 0, 0)), pl.BlockSpec(one, lambda s: (0, 8, 0, 0))]
        weights = planes, planes
    block = lambda s: (0, 0)
    outs = [
        (pl.BlockSpec((rows, width), block), (rows, width), f32),
        (pl.BlockSpec((rows, width), block), (rows, width), bf16),
        (across(rows, width), (rows, 4 * width), bf16),
        (across(rows, width), (rows, 4 * width), f32),
        (across(width, width), (width, 4 * width), bf16),
        (pl.BlockSpec((width, width), block), (width, width), bf16),
    ]
    return pl.pallas_call(
        up_kernel,
        grid=(4,),
        in_specs=[
            whole_spec(x), *[whole_spec(a) for a in attended], whole_spec(vecs), across(8, width),
            *specs,
        ],
        out_specs=[spec for spec, _, _ in outs],
        out_shape=[jax.ShapeDtypeStruct(shape, kind) for _, shape, kind in outs],
        compiler_params=BIG,
        cost_estimate=cost(15 * 10**9),
        name="up_ahead",
    )(x, *attended, vecs, up_add, *weights)


def down_ahead(active, slope, middle, g, vecs, weight):
    rows, width = middle.shape
    below = pl.BlockSpec((width, width), lambda s: (s, 0))
    scratch = [pltpu.VMEM((rows, width), f32)]
    spec = below
    if len(weight.shape) > 2:
        devices, _, *tile = weight.shape
        spec = pl.BlockSpec((devices // 4, 4, *tile), lambda s: (s, 1, 0, 0))
        scratch.append(pltpu.VMEM((width, width), bf16))
    outs = [
        (pl.BlockSpec((rows, width), lambda s: (0, 0)), (rows, width), bf16),
        (below, (4 * width, width), bf16),
        (across(rows, width), (rows, 4 * width), bf16),
        (across(8, width), (8, 4 * width), f32),
    ]
    return pl.pallas_call(
        down_kernel,
        grid=(4,),
        in_specs=[
            across(rows, width), across(rows, width), whole_spec(middle), whole_spec(g),
            whole_spec(vecs), spec,
        ],
        out_specs=[spec for spec, _, _ in outs],
        out_shape=[jax.ShapeDtypeStruct(shape, kind) for _, shape, kind in outs],
        scratch_shapes=scratch,
        compiler_params=BIG,
        cost_estimate=cost(15 * 10**9),
        name="down_ahead",
    )(active, slope, middle, g, vecs, weight)


def mlp_back(second, inner_grad, up, middle, g, attended, proj, vecs, pieced):
    rows, width = second.shape
    shard = width // 8
    sums = jax.ShapeDtypeStruct((8, width), f32)
    upto = lambda count: pl.BlockSpec((count, width), lambda s: (0, jnp.minimum(s, 3)))
    block = pl.BlockSpec((4, 1, shard, width), lambda s: (0, s, 0, 0))
    planes = jax.ShapeDtypeStruct((4, 5, shard, width), bf16)
    return pl.pallas_call(
        lambda *refs: mlp_back_kernel(pieced, *refs),
        grid=(5,),
        in_specs=[
            whole_spec(second), upto(rows), upto(width), whole_spec(middle), whole_spec(g),
            *[whole_spec(a) for a in attended], whole_spec(proj), whole_spec(vecs),
        ],
        out_specs=[block, block, whole_spec(second), whole_spec(second), whole_spec(sums)],
        out_shape=[
            planes,
            planes,
            jax.ShapeDtypeStruct((rows, width), f32),
            jax.ShapeDtypeStruct((rows, width), bf16),
            sums,
        ],
        scratch_shapes=[pltpu.VMEM((rows, width), f32), pltpu.VMEM((width, width), f32)],
        compiler_params=BIG,
        cost_estimate=cost(15 * 10**9),
        name="mlp_back",
    )(second, inner_grad, up, middle, g, *attended, proj, vecs)


def qkv_back(hidden, pieces, weight, middle_grad, x, real, vecs, pieced):
    rows, width = hidden.shape
    shard = width // 8
    sums = jax.ShapeDtypeStruct((8, width), f32)
    block = pl.BlockSpec((4, 1, shard, width), lambda s: (0, s, 0, 0))
    planes = jax.ShapeDtypeStruct((4, 3, shard, width), bf16)
    return pl.pallas_call(
        lambda *refs: qkv_back_kernel(pieced, *refs),
        grid=(3,),
        in_specs=[
            whole_spec(hidden),
            *[pl.BlockSpec((1, *p.shape[1:]), lambda s: (s, 0, 0)) for p in pieces],
            across(width, width), whole_spec(middle_grad), whole_spec(x), whole_spec(real),
            whole_spec(vecs),
        ],
        out_specs=[
            block,
            block,
            pl.BlockSpec((1, 8, width), lambda s: (s, 0, 0)),
            whole_spec(middle_grad), whole_spec(sums),
        ],
        out_shape=[
            planes,
            planes,
            jax.ShapeDtypeStruct((3, 8, width), f32),
            jax.ShapeDtypeStruct((rows, width), f32),
            sums,
        ],
        scratch_shapes=[pltpu.VMEM((rows, width), f32), pltpu.VMEM((width, width), f32)],
        compiler_params=BIG,
        cost_estimate=cost(10**10),
        name="qkv_back",
    )(hidden, *pieces, weight, middle_grad, x, real, vecs)


SUM_ROWS = 24
SUM_AT = dict(query=0, value=1, proj=2, pre=3, mid=5, up=7, down=11, tables=16)


def small_sums_kernel(swapped_ref, column_ref, extra_ref, two_ref, one_ref, up_ref, *refs):
    table_refs, out_ref = refs[:-1], refs[-1]
    width = out_ref.shape[1]
    out_ref[...] = jnp.zeros_like(out_ref)

    def put(name, value, more=0):
        at = SUM_AT[name] + more
        out_ref[at : at + 1, :] = value

    put("query", column_ref[0, 0:1, :])
    extra = jnp.concatenate([extra_ref[p, 0:1, :] for p in range(width // LANES)], 1)
    put("value", column_ref[2, 0:1, :] + extra)
    put("proj", two_ref[2:3, :])
    for k in range(2):
        put("pre", one_ref[k : k + 1, :], k)
        put("mid", two_ref[k : k + 1, :], k)
    for k in range(4):
        put("up", up_ref[0:1, width * k : width * (k + 1)], k)
    put("down", two_ref[3:4, :])
    count = 32
    sums = [jnp.zeros((count, HEAD), f32) for _ in range(2)]
    for s in range(table_refs[0].shape[0]):
        grad = table_refs[0][s]
        for ref in table_refs[1:]:
            grad = grad + ref[s]
        both = (grad[:HEAD, HEAD:] + grad[HEAD:, :HEAD]).T
        parts = (both[:count], both[COLTABLE : COLTABLE + count])
        swap = swapped_ref[s] != 0
        sums[0] = sums[0] + jnp.where(swap, parts[1], parts[0])
        sums[1] = sums[1] + jnp.where(swap, parts[0], parts[1])
    tables = jnp.concatenate(sums, 1)
    at = SUM_AT["tables"]
    for k in range(4):
        out_ref[at : at + 8, LANES * k : LANES * (k + 1)] = tables[8 * k : 8 * k + 8]


def small_sums(swapped, column_sums, extra, two, one, up, tables):
    whole = lambda a: pl.BlockSpec(a.shape, lambda s, w: (0,) * a.ndim)
    given = (column_sums, extra, two, one, up, *tables)
    return pl.pallas_call(
        small_sums_kernel,
        grid_spec=pltpu.PrefetchScalarGridSpec(
            num_scalar_prefetch=1,
            grid=(1,),
            in_specs=[whole(a) for a in given],
            out_specs=pl.BlockSpec((SUM_ROWS, two.shape[1]), lambda s, w: (0, 0)),
        ),
        out_shape=jax.ShapeDtypeStruct((SUM_ROWS, two.shape[1]), f32),
        name="small_sums",
    )(swapped, *given)


def split_sums(total):
    count = lax.axis_size("dp") * lax.axis_size("row") * lax.axis_size("col")
    width = total.shape[1]

    def share(name, more=0, rows=1):
        at = SUM_AT[name] + more
        size = rows * width // count
        return lax.dynamic_slice(total[at : at + rows].reshape(-1), (device_number() * size,), (size,))

    at = SUM_AT["tables"]
    tables = jnp.concatenate([total[at : at + 8, LANES * k : LANES * (k + 1)] for k in range(4)], 0)
    tables = tables[: 2 * WIN - 1]
    vectors = (
        share("query", 0, 2), share("proj"), share("pre"), share("pre", 1), share("mid"),
        share("mid", 1), share("up", 0, 4), share("down"),
    )
    return vectors, (tables[:, :HEAD], tables[:, HEAD:])


def body(
    images, qkv_weight, qv_bias, proj_weight, proj_bias, pre_gain, pre_shift, mid_gain, mid_shift,
    up_weight, up_bias, down_weight, down_bias, rel_rows, rel_cols, cotangent,
):
    width = images.shape[-1]
    torus = on_torus()
    plan = plan_for(lax.axis_size("row"), lax.axis_size("col"), images.shape[0] * images.shape[1])
    move = Mover(plan)
    counts = plan.counts
    groups = (0, 2, 4)
    small = (qv_bias, proj_bias, pre_gain, pre_shift, mid_gain, mid_shift, up_bias, down_bias)
    pixels, cot = images.reshape(-1, width), cotangent.reshape(-1, width)
    swapped = move.swapped

    if torus:
        planes = gathered_planes(up_weight, down_weight, proj_weight)
        up_pieces, down_pieces = (planes,), planes
        first_steps = Steps(first_weights(qkv_weight, small))
        first_steps()
        sent = first_steps(move.send(move.pack(pixels, cot)))
        x, g, real = move.receive(pixels, cot, arrived=sent, masked=True)
        (rel_rows,) = after((rel_rows,), x)
        tables, tables_back = position_tables(swapped, rel_rows, rel_cols)
        tables = first_steps(tables)
        qkv = first_steps.arrays
        vecs, up_add, bias, bias_v = vectors(qkv)
    else:
        sent = move.send(move.pack(pixels, cot))
        x, g, real = move.receive(pixels, cot, arrived=sent, masked=True)
        whole_qkv, proj, up, down = gather_at_once(qkv_weight, proj_weight, up_weight, down_weight)
        qkv, up_pieces, down_pieces = (whole_qkv,), (up, proj), down
        tables, tables_back = position_tables(swapped, rel_rows, rel_cols)
        vecs, up_add, bias, bias_v = gathered_vectors(small)

    hidden, projected, qkv = qkv_ahead(x, real, vecs, bias, qkv)
    attended, logsum = [], []
    for first in groups:
        one, two = attend(projected, bias_v, tables, counts, first, 2)
        attended.append(one)
        logsum.append(two)
        projected, _ = after((projected, one), one)
    middle, second, active, slope, up, proj = up_ahead(x, attended, vecs, up_add, up_pieces)
    result, down_grad, inner_grad, up_add_grad = down_ahead(
        active, slope, middle, g, vecs, down_pieces
    )
    idle = lambda *values: values if len(values) != 1 else values[0]
    up_sum = qkv_sum = idle
    if torus:
        down_grad = sum_at_once(down_grad).astype(f32)
    packed = move.pack_back(result)
    second, packed = after((second, packed), result)
    out_sent = move.send_back(packed)
    mine, other, middle_grad, attended_grad, sums_two = mlp_back(
        second, inner_grad, up, middle, g, attended, proj, vecs, torus
    )
    if torus:
        up_sum = Steps(scatter_sum(mine, other, False))
    else:
        blocks = jnp.concatenate([mine, other], 0)
        up_grad = jnp.swapaxes(blocks[:, :4], 1, 2).reshape(width, -1)
        proj_grad = blocks[:, 4].reshape(width, width)
    attended_grad, out_sent = up_sum(attended_grad, out_sent)
    pieces, table_grads, extra = [], [], []
    for first, sums in zip(groups, logsum):
        one, two, three = attend_back(
            projected, attended_grad, sums, bias_v, tables, tables_back, counts, first
        )
        pieces.append(one)
        table_grads.append(two)
        extra.append(three)
        attended_grad, _ = after((attended_grad, one), one)
        if first == groups[0]:
            attended_grad = up_sum(attended_grad)
            attended_grad = up_sum(attended_grad)
    pieces, _ = after((pieces, attended_grad), attended_grad)
    mine, other, column_sums, images_grad, sums_one = qkv_back(
        hidden, pieces, qkv, middle_grad, x, real, vecs, torus
    )
    if torus:
        qkv_sum = Steps(scatter_sum(mine, other, False))
        images_grad = up_sum(images_grad)
    else:
        blocks = jnp.concatenate([mine, other], 0)
        qkv_grad = jnp.swapaxes(blocks, 1, 2).reshape(width, -1)
    images_grad = qkv_sum(images_grad)
    packed = move.pack_back(images_grad)
    sums = small_sums(
        swapped, column_sums, jnp.concatenate(extra, 0), sums_two, sums_one, up_add_grad, table_grads
    )
    if torus:
        packed, sums = up_sum(packed, sums)
        sent = move.send_back(packed)
        sums = sums + over_col(sums, 1) + over_col(sums, 2) + over_col(sums, 3)
        sums = qkv_sum(sums)
        sums = qkv_sum(sums)
        sums = sums + over_dp(sums) + over_y(sums) + over_both(sums)
        (out,) = move.receive_back(result, arrived=out_sent)
        sums, sent, out = qkv_sum(sums, sent, out)
        sums, sent, out = qkv_sum(sums, sent, out)
        sums, sent, out = up_sum(sums, sent, out)
        sums = sums + over_core(sums)
    else:
        sent = move.send_back(packed)
        (out,) = move.receive_back(result, arrived=out_sent)
        sums = lax.psum(sums, AXES)
    (images_grad,) = move.receive_back(images_grad, arrived=sent)
    mine, full = split_sums(sums)
    if torus:
        (total,) = up_sum.arrays
        up_grad = jnp.swapaxes(total[:4], 0, 1).reshape(-1, 4 * width)
        proj_grad = total[4]
        qkv_sum()
        (total,) = qkv_sum.arrays
        qkv_grad = jnp.swapaxes(total, 0, 1).reshape(-1, 3 * width)
    else:
        qkv_grad, proj_grad, up_grad, down_grad = [
            sum_at_once(g.astype(f32)) for g in (qkv_grad, proj_grad, up_grad, down_grad)
        ]
    return (
        out.reshape(images.shape),
        images_grad.reshape(images.shape),
        qkv_grad,
        mine[0],
        proj_grad,
        mine[1],
        mine[2],
        mine[3],
        mine[4],
        mine[5],
        up_grad,
        mine[6],
        down_grad,
        mine[7],
        full[0],
        full[1],
    )


PLANS = {}


def plan_for(rows, cols, images):
    key = (rows, cols, images)
    if key not in PLANS:
        PLANS[key] = Plan(*key)
    return PLANS[key]


def solution(mesh):
    tokens = P(None, "dp", "row", "col", None)
    rows = P(AXES, None)
    vector = P(AXES)
    placed = (
        tokens, rows, vector, rows, vector, vector, vector, vector, vector,
        rows, vector, rows, vector, P(), P(), tokens,
    )
    given = (tokens, tokens, rows, vector, rows, vector, vector, vector, vector, vector,
             rows, vector, rows, vector, P(), P())
    return jax.shard_map(body, mesh=mesh, in_specs=placed, out_specs=given, check_vma=False)
```

```python
import math

import jax
import jax.numpy as jnp
import numpy as np
from jax import lax
from jax.experimental import pallas as pl
from jax.experimental.pallas import tpu as pltpu
from jax.sharding import PartitionSpec as P

HEAD = 64
WIN = 14
GRID = 64
NWIN = 5
PITCH = 16
KEYS = WIN * PITCH
LANES = 128
ROWFIELD, COLFIELD, LOWFIELD, MASKLANE = 0, 14, 28, 56
COLTABLE = 32
NEG = -1e30
COST = 1024
EDGE = GRID - WIN * (NWIN - 1)
epsilon = 1e-06
bf16 = jnp.bfloat16
f32 = jnp.float32


def cost(flops):
    return pl.CostEstimate(flops=COST, bytes_accessed=1024, transcendentals=0)


def dot_nn(a, b):
    return lax.dot_general(a, b, (((1,), (0,)), ((), ())), preferred_element_type=f32)


def dot_nt(a, b):
    return lax.dot_general(a, b, (((1,), (1,)), ((), ())), preferred_element_type=f32)


def dot_tn(a, b):
    return lax.dot_general(a, b, (((0,), (0,)), ((), ())), preferred_element_type=f32)


def key_fields(reverse):
    shape = (KEYS, LANES)
    t = lax.broadcasted_iota(jnp.int32, shape, 0)
    a, b = t // PITCH, t % PITCH
    lane = lax.broadcasted_iota(jnp.int32, shape, 1) % HEAD
    if reverse:
        one = (lane == ROWFIELD + WIN - 1 - a) | (lane == COLFIELD + WIN - 1 - b)
        return jnp.where(one & (b < WIN), 1.0, 0.0).astype(bf16)
    one = (lane == ROWFIELD + a) | (lane == LOWFIELD + ROWFIELD + a)
    one = one | (lane == COLFIELD + b) | (lane == LOWFIELD + COLFIELD + b)
    out = jnp.where(one & (b < WIN), 1.0, 0.0)
    return jnp.where((lane == MASKLANE) & (b >= WIN), NEG, out).astype(bf16)


def tables_kernel(swapped_ref, rows_ref, cols_ref, ahead_ref, back_ref):
    shape = (2 * WIN - 1, HEAD)
    index = lax.broadcasted_iota(jnp.int32, shape, 0)
    lane = lax.broadcasted_iota(jnp.int32, shape, 1)
    empty = jnp.zeros((HEAD, HEAD), f32)
    for ref, place in ((ahead_ref, 2 * WIN - 2 - index), (back_ref, index)):
        spots = [jnp.where(lane == place + start, 1.0, 0.0).astype(bf16) for start in (0, COLTABLE)]
        both = []
        for one, two in ((rows_ref, cols_ref), (cols_ref, rows_ref)):
            half = dot_tn(one[...], spots[0]) + dot_tn(two[...], spots[1])
            full = [jnp.concatenate(pair, 1) for pair in ((empty, half), (half, empty))]
            both.append(jnp.concatenate(full, 0).astype(bf16))
        for s in range(ref.shape[0]):

            @pl.when(swapped_ref[s] == 0)
            def _():
                ref[s] = both[0]

            @pl.when(swapped_ref[s] != 0)
            def _():
                ref[s] = both[1]


def position_tables(swapped, rel_rows, rel_cols):
    one = jax.ShapeDtypeStruct((swapped.shape[0], LANES, LANES), bf16)
    return pl.pallas_call(
        tables_kernel,
        grid_spec=pltpu.PrefetchScalarGridSpec(
            num_scalar_prefetch=1,
            grid=(1,),
            in_specs=[pl.BlockSpec(rel_rows.shape, lambda s, w: (0, 0))] * 2,
            out_specs=[pl.BlockSpec(one.shape, lambda s, w: (0, 0, 0))] * 2,
        ),
        out_shape=[one, one],
        cost_estimate=cost(0),
        name="position_tables",
    )(swapped, rel_rows, rel_cols)


def lane_in(shape, start, count):
    lane = lax.broadcasted_iota(jnp.int32, shape, 1) % HEAD
    return (lane >= start) & (lane < start + count)


def query_fields(q2, table):
    turned = dot_nn(q2, table)
    parts = []
    shape = (PITCH, LANES)
    in_rows = lane_in(shape, ROWFIELD, WIN)
    in_cols = lane_in(shape, COLFIELD, WIN)
    for a in range(q2.shape[0] // PITCH):
        t = turned[PITCH * a : PITCH * (a + 1)]
        r = pltpu.roll(t, (a - WIN + 1) % LANES, 1)
        c = pltpu.roll(t, LANES - (COLTABLE + 2 * WIN - 2 - (WIN - 1) - COLFIELD), 1, stride=1, stride_axis=0)
        parts.append(jnp.where(in_rows, r, jnp.where(in_cols, c, 0.0)))
    full = jnp.concatenate(parts, 0)
    high = full.astype(bf16).astype(f32)
    low = pltpu.roll(full - high, LOWFIELD, 1)
    one = jnp.where(lane_in(full.shape, MASKLANE, 1), 1.0, 0.0)
    return (high + low + one).astype(bf16)


def field_tables(fields):
    parts = []
    shape = (PITCH, LANES)
    in_rows = lane_in(shape, ROWFIELD, WIN)
    in_cols = lane_in(shape, COLFIELD, WIN)
    for a in range(fields.shape[0] // PITCH):
        t = fields[PITCH * a : PITCH * (a + 1)]
        r = jnp.where(in_rows, t, 0.0)
        c = jnp.where(in_cols, t, 0.0)
        r = pltpu.roll(r, a, 1) if a else r
        c = pltpu.roll(c, COLTABLE - COLFIELD, 1, stride=1, stride_axis=0)
        parts.append(r + c)
    return jnp.concatenate(parts, 0)


def first_half(shape, axis):
    return lax.broadcasted_iota(jnp.int32, shape, axis) < HEAD


def padded_rows(block, fill):
    if block.shape[0] == KEYS:
        return block
    rest = (KEYS - block.shape[0], LANES)
    return jnp.concatenate([block, jnp.broadcast_to(fill, rest).astype(block.dtype)], 0)


def attend_kernel(slots, q_ref, k_ref, v_ref, vb_ref, tab_ref, att_ref, lse_ref):
    kf = key_fields(False)
    for s, (row, count, lane0) in enumerate(slots):
        rows = pl.ds(row, count)
        q2 = q_ref[rows, :]
        k2 = padded_rows(k_ref[rows, :] * bf16(HEAD ** -0.5), jnp.zeros((1, LANES), bf16))
        v2 = padded_rows(v_ref[rows, :], vb_ref[0:1, :])
        x2 = query_fields(q2, tab_ref[s])
        left = first_half((count, LANES), 1)
        leftk = first_half((KEYS, LANES), 1)
        outs = []
        for e in range(2):
            qa = jnp.where(left, q2, x2) if e == 0 else jnp.where(left, x2, q2)
            ka = jnp.where(leftk, k2, kf) if e == 0 else jnp.where(leftk, kf, k2)
            one = jnp.ones((KEYS, LANES), bf16)
            va = jnp.where(leftk, v2, one) if e == 0 else jnp.where(leftk, one, v2)
            st = dot_nt(ka, qa)
            peak = jnp.max(st, axis=0, keepdims=True)
            pt = jnp.exp(st - peak).astype(bf16)
            ot = dot_tn(va, pt)
            mass = ot[HEAD : HEAD + 1] if e == 0 else ot[0:1]
            lse_ref[0, e : e + 1, lane0 : lane0 + count] = peak + jnp.log(mass)
            outs.append(ot * (1.0 / mass))
        both = jnp.where(first_half((LANES, count), 0), outs[0], outs[1])
        att_ref[rows, :] = both.T.astype(bf16)


def attend_back_kernel(
    slots, q_ref, k_ref, v_ref, do_ref, lse_ref, vb_ref, tab_ref, tabb_ref,
    dqkv_ref, dtab_ref, dvb_ref,
):
    kf = key_fields(False)
    kb = key_fields(True)
    extra = jnp.zeros((1, LANES), f32)

    @pl.when(pl.program_id(0) == 0)
    def _():
        dtab_ref[...] = jnp.zeros_like(dtab_ref)

    for s, (row, count, lane0) in enumerate(slots):
        rows = pl.ds(row, count)
        q2 = q_ref[rows, :]
        do2 = do_ref[rows, :]
        k2 = padded_rows(k_ref[rows, :] * bf16(HEAD ** -0.5), jnp.zeros((1, LANES), bf16))
        v2 = padded_rows(v_ref[rows, :], vb_ref[0:1, :])
        x2 = query_fields(q2, tab_ref[s])
        left = first_half((count, LANES), 1)
        leftk = first_half((KEYS, LANES), 1)
        zero = jnp.zeros((KEYS, LANES), bf16)
        dq, dk, dv = [], [], []
        for e in range(2):
            qa = jnp.where(left, q2, x2) if e == 0 else jnp.where(left, x2, q2)
            ka = jnp.where(leftk, k2, kf) if e == 0 else jnp.where(leftk, kf, k2)
            kr = jnp.where(leftk, k2, kb) if e == 0 else jnp.where(leftk, kb, k2)
            va = jnp.where(leftk, v2, zero) if e == 0 else jnp.where(leftk, zero, v2)
            st = dot_nt(ka, qa)
            pt = jnp.exp(st - lse_ref[0, e : e + 1, lane0 : lane0 + count])
            dpt = dot_nt(va, do2)
            mean = jnp.sum(pt * dpt, axis=0, keepdims=True)
            dst = (pt * (dpt - mean)).astype(bf16)
            dv.append(dot_nn(pt.astype(bf16), do2))
            dk.append(dot_nn(dst, qa))
            dq.append(dot_tn(dst, kr))
        fields = jnp.where(left, dq[1], dq[0])
        dt = field_tables(fields)
        high = dt.astype(bf16)
        low = (dt - high.astype(f32)).astype(bf16)
        tabb = tabb_ref[s]
        dq2 = jnp.where(left, dq[0], dq[1]) + dot_nt(high, tabb) + dot_nt(low, tabb)
        dk2 = jnp.where(leftk, dk[0], dk[1]) * (HEAD ** -0.5)
        dv2 = jnp.where(leftk, dv[0], dv[1])
        dqkv_ref[0, rows, :] = dq2.astype(bf16)
        dqkv_ref[1, rows, :] = dk2[:count].astype(bf16)
        dqkv_ref[2, rows, :] = dv2[:count].astype(bf16)
        if count < KEYS:
            extra = extra + jnp.sum(dv2[count:], axis=0, keepdims=True)
        dtab_ref[s] += dot_tn(q2, high) + dot_tn(q2, low)
    dvb_ref[0] = jnp.broadcast_to(extra, (8, LANES))


def slot_places(counts):
    places, row, lane = [], 0, 0
    for count in counts:
        places.append((row, count, lane))
        row += count
        lane += -(-count // LANES) * LANES
    return tuple(places), row, lane


def attend(projected, bias_v, tables, counts, first, count):
    slots, rows, lanes = slot_places(counts)
    width = projected.shape[1] // 3
    pairs = width // LANES
    col = lambda off: pl.BlockSpec((rows, LANES), lambda p: (0, off * pairs + first + p))
    return pl.pallas_call(
        lambda *refs: attend_kernel(slots, *refs),
        grid=(count,),
        in_specs=[
            col(0), col(1), col(2),
            pl.BlockSpec((8, LANES), lambda p: (0, first + p)),
            pl.BlockSpec((len(counts), LANES, LANES), lambda p: (0, 0, 0)),
        ],
        out_specs=[
            pl.BlockSpec((rows, LANES), lambda p: (0, p)),
            pl.BlockSpec((1, 8, lanes), lambda p: (p, 0, 0)),
        ],
        out_shape=[
            jax.ShapeDtypeStruct((rows, count * LANES), bf16),
            jax.ShapeDtypeStruct((count, 8, lanes), f32),
        ],
        compiler_params=pltpu.CompilerParams(vmem_limit_bytes=48 << 20),
        cost_estimate=pl.CostEstimate(flops=COST, bytes_accessed=1024, transcendentals=0),
        name="attend",
    )(projected, projected, projected, bias_v, tables)


def attend_back(projected, upstream, lse, bias_v, tables, tables_back, counts, first):
    count = lse.shape[0]
    slots, rows, lanes = slot_places(counts)
    width = projected.shape[1] // 3
    pairs = width // LANES
    col = lambda off: pl.BlockSpec((rows, LANES), lambda p: (0, off * pairs + first + p))
    n = len(counts)
    return pl.pallas_call(
        lambda *refs: attend_back_kernel(slots, *refs),
        grid=(count,),
        in_specs=[
            col(0), col(1), col(2), col(0),
            pl.BlockSpec((1, 8, lanes), lambda p: (p, 0, 0)),
            pl.BlockSpec((8, LANES), lambda p: (0, first + p)),
            pl.BlockSpec((n, LANES, LANES), lambda p: (0, 0, 0)),
            pl.BlockSpec((n, LANES, LANES), lambda p: (0, 0, 0)),
        ],
        out_specs=[
            pl.BlockSpec((3, rows, LANES), lambda p: (0, 0, p)),
            pl.BlockSpec((n, LANES, LANES), lambda p: (0, 0, 0)),
            pl.BlockSpec((1, 8, LANES), lambda p: (p, 0, 0)),
        ],
        out_shape=[
            jax.ShapeDtypeStruct((3, rows, count * LANES), bf16),
            jax.ShapeDtypeStruct((n, LANES, LANES), f32),
            jax.ShapeDtypeStruct((count, 8, LANES), f32),
        ],
        compiler_params=pltpu.CompilerParams(vmem_limit_bytes=48 << 20),
        cost_estimate=pl.CostEstimate(flops=COST, bytes_accessed=1024, transcendentals=0),
        name="attend_back",
    )(projected, projected, projected, upstream, lse, bias_v, tables, tables_back)


def sides(index):
    return WIN * index, min(WIN * index + WIN, GRID)


class Plan:
    def __init__(self, rows, cols, images):
        self.rows, self.cols, self.images = rows, cols, images
        self.devices = rows * cols
        self.tile_rows, self.tile_cols = GRID // rows, GRID // cols
        self.tokens = images * self.tile_rows * self.tile_cols
        kinds = ([], [], [])
        for n in range(images):
            for i in range(NWIN):
                for j in range(NWIN):
                    kinds[(i == NWIN - 1) + (j == NWIN - 1)].append((n, i, j))
        self.caps = tuple(-(-len(kind) // self.devices) for kind in kinds)
        self.parts = {w: self._sources(w) for kind in kinds for w in kind}
        owner = self._assign(kinds)
        self.counts = (KEYS,) * self.caps[0] + (EDGE * PITCH,) * (self.caps[1] + self.caps[2])
        _, self.window_rows, _ = slot_places(self.counts)
        self._tables(kinds, owner)

    def _distance(self, one, two):
        r, c = divmod(one, self.cols)
        q, e = divmod(two, self.cols)
        return abs(c - e) + abs(r // 2 - q // 2) + (0.125 if r % 2 != q % 2 else 0.0)

    def _sources(self, window):
        _, i, j = window
        (r0, r1), (c0, c1) = sides(i), sides(j)
        tr, tc = self.tile_rows, self.tile_cols
        found = {}
        for r in range(r0 // tr, (r1 - 1) // tr + 1):
            for c in range(c0 // tc, (c1 - 1) // tc + 1):
                high = min(r1, (r + 1) * tr) - max(r0, r * tr)
                wide = min(c1, (c + 1) * tc) - max(c0, c * tc)
                found[r * self.cols + c] = high * wide
        return found

    def _rounds(self, owner):
        pairs = {}
        for window, dev in owner.items():
            for source, amount in self.parts[window].items():
                if source != dev:
                    pairs[source, dev] = pairs.get((source, dev), 0) + amount
        rounds = []
        for pair, amount in sorted(pairs.items(), key=lambda p: (-p[1], p[0])):
            for senders, takers, members in rounds:
                if pair[0] not in senders and pair[1] not in takers:
                    break
            else:
                senders, takers, members = set(), set(), []
                rounds.append((senders, takers, members))
            senders.add(pair[0])
            takers.add(pair[1])
            members.append(pair)
        return pairs, [members for _, _, members in rounds]

    def _cost(self, owner):
        pairs, rounds = self._rounds(owner)
        moved = sum(amount * self._distance(*pair) for pair, amount in pairs.items())
        return moved / 4 + sum(64 + max(pairs[p] for p in members) for members in rounds)

    def _assign(self, kinds):
        owner = {}
        room = {}
        for kind, windows in enumerate(kinds):
            room[kind] = [self.caps[kind]] * self.devices
            for window in sorted(windows, key=lambda w: (-(w[1] + w[2]), w)):
                far = lambda d: sum(t * self._distance(s, d) for s, t in self.parts[window].items())
                dev = min((d for d in range(self.devices) if room[kind][d]), key=lambda d: (far(d), d))
                owner[window] = dev
                room[kind][dev] -= 1
        best = self._cost(owner)
        for _ in range(4):
            before = best
            for kind in (1, 2, 0):
                for one in kinds[kind]:
                    for dev in range(self.devices):
                        if dev == owner[one]:
                            continue
                        trials = []
                        if room[kind][dev]:
                            trials.append({**owner, one: dev})
                        for two in kinds[kind]:
                            if owner[two] == dev:
                                trials.append({**owner, one: dev, two: owner[one]})
                        for trial in trials:
                            price = self._cost(trial)
                            if price < best - 1e-9:
                                if sum(trial[w] != owner[w] for w in kinds[kind]) == 1:
                                    room[kind][owner[one]] += 1
                                    room[kind][dev] -= 1
                                owner, best = trial, price
                                break
            if best >= before:
                break
        return owner

    def _tables(self, kinds, owner):
        places, _, _ = slot_places(self.counts)
        starts = (0, self.caps[0], self.caps[0] + self.caps[1])
        self.swapped = np.zeros((self.devices, len(self.counts)), np.int32)
        taken = {}
        moves = {}
        for kind, windows in enumerate(kinds):
            for window in windows:
                n, i, j = window
                dev = owner[window]
                slot = starts[kind] + taken.get((dev, kind), 0)
                taken[dev, kind] = taken.get((dev, kind), 0) + 1
                swap = kind == 1 and j == NWIN - 1
                self.swapped[dev, slot] = swap
                (r0, r1), (c0, c1) = sides(i), sides(j)
                for r in range(r0, r1):
                    for c in range(c0, c1):
                        a, b = (c - c0, r - r0) if swap else (r - r0, c - c0)
                        row = places[slot][0] + PITCH * a + b
                        source = (r // self.tile_rows) * self.cols + c // self.tile_cols
                        token = (n * self.tile_rows + r % self.tile_rows) * self.tile_cols
                        token += c % self.tile_cols
                        moves.setdefault((source, dev), []).append((token, row))
        _, rounds = self._rounds(owner)
        self.perms = rounds
        self.sizes = [-(-max(len(moves[p]) for p in members) // PITCH) * PITCH for members in rounds]
        total = sum(self.sizes)
        self.pack = np.full((self.devices, total), -1, np.int32)
        self.take = np.full((self.devices, self.window_rows), -1, np.int32)
        self.pack_back = np.full((self.devices, total), -1, np.int32)
        self.take_back = np.full((self.devices, self.tokens), -1, np.int32)
        for dev in range(self.devices):
            for token, row in moves.get((dev, dev), ()):
                self.take[dev, row] = token
                self.take_back[dev, token] = row
        at = 0
        for members, size in zip(rounds, self.sizes):
            for source, dev in members:
                for k, (token, row) in enumerate(moves[source, dev]):
                    self.pack[source, at + k] = token
                    self.take[dev, row] = self.tokens + at + k
                    self.pack_back[dev, at + k] = row
                    self.take_back[source, token] = self.window_rows + at + k
            at += size


def chosen(index, start, count):
    spot = lax.broadcasted_iota(jnp.int32, (count, index.shape[1]), 0) + start
    return jnp.where(spot == index, 1.0, 0.0).astype(bf16)


def pack_kernel(sizes, index_ref, *refs):
    token_refs, out_refs = refs[: len(refs) - len(sizes)], refs[len(refs) - len(sizes) :]
    at = 0
    for size, out_ref in zip(sizes, out_refs):
        hot = chosen(index_ref[0:1, at : at + size], 0, token_refs[0].shape[0])
        for k, ref in enumerate(token_refs):
            width = ref.shape[1]
            moved = dot_tn(hot, ref[...].astype(bf16)).astype(bf16)
            out_ref[:, width * k : width * (k + 1)] = moved
        at += size


def pack(index, tokens, sizes):
    width = sum(t.shape[1] for t in tokens)
    return pl.pallas_call(
        lambda *refs: pack_kernel(sizes, *refs),
        out_shape=[jax.ShapeDtypeStruct((size, width), bf16) for size in sizes],
        compiler_params=pltpu.CompilerParams(vmem_limit_bytes=40 << 20),
        cost_estimate=cost(0),
        name="pack",
    )(index[None], *tokens)


def take_kernel(count, masked, index_ref, *refs):
    local_refs, arrived, out_refs = refs[:count], refs[count : -count - masked], refs[-count - masked :]
    index = index_ref[...]
    at = local_refs[0].shape[0]
    hot = chosen(index, 0, at)
    totals = []
    for ref in local_refs:
        local = ref[...]
        total = dot_tn(hot, local.astype(bf16))
        if local.dtype == f32:
            total = total + dot_tn(hot, (local - local.astype(bf16).astype(f32)).astype(bf16))
        totals.append(total)
    for ref in arrived:
        hot = chosen(index, at, ref.shape[0])
        width = ref.shape[1] // count
        totals = [
            t + dot_tn(hot, ref[:, width * k : width * (k + 1)]) for k, t in enumerate(totals)
        ]
        at += ref.shape[0]
    for ref, total in zip(out_refs, totals):
        ref[...] = total.astype(ref.dtype)
    if masked:
        row = jnp.where(index >= 0, 1.0, 0.0)
        out_refs[-1][...] = jnp.broadcast_to(row, (LANES, row.shape[1])).T


def take(index, locals_, arrived, masked=False):
    shapes = [((index.shape[0], local.shape[1]), local.dtype) for local in locals_]
    if masked:
        shapes.append(((index.shape[0], LANES), f32))
    return pl.pallas_call(
        lambda *refs: take_kernel(len(locals_), int(masked), *refs),
        out_shape=[jax.ShapeDtypeStruct(*shape) for shape in shapes],
        compiler_params=pltpu.CompilerParams(vmem_limit_bytes=40 << 20),
        cost_estimate=cost(0),
        name="take",
    )(index[None], *locals_, *arrived)


class Mover:
    def __init__(self, plan):
        self.plan = plan
        here = lax.axis_index("row") * plan.cols + lax.axis_index("col")
        mine = lambda table: lax.dynamic_index_in_dim(jnp.asarray(table), here, 0, keepdims=False)
        self.index = {name: mine(getattr(plan, name)) for name in ("pack", "take", "pack_back", "take_back")}
        self.swapped = mine(plan.swapped)

    def pack(self, *tokens):
        return pack(self.index["pack"], tokens, self.plan.sizes)

    def send(self, packed):
        return [lax.ppermute(s, ("row", "col"), perm) for s, perm in zip(packed, self.plan.perms)]

    def receive(self, *tokens, arrived, masked=False):
        return take(self.index["take"], tokens, arrived, masked)

    def pack_back(self, *rows):
        return pack(self.index["pack_back"], rows, self.plan.sizes)

    def send_back(self, packed):
        back = [[(two, one) for one, two in perm] for perm in self.plan.perms]
        return [lax.ppermute(s, ("row", "col"), perm) for s, perm in zip(packed, back)]

    def receive_back(self, *rows, arrived):
        return take(self.index["take_back"], rows, arrived)


AXES = ("dp", "row", "col")
TORUS = (2, 4, 4)


def order(*values):
    return lax.optimization_barrier(values)


def over_dp(v):
    return lax.ppermute(v, "dp", [(0, 1), (1, 0)])


def over_y(v):
    return lax.ppermute(v, "row", [(r, (r + 2) % 4) for r in range(4)])


def over_both(v):
    return lax.ppermute(v, ("dp", "row"), [(k, (k // 4 + 1) % 2 * 4 + (k % 4 + 2) % 4) for k in range(8)])


def over_core(v):
    return lax.ppermute(v, "row", [(r, r ^ 1) for r in range(4)])


def over_col(v, steps):
    return lax.ppermute(v, "col", [(c, (c + steps) % 4) for c in range(4)])


def block_at(flip_dp, flip_y, flip_core):
    dp, row = lax.axis_index("dp"), lax.axis_index("row")
    return (
        ((dp + flip_dp) % 2) * 4 + ((row // 2 + flip_y) % 2) * 2 + (row % 2 + flip_core) % 2
    )


KINDS = ((0, 0), (1, 0), (0, 1), (1, 1))


def column_kernel(store, *refs):
    seen, out_ref = refs[:4], refs[4]
    place = lax.axis_index("col")
    for j in range(4):
        for k in range(4):

            @pl.when((place - j) % 4 == k)
            def _():
                store(out_ref, j, seen[k])


def in_column(shard, store, shape):
    seen = [shard] + [over_col(shard, k) for k in (1, 2, 3)]
    return pl.pallas_call(
        lambda *refs: column_kernel(store, *refs),
        out_shape=jax.ShapeDtypeStruct(shape, bf16),
        cost_estimate=cost(0),
        name="in_column",
    )(*seen)


SMALL = 8


def shards_kernel(qkv_ref, up_ref, down_ref, proj_ref, *refs):
    first_ref, planes_ref = refs[-2:]
    rows, width = proj_ref.shape
    for k in range(3):
        first_ref[rows * k : rows * (k + 1), :] = qkv_ref[:, width * k : width * (k + 1)]
    first_ref[3 * rows :, :] = jnp.zeros((SMALL, width), bf16)
    for k, ref in enumerate(refs[:-2]):
        first_ref[3 * rows + k : 3 * rows + k + 1, 0 : ref.shape[1]] = ref[...]
    for k in range(4):
        planes_ref[0, k] = up_ref[:, width * k : width * (k + 1)]
        planes_ref[0, 4 + k] = down_ref[rows * k : rows * (k + 1), :]
    planes_ref[0, 8] = proj_ref[...]


def sent_shards(qkv_weight, up_weight, down_weight, proj_weight, small):
    rows, width = proj_weight.shape
    return pl.pallas_call(
        shards_kernel,
        out_shape=[
            jax.ShapeDtypeStruct((3 * rows + SMALL, width), bf16),
            jax.ShapeDtypeStruct((1, 9, rows, width), bf16),
        ],
        cost_estimate=cost(0),
        name="sent_shards",
    )(qkv_weight, up_weight, down_weight, proj_weight, *[v[None] for v in small])


def first_weights(shard):
    rows, width = (shard.shape[0] - SMALL) // 3, shard.shape[1]
    (shard,) = yield (shard,)

    def store(ref, j, shard):
        for plane in range(3):
            at = rows * (4 * plane + j)
            ref[at : at + rows, :] = shard[rows * plane : rows * (plane + 1), :]
        at = 12 * rows + SMALL * j
        ref[at : at + SMALL, :] = shard[3 * rows :, :]

    own = in_column(shard, store, (12 * rows + 4 * SMALL, width))
    (own,) = yield (own,)
    pieces = [own, over_dp(own), over_y(own), over_both(own)]
    pieces = yield pieces
    pieces = [*pieces, *[over_core(p) for p in pieces]]
    yield pieces


PAIR = 48


def put_rows(ref, at, value):
    high = value.astype(bf16)
    count = value.shape[0]
    ref[at : at + count, :] = high
    ref[at + count : at + 2 * count, :] = (value - high.astype(f32)).astype(bf16)


def both_rows(ref, at):
    half = PAIR // 2
    return ref[at : at + half, :].astype(f32) + ref[at + half : at + 2 * half, :].astype(f32)


def core_kernel(planes, small, mine_ref, came_ref, *refs):
    own_ref, sent_refs = refs[small], refs[small + 1 : small + 4]
    rows = mine_ref.shape[1]
    for plane in range(planes):
        at = rows * plane
        for k in range(4):
            total = mine_ref[4 * plane + k].astype(f32) + came_ref[4 * plane + k].astype(f32)
            if k:
                sent_refs[k - 1][at : at + rows, :] = total.astype(bf16)
            else:
                own_ref[at : at + rows, :] = total
    if small:
        high = came_ref[4 * planes]
        half = PAIR // 2
        total = refs[0][...] + high[:half].astype(f32) + high[half:PAIR].astype(f32)
        refs[-1][...] = total
        for ref in sent_refs:
            put_rows(ref, rows * planes, total)


def chips_kernel(planes, small, own_ref, dp_ref, y_ref, both_ref, *refs):
    mine_ref, sent_refs, column = refs[small], refs[small + 1 : small + 4], refs[-1]
    count = own_ref.shape[0] // planes // 4
    total = own_ref[...]
    for ref in (dp_ref, y_ref, both_ref):
        total = total + ref[: own_ref.shape[0], :].astype(f32)
    column[...] = total
    place = lax.axis_index("col")
    for k in range(4):
        for plane in range(planes):
            at = pl.multiple_of(4 * count * plane + (place + k) % 4 * count, count)
            rows = column[pl.ds(at, count), :]
            if k:
                sent_refs[k - 1][count * plane : count * (plane + 1), :] = rows.astype(bf16)
            else:
                mine_ref[plane] = rows
    if small:
        total = refs[0][...]
        for ref in (dp_ref, y_ref, both_ref):
            total = total + both_rows(ref, own_ref.shape[0])
        refs[-2][...] = total
        for ref in sent_refs:
            put_rows(ref, count * planes, total)


def column_sum_kernel(planes, small, mine_ref, *refs):
    came = refs[:3]
    out_refs = refs[3 + small :]
    count, width = mine_ref.shape[1:]
    for plane in range(planes):
        total = mine_ref[plane]
        for ref in came:
            total = total + ref[count * plane : count * (plane + 1), :].astype(f32)
        wide = out_refs[0].shape[1] // width
        if plane < wide:
            out_refs[0][:, width * plane : width * (plane + 1)] = total
        else:
            out_refs[1][...] = total
    if small:
        total = refs[3][...]
        for ref in came:
            total = total + both_rows(ref, count * planes)
        out_refs[-1][...] = total


def scatter_sum(mine, other, planes, small=None):
    rows, width = mine.shape[1:]
    extra = PAIR if small is not None else 0
    params = pltpu.CompilerParams(vmem_limit_bytes=40 << 20)
    shape = lambda kind, *dims: jax.ShapeDtypeStruct(dims, kind)
    has = int(small is not None)
    given = [small] if has else []
    sums = [shape(f32, PAIR // 2, width)] * has
    (other,) = yield (other,)
    came = over_core(other)
    (came,) = yield (came,)
    own, *rest = pl.pallas_call(
        lambda *refs: core_kernel(planes, has, *refs),
        out_shape=[shape(f32, planes * rows, width)]
        + [shape(bf16, planes * rows + extra, width)] * 3
        + sums,
        compiler_params=params,
        cost_estimate=cost(0),
        name="core_sum",
    )(mine, came, *given)
    own, *rest = yield (own, *rest)
    given = rest[3:]
    came = yield (over_dp(rest[0]), over_y(rest[1]), over_both(rest[2]))
    count = rows // 4
    mine, *rest = pl.pallas_call(
        lambda *refs: chips_kernel(planes, has, *refs),
        out_shape=[shape(f32, planes, count, width)]
        + [shape(bf16, planes * count + extra, width)] * 3
        + sums,
        scratch_shapes=[pltpu.VMEM((planes * rows, width), f32)],
        compiler_params=params,
        cost_estimate=cost(0),
        name="chips_sum",
    )(own, *came, *given)
    mine, *rest = yield (mine, *rest)
    given = rest[3:]
    came = yield [over_col(v, k) for k, v in zip((1, 2, 3), rest)]
    wide = min(planes, 4)
    yield pl.pallas_call(
        lambda *refs: column_sum_kernel(planes, has, *refs),
        out_shape=[shape(f32, count, wide * width)]
        + [shape(f32, count, width)] * (planes - wide)
        + sums,
        compiler_params=params,
        cost_estimate=cost(0),
        name="column_sum",
    )(mine, *came, *given)


class Steps:
    def __init__(self, steps):
        self.steps = steps
        self.arrays = tuple(next(steps))

    def __call__(self, *values):
        values, arrays = lax.optimization_barrier((values, self.arrays))
        self.arrays = tuple(self.steps.send(arrays))
        return values if len(values) != 1 else values[0]


def on_torus():
    return tuple(lax.axis_size(a) for a in AXES) == TORUS


def device_number():
    return (lax.axis_index("dp") * lax.axis_size("row") + lax.axis_index("row")) * lax.axis_size(
        "col"
    ) + lax.axis_index("col")


def gather_at_once(*shards):
    return tuple(lax.all_gather(s, AXES, axis=0, tiled=True) for s in shards)


def sum_at_once(grad):
    return lax.psum_scatter(grad, AXES, scatter_dimension=0, tiled=True)


SPREAD = 0.3275911
TAIL_COEFFICIENTS = (0.1850680112838745, 0.18050004541873932, 0.20733030140399933, 0.020621487870812416, 0.46248844265937805, -0.41615772247314453, 0.5027683973312378, -0.14261901378631592)


def normal_parts(u):
    z = jnp.abs(u) * (2.0 ** -0.5)
    t = 1.0 / (1.0 + SPREAD * z)
    bell = jnp.exp(-0.5 * u * u)
    total = jnp.full_like(t, TAIL_COEFFICIENTS[-1])
    for coefficient in TAIL_COEFFICIENTS[-2::-1]:
        total = total * t + coefficient
    tail = 0.5 * total * t * bell
    return jnp.where(u < 0, tail, 1.0 - tail), bell * (2.0 * math.pi) ** -0.5


def normalize(values):
    center = values - jnp.mean(values, axis=-1, keepdims=True)
    inverse = lax.rsqrt(jnp.mean(center * center, axis=-1, keepdims=True) + epsilon)
    return center * inverse, inverse


def norm_back(upstream, normed, inverse, gain):
    scaled = upstream * gain
    inner = jnp.mean(scaled, axis=-1, keepdims=True)
    cross = jnp.mean(scaled * normed, axis=-1, keepdims=True)
    result = inverse * (scaled - inner - normed * cross)
    sums = [jnp.sum(v, axis=0, keepdims=True) for v in (upstream * normed, upstream)]
    return result, sums


def store_blocks(grad, kept, refs, first):
    rows = grad.shape[0] // 8
    if kept is not None:
        kept[...] = grad
    for core, ref in enumerate(refs):
        for k, kind in enumerate(KINDS):
            if kept is None:
                at = rows * (4 * core + k)
                ref[first + k] = grad[at : at + rows].astype(bf16)
            else:
                at = pl.multiple_of(block_at(*kind, core) * rows, rows)
                ref[first + k] = kept[pl.ds(at, rows), :].astype(bf16)


def stacked_rows(rows):
    spare = jnp.zeros((8 - len(rows), rows[0].shape[1]), f32)
    return jnp.concatenate([*rows, spare], 0)


def spread(count, width):
    return jnp.asarray(np.arange(width)[None] % count == np.arange(LANES)[:, None], bf16)


QV, PROJ_ADD, GAIN_ONE, SHIFT_ONE, GAIN_TWO, SHIFT_TWO, UP_ADD, DOWN_ADD = range(8)
HELD = (48, 24, 24, 24, 24, 24, 96, 24)


def row(ref, k):
    return ref[k : k + 1, :]


def vectors_kernel(*refs):
    pieces, spreads = refs[:8], refs[8:11]
    vecs_ref, up_add_ref, bias_ref, bias_v_ref = refs[11:]
    rows = jnp.concatenate([piece[:, 0:LANES] for piece in pieces], 0)
    whole = []
    for count, spread_ref in zip((24, 48, 96), spreads):
        wide = dot_nn(rows, spread_ref[...])
        total = jnp.zeros((SMALL, wide.shape[1]), f32)
        group = lax.broadcasted_iota(jnp.int32, total.shape, 1) // count
        for k in range(8):
            block = block_at(*KINDS[k % 4], k // 4)
            for col in range(4):
                at = SMALL * (4 * k + col)
                total = total + jnp.where(group == 4 * block + col, wide[at : at + SMALL], 0.0)
        whole.append(total)
    vecs_ref[...] = whole[0]
    up_add_ref[...] = whole[2]
    qv = whole[1][QV : QV + 1]
    width = vecs_ref.shape[1]
    bias_ref[...] = jnp.concatenate([qv[:, :width], jnp.zeros((1, width), f32), qv[:, width:]], 1)
    bias_v_ref[...] = jnp.broadcast_to(qv[:, width:], bias_v_ref.shape).astype(bf16)


def vectors(pieces):
    rows, width = pieces[0].shape
    spreads = [spread(count, 32 * count) for count in (24, 48, 96)]
    tail = pl.BlockSpec((4 * SMALL, width), lambda s: (rows // (4 * SMALL) - 1, 0))
    shapes = [((SMALL, width), f32), ((SMALL, 4 * width), f32), ((1, 3 * width), f32), ((8, width), bf16)]
    return pl.pallas_call(
        vectors_kernel,
        grid=(1,),
        in_specs=[tail] * 8 + [whole_spec(s) for s in spreads],
        out_specs=[pl.BlockSpec(shape, lambda s: (0, 0)) for shape, _ in shapes],
        out_shape=[jax.ShapeDtypeStruct(*shape) for shape in shapes],
        cost_estimate=cost(0),
        name="vectors",
    )(*pieces, *spreads)


def gathered_vectors(small):
    whole = [v.astype(f32) for v in gather_at_once(*small)]
    width = whole[PROJ_ADD].shape[0]
    none = jnp.zeros((width,), f32)
    vecs = jnp.stack([v if v.shape[0] == width else none for v in whole])
    up_add = jnp.broadcast_to(whole[UP_ADD][None], (SMALL, 4 * width))
    query, value = whole[QV][:width], whole[QV][width:]
    bias = jnp.concatenate([query, none, value])[None]
    return vecs, up_add, bias, jnp.broadcast_to(value[None], (8, width)).astype(bf16)


def assemble(target, pieces):
    for k, piece in enumerate(pieces):
        if piece is None:
            continue
        rows = piece.shape[-2]
        at = pl.multiple_of(block_at(*KINDS[k % 4], k // 4) * rows, rows)
        target[pl.ds(at, rows), :] = piece[...].reshape(rows, piece.shape[-1])


def qkv_ahead_kernel(x_ref, real_ref, vecs_ref, bias_ref, *refs):
    weight_refs, (hidden_ref, out_ref, w_ref) = refs[:-3], refs[-3:]

    @pl.when(pl.program_id(0) == 0)
    def _():
        plain, _ = normalize(x_ref[...].astype(f32))
        hidden = plain * row(vecs_ref, GAIN_ONE) + row(vecs_ref, SHIFT_ONE)
        hidden = hidden * real_ref[:, 0:1]
        hidden_ref[...] = hidden.astype(bf16)

    if len(weight_refs) == 1:
        w_ref[...] = weight_refs[0][...]
    else:
        assemble(w_ref, weight_refs)
    out_ref[...] = (dot_nn(hidden_ref[...], w_ref[...]) + bias_ref[...]).astype(bf16)


def join_rows(target, source, planes):
    rows = source.shape[2]
    at = 0
    for device in range(source.shape[0]):
        for plane in range(planes):
            target[at : at + rows, :] = source[device, plane]
            at += rows


def up_kernel(x_ref, a0_ref, a1_ref, a2_ref, vecs_ref, up_add_ref, w_ref, p_ref, *refs):
    middle_ref, second_ref, active_ref, slope_ref, up_ref, proj_ref = refs
    pieced = len(w_ref.shape) > 2

    @pl.when(pl.program_id(0) == 0)
    def _():
        if pieced:
            join_rows(proj_ref, p_ref, 1)
        else:
            proj_ref[...] = p_ref[...]
        middle = x_ref[...].astype(f32) + row(vecs_ref, PROJ_ADD)
        for k, ref in enumerate((a0_ref, a1_ref, a2_ref)):
            size = ref.shape[1]
            middle = middle + dot_nn(ref[...], proj_ref[size * k : size * (k + 1), :])
        plain, _ = normalize(middle)
        middle_ref[...] = middle
        second = plain * row(vecs_ref, GAIN_TWO) + row(vecs_ref, SHIFT_TWO)
        second_ref[...] = second.astype(bf16)

    if pieced:
        join_rows(up_ref, w_ref, 1)
    else:
        up_ref[...] = w_ref[...]
    inner = dot_nn(second_ref[...], up_ref[...]) + row(up_add_ref, UP_ADD)
    below, density = normal_parts(inner)
    active_ref[...] = (inner * below).astype(bf16)
    slope_ref[...] = below + inner * density


def down_kernel(active_ref, slope_ref, middle_ref, g_ref, vecs_ref, w_ref, *refs):
    out_ref, grad_ref, inner_grad_ref, up_add_grad_ref, total = refs[:5]
    step = pl.program_id(0)

    @pl.when(step == 0)
    def _():
        total[...] = middle_ref[...] + row(vecs_ref, DOWN_ADD)

    if len(w_ref.shape) > 2:
        join_rows(refs[5], w_ref, 4)
        down = refs[5][...]
    else:
        down = w_ref[...]
    active = active_ref[...]
    g = g_ref[...]
    inner_grad = (dot_nt(g, down) * slope_ref[...]).astype(bf16)
    inner_grad_ref[...] = inner_grad
    up_add_grad_ref[...] = jnp.broadcast_to(
        jnp.sum(inner_grad.astype(f32), axis=0, keepdims=True), up_add_grad_ref.shape
    )
    total[...] += dot_nn(active, down)
    grad_ref[...] = dot_tn(active, g).astype(bf16)

    @pl.when(step == pl.num_programs(0) - 1)
    def _():
        out_ref[...] = total[...].astype(bf16)


def mlp_back_kernel(
    pieced, second_ref, inner_grad_ref, up_ref, middle_ref, g_ref, a0_ref, a1_ref, a2_ref, proj_ref,
    vecs_ref, mine_ref, other_ref, middle_grad_ref, attended_grad_ref, sums_ref, total, kept,
):
    step = pl.program_id(0)
    last = pl.num_programs(0) - 1

    def store(grad):
        store_blocks(grad, kept if pieced else None, (mine_ref, other_ref), 0)

    @pl.when(step == 0)
    def _():
        total[...] = jnp.zeros_like(total)

    @pl.when(step < last)
    def _():
        inner_grad = inner_grad_ref[...]
        total[...] += dot_nt(inner_grad, up_ref[...])
        store(dot_tn(second_ref[...], inner_grad))

    @pl.when(step == last)
    def _():
        plain, inverse = normalize(middle_ref[...])
        flow = g_ref[...].astype(f32)
        part, sums = norm_back(total[...], plain, inverse, row(vecs_ref, GAIN_TWO))
        middle_grad = flow + part
        middle_grad_ref[...] = middle_grad
        branch = middle_grad.astype(bf16)
        attended_grad_ref[...] = dot_nt(branch, proj_ref[...]).astype(bf16)
        store(jnp.concatenate([dot_tn(ref[...], branch) for ref in (a0_ref, a1_ref, a2_ref)], 0))
        column = lambda v: jnp.sum(v, axis=0, keepdims=True)
        sums_ref[...] = stacked_rows([*sums, column(branch.astype(f32)), column(flow)])


def qkv_back_kernel(
    pieced, swapped_ref, hidden_ref, d0_ref, d1_ref, d2_ref, w_ref, middle_grad_ref, x_ref, real_ref,
    vecs_ref, e0_ref, e1_ref, e2_ref, two_ref, up_ref, t0_ref, t1_ref, t2_ref,
    mine_ref, other_ref, images_grad_ref, small_ref, total, columns, kept,
):
    step = pl.program_id(0)

    @pl.when(step == 0)
    def _():
        total[...] = jnp.zeros_like(total)
        other_ref[other_ref.shape[0] - 1] = jnp.zeros(other_ref.shape[1:], bf16)

    back = jnp.concatenate([ref[0] for ref in (d0_ref, d1_ref, d2_ref)], 1)
    total[...] += dot_nt(back, w_ref[...])
    grad = dot_tn(hidden_ref[...], back)
    store_blocks(grad, kept if pieced else None, (mine_ref, other_ref), 4 * step)
    columns[step] = jnp.broadcast_to(
        jnp.sum(back.astype(f32), axis=0, keepdims=True), columns.shape[1:]
    )

    @pl.when(step == pl.num_programs(0) - 1)
    def _():
        hidden_grad = total[...].astype(bf16).astype(f32) * real_ref[:, 0:1]
        plain, inverse = normalize(x_ref[...].astype(f32))
        part, sums = norm_back(hidden_grad, plain, inverse, row(vecs_ref, GAIN_ONE))
        images_grad_ref[...] = middle_grad_ref[...] + part
        small_sums(
            swapped_ref, columns, (e0_ref, e1_ref, e2_ref), two_ref, sums, up_ref,
            (t0_ref, t1_ref, t2_ref), small_ref,
        )
        put_rows(other_ref.at[other_ref.shape[0] - 1], 0, small_ref[...])


def whole_spec(array):
    return pl.BlockSpec(array.shape, lambda s: (0,) * array.ndim)


def across(rows, width):
    return pl.BlockSpec((rows, width), lambda s: (0, s))


BIG = pltpu.CompilerParams(vmem_limit_bytes=56 << 20)


def qkv_ahead(x, real, vecs, bias, weights):
    rows, width = x.shape
    shard = width // 8
    if len(weights) == 1:
        specs = [across(width, width)]
    else:
        specs = [pl.BlockSpec((shard, width), lambda s: (s, 0))] * 8
    return pl.pallas_call(
        qkv_ahead_kernel,
        grid=(3,),
        in_specs=[
            whole_spec(x), whole_spec(real), whole_spec(vecs), across(1, width), *specs,
        ],
        out_specs=[whole_spec(x), across(rows, width), across(width, width)],
        out_shape=[
            jax.ShapeDtypeStruct((rows, width), bf16),
            jax.ShapeDtypeStruct((rows, 3 * width), bf16),
            jax.ShapeDtypeStruct((width, 3 * width), bf16),
        ],
        compiler_params=BIG,
        cost_estimate=cost(5 * 10**9),
        name="qkv_ahead",
    )(x, real, vecs, bias, *weights)


def up_ahead(x, attended, vecs, up_add, weights):
    rows, width = x.shape
    if len(weights) == 2:
        specs = [across(width, width), whole_spec(weights[1])]
    else:
        (planes,) = weights
        one = (planes.shape[0], 1, *planes.shape[2:])
        specs = [pl.BlockSpec(one, lambda s: (0, s, 0, 0)), pl.BlockSpec(one, lambda s: (0, 8, 0, 0))]
        weights = planes, planes
    block = lambda s: (0, 0)
    outs = [
        (pl.BlockSpec((rows, width), block), (rows, width), f32),
        (pl.BlockSpec((rows, width), block), (rows, width), bf16),
        (across(rows, width), (rows, 4 * width), bf16),
        (across(rows, width), (rows, 4 * width), f32),
        (across(width, width), (width, 4 * width), bf16),
        (pl.BlockSpec((width, width), block), (width, width), bf16),
    ]
    return pl.pallas_call(
        up_kernel,
        grid=(4,),
        in_specs=[
            whole_spec(x), *[whole_spec(a) for a in attended], whole_spec(vecs), across(8, width),
            *specs,
        ],
        out_specs=[spec for spec, _, _ in outs],
        out_shape=[jax.ShapeDtypeStruct(shape, kind) for _, shape, kind in outs],
        compiler_params=BIG,
        cost_estimate=cost(15 * 10**9),
        name="up_ahead",
    )(x, *attended, vecs, up_add, *weights)


def down_ahead(active, slope, middle, g, vecs, weight):
    rows, width = middle.shape
    below = pl.BlockSpec((width, width), lambda s: (s, 0))
    scratch = [pltpu.VMEM((rows, width), f32)]
    spec = below
    if len(weight.shape) > 2:
        devices, _, *tile = weight.shape
        spec = pl.BlockSpec((devices // 4, 4, *tile), lambda s: (s, 1, 0, 0))
        scratch.append(pltpu.VMEM((width, width), bf16))
    outs = [
        (pl.BlockSpec((rows, width), lambda s: (0, 0)), (rows, width), bf16),
        (below, (4 * width, width), bf16),
        (across(rows, width), (rows, 4 * width), bf16),
        (across(8, width), (8, 4 * width), f32),
    ]
    return pl.pallas_call(
        down_kernel,
        grid=(4,),
        in_specs=[
            across(rows, width), across(rows, width), whole_spec(middle), whole_spec(g),
            whole_spec(vecs), spec,
        ],
        out_specs=[spec for spec, _, _ in outs],
        out_shape=[jax.ShapeDtypeStruct(shape, kind) for _, shape, kind in outs],
        scratch_shapes=scratch,
        compiler_params=BIG,
        cost_estimate=cost(15 * 10**9),
        name="down_ahead",
    )(active, slope, middle, g, vecs, weight)


def mlp_back(second, inner_grad, up, middle, g, attended, proj, vecs, pieced):
    rows, width = second.shape
    shard = width // 8
    sums = jax.ShapeDtypeStruct((8, width), f32)
    upto = lambda count: pl.BlockSpec((count, width), lambda s: (0, jnp.minimum(s, 3)))
    block = pl.BlockSpec((4, shard, width), lambda s: (s, 0, 0))
    planes = jax.ShapeDtypeStruct((4 * 5, shard, width), bf16)
    return pl.pallas_call(
        lambda *refs: mlp_back_kernel(pieced, *refs),
        grid=(5,),
        in_specs=[
            whole_spec(second), upto(rows), upto(width), whole_spec(middle), whole_spec(g),
            *[whole_spec(a) for a in attended], whole_spec(proj), whole_spec(vecs),
        ],
        out_specs=[block, block, whole_spec(second), whole_spec(second), whole_spec(sums)],
        out_shape=[
            planes,
            planes,
            jax.ShapeDtypeStruct((rows, width), f32),
            jax.ShapeDtypeStruct((rows, width), bf16),
            sums,
        ],
        scratch_shapes=[pltpu.VMEM((rows, width), f32), pltpu.VMEM((width, width), f32)],
        compiler_params=BIG,
        cost_estimate=cost(15 * 10**9),
        name="mlp_back",
    )(second, inner_grad, up, middle, g, *attended, proj, vecs)


def qkv_back(hidden, pieces, weight, middle_grad, x, real, vecs, swapped, small, pieced):
    rows, width = hidden.shape
    shard = width // 8
    extra, two, up, tables = small
    whole = lambda a: pl.BlockSpec(a.shape, lambda s, w: (0,) * len(a.shape))
    shape = lambda kind, *dims: jax.ShapeDtypeStruct(dims, kind)
    outs = [
        shape(bf16, 12, shard, width), shape(bf16, 13, shard, width), shape(f32, rows, width),
        shape(f32, SUM_ROWS, width),
    ]
    return pl.pallas_call(
        lambda *refs: qkv_back_kernel(pieced, *refs),
        grid_spec=pltpu.PrefetchScalarGridSpec(
            num_scalar_prefetch=1,
            grid=(3,),
            in_specs=[
                whole(hidden),
                *[pl.BlockSpec((1, *p.shape[1:]), lambda s, w: (s, 0, 0)) for p in pieces],
                pl.BlockSpec((width, width), lambda s, w: (0, s)),
                *[whole(a) for a in (middle_grad, x, real, vecs, *extra, two, up, *tables)],
            ],
            out_specs=[whole(out) for out in outs],
            scratch_shapes=[
                pltpu.VMEM((rows, width), f32),
                pltpu.VMEM((3, 8, width), f32),
                pltpu.VMEM((width, width), f32),
            ],
        ),
        out_shape=outs,
        compiler_params=BIG,
        cost_estimate=cost(10**10),
        name="qkv_back",
    )(swapped, hidden, *pieces, weight, middle_grad, x, real, vecs, *extra, two, up, *tables)


SUM_ROWS = 24
SUM_AT = dict(query=0, value=1, proj=2, pre=3, mid=5, up=7, down=11, tables=16)


def small_sums(swapped_ref, column_ref, extra_refs, two_ref, one, up_ref, table_refs, out_ref):
    width = out_ref.shape[1]
    out_ref[...] = jnp.zeros_like(out_ref)

    def put(name, value, more=0):
        at = SUM_AT[name] + more
        out_ref[at : at + 1, :] = value

    put("query", column_ref[0, 0:1, :])
    extra = jnp.concatenate([ref[p, 0:1, :] for ref in extra_refs for p in range(ref.shape[0])], 1)
    put("value", column_ref[2, 0:1, :] + extra)
    put("proj", two_ref[2:3, :])
    for k in range(2):
        put("pre", one[k], k)
        put("mid", two_ref[k : k + 1, :], k)
    for k in range(4):
        put("up", up_ref[0:1, width * k : width * (k + 1)], k)
    put("down", two_ref[3:4, :])
    count = 32
    sums = [jnp.zeros((count, HEAD), f32) for _ in range(2)]
    for s in range(table_refs[0].shape[0]):
        grad = table_refs[0][s]
        for ref in table_refs[1:]:
            grad = grad + ref[s]
        both = (grad[:HEAD, HEAD:] + grad[HEAD:, :HEAD]).T
        parts = (both[:count], both[COLTABLE : COLTABLE + count])
        swap = swapped_ref[s] != 0
        sums[0] = sums[0] + jnp.where(swap, parts[1], parts[0])
        sums[1] = sums[1] + jnp.where(swap, parts[0], parts[1])
    tables = jnp.concatenate(sums, 1)
    at = SUM_AT["tables"]
    for k in range(4):
        out_ref[at : at + 8, LANES * k : LANES * (k + 1)] = tables[8 * k : 8 * k + 8]


def split_sums(total):
    count = lax.axis_size("dp") * lax.axis_size("row") * lax.axis_size("col")
    width = total.shape[1]

    def share(name, more=0, rows=1):
        at = SUM_AT[name] + more
        size = rows * width // count
        return lax.dynamic_slice(total[at : at + rows].reshape(-1), (device_number() * size,), (size,))

    at = SUM_AT["tables"]
    tables = jnp.concatenate([total[at : at + 8, LANES * k : LANES * (k + 1)] for k in range(4)], 0)
    tables = tables[: 2 * WIN - 1]
    vectors = (
        share("query", 0, 2), share("proj"), share("pre"), share("pre", 1), share("mid"),
        share("mid", 1), share("up", 0, 4), share("down"),
    )
    return vectors, (tables[:, :HEAD], tables[:, HEAD:])


def body(
    images, qkv_weight, qv_bias, proj_weight, proj_bias, pre_gain, pre_shift, mid_gain, mid_shift,
    up_weight, up_bias, down_weight, down_bias, rel_rows, rel_cols, cotangent,
):
    width = images.shape[-1]
    torus = on_torus()
    plan = plan_for(lax.axis_size("row"), lax.axis_size("col"), images.shape[0] * images.shape[1])
    move = Mover(plan)
    counts = plan.counts
    groups = (0, 2, 4)
    small = (qv_bias, proj_bias, pre_gain, pre_shift, mid_gain, mid_shift, up_bias, down_bias)
    pixels, cot = images.reshape(-1, width), cotangent.reshape(-1, width)
    swapped = move.swapped

    if torus:
        shard, planes = sent_shards(qkv_weight, up_weight, down_weight, proj_weight, small)
        first_steps = Steps(first_weights(shard))
        first_steps()
        (planes,) = gather_at_once(planes)
        up_pieces, down_pieces = (planes,), planes
        sent, cot = first_steps(move.send(move.pack(pixels)), cot)
        x, real = move.receive(pixels, arrived=sent, masked=True)
        x, rel_rows, cot = order(x, rel_rows, cot)
        tables, tables_back = position_tables(swapped, rel_rows, rel_cols)
        cot_sent = move.send(move.pack(cot))
        tables, cot_sent = first_steps(tables, cot_sent)
        (g,) = move.receive(cot, arrived=cot_sent)
        qkv = first_steps.arrays
        vecs, up_add, bias, bias_v = vectors(qkv)
    else:
        sent = move.send(move.pack(pixels, cot))
        x, g, real = move.receive(pixels, cot, arrived=sent, masked=True)
        whole_qkv, proj, up, down = gather_at_once(qkv_weight, proj_weight, up_weight, down_weight)
        qkv, up_pieces, down_pieces = (whole_qkv,), (up, proj), down
        tables, tables_back = position_tables(swapped, rel_rows, rel_cols)
        vecs, up_add, bias, bias_v = gathered_vectors(small)

    hidden, projected, qkv = qkv_ahead(x, real, vecs, bias, qkv)
    attended, logsum = [], []
    for first in groups:
        one, two = attend(projected, bias_v, tables, counts, first, 2)
        attended.append(one)
        logsum.append(two)
        projected, attended[-1] = order(projected, one)
    middle, second, active, slope, up, proj = up_ahead(x, attended, vecs, up_add, up_pieces)
    result, down_grad, inner_grad, up_add_grad = down_ahead(
        active, slope, middle, g, vecs, down_pieces
    )
    idle = lambda *values: values if len(values) != 1 else values[0]
    up_sum = qkv_sum = idle
    if torus:
        down_grad = sum_at_once(down_grad).astype(f32)
    mine, other, middle_grad, attended_grad, sums_two = mlp_back(
        second, inner_grad, up, middle, g, attended, proj, vecs, torus
    )
    if torus:
        up_sum = Steps(scatter_sum(mine, other, 5))
    else:
        blocks = jnp.concatenate([mine.reshape(5, 4, -1, width), other.reshape(5, 4, -1, width)], 1)
        blocks = blocks.reshape(5, width, width)
        up_grad, proj_grad = jnp.swapaxes(blocks[:4], 0, 1).reshape(width, -1), blocks[4]
    attended_grad = up_sum(attended_grad)
    attended_grad = up_sum(attended_grad)
    attended_grad = up_sum(attended_grad)
    pieces, table_grads, extra = [], [], []
    for first, sums in zip(groups, logsum):
        one, two, three = attend_back(
            projected, attended_grad, sums, bias_v, tables, tables_back, counts, first
        )
        pieces.append(one)
        table_grads.append(two)
        extra.append(three)
        attended_grad, pieces[-1] = order(attended_grad, one)
    if torus:
        pieces = up_sum(*pieces)
        pieces = up_sum(*pieces)
    small = extra, sums_two, up_add_grad, table_grads
    mine, other, images_grad, sums = qkv_back(
        hidden, pieces, qkv, middle_grad, x, real, vecs, swapped, small, torus
    )
    if torus:
        qkv_sum = Steps(scatter_sum(mine, other, 3, sums))
        images_grad = qkv_sum(images_grad)
        images_grad = up_sum(images_grad)
        up_grad, proj_grad = up_sum.arrays
        images_grad = qkv_sum(images_grad)
        images_grad = qkv_sum(images_grad)
        sent = move.send_back(move.pack_back(result, images_grad))
        sent = qkv_sum(sent)
        sent = qkv_sum(sent)
        out, images_grad = move.receive_back(result, images_grad, arrived=sent)
        out, down_grad = qkv_sum(out, down_grad)
        qkv_grad, sums = qkv_sum.arrays
    else:
        blocks = jnp.concatenate(
            [mine.reshape(3, 4, -1, width), other[:12].reshape(3, 4, -1, width)], 1
        ).reshape(3, width, width)
        qkv_grad = jnp.swapaxes(blocks, 0, 1).reshape(width, -1)
        sent = move.send_back(move.pack_back(result, images_grad))
        out, images_grad = move.receive_back(result, images_grad, arrived=sent)
        sums = lax.psum(sums, AXES)
        qkv_grad, proj_grad, up_grad, down_grad = [
            sum_at_once(g.astype(f32)) for g in (qkv_grad, proj_grad, up_grad, down_grad)
        ]
    mine, full = split_sums(sums)
    return (
        out.reshape(images.shape),
        images_grad.reshape(images.shape),
        qkv_grad,
        mine[0],
        proj_grad,
        mine[1],
        mine[2],
        mine[3],
        mine[4],
        mine[5],
        up_grad,
        mine[6],
        down_grad,
        mine[7],
        full[0],
        full[1],
    )


PLANS = {}


def plan_for(rows, cols, images):
    key = (rows, cols, images)
    if key not in PLANS:
        PLANS[key] = Plan(*key)
    return PLANS[key]


def solution(mesh):
    tokens = P(None, "dp", "row", "col", None)
    rows = P(AXES, None)
    vector = P(AXES)
    placed = (
        tokens, rows, vector, rows, vector, vector, vector, vector, vector,
        rows, vector, rows, vector, P(), P(), tokens,
    )
    given = (tokens, tokens, rows, vector, rows, vector, vector, vector, vector, vector,
             rows, vector, rows, vector, P(), P())
    return jax.shard_map(body, mesh=mesh, in_specs=placed, out_specs=given, check_vma=False)
```

```python
import math

import jax
import jax.numpy as jnp
import numpy as np
from jax import lax
from jax.experimental import pallas as pl
from jax.experimental.pallas import tpu as pltpu
from jax.sharding import PartitionSpec as P

HEAD = 64
WIN = 14
GRID = 64
NWIN = 5
PITCH = 16
KEYS = WIN * PITCH
LANES = 128
ROWFIELD, COLFIELD, LOWFIELD, MASKLANE = 0, 14, 28, 56
COLTABLE = 32
NEG = -1e30
GROUP = 4
COST = 1024
EDGE = GRID - WIN * (NWIN - 1)
epsilon = 1e-06
bf16 = jnp.bfloat16
f32 = jnp.float32


def cost(flops):
    return pl.CostEstimate(flops=COST, bytes_accessed=1024, transcendentals=0)


def dot_nn(a, b):
    return lax.dot_general(a, b, (((1,), (0,)), ((), ())), preferred_element_type=f32)


def dot_nt(a, b):
    return lax.dot_general(a, b, (((1,), (1,)), ((), ())), preferred_element_type=f32)


def dot_tn(a, b):
    return lax.dot_general(a, b, (((0,), (0,)), ((), ())), preferred_element_type=f32)


def key_fields(reverse):
    shape = (KEYS, LANES)
    t = lax.broadcasted_iota(jnp.int32, shape, 0)
    a, b = t // PITCH, t % PITCH
    lane = lax.broadcasted_iota(jnp.int32, shape, 1) % HEAD
    if reverse:
        one = (lane == ROWFIELD + WIN - 1 - a) | (lane == COLFIELD + WIN - 1 - b)
        return jnp.where(one & (b < WIN), 1.0, 0.0).astype(bf16)
    one = (lane == ROWFIELD + a) | (lane == LOWFIELD + ROWFIELD + a)
    one = one | (lane == COLFIELD + b) | (lane == LOWFIELD + COLFIELD + b)
    out = jnp.where(one & (b < WIN), 1.0, 0.0)
    return jnp.where((lane == MASKLANE) & (b >= WIN), NEG, out).astype(bf16)


def tables_kernel(swapped_ref, rows_ref, cols_ref, ahead_ref, back_ref):
    shape = (2 * WIN - 1, HEAD)
    index = lax.broadcasted_iota(jnp.int32, shape, 0)
    lane = lax.broadcasted_iota(jnp.int32, shape, 1)
    empty = jnp.zeros((HEAD, HEAD), f32)
    for ref, place in ((ahead_ref, 2 * WIN - 2 - index), (back_ref, index)):
        spots = [jnp.where(lane == place + start, 1.0, 0.0).astype(bf16) for start in (0, COLTABLE)]
        both = []
        for one, two in ((rows_ref, cols_ref), (cols_ref, rows_ref)):
            half = dot_tn(one[...], spots[0]) + dot_tn(two[...], spots[1])
            full = [jnp.concatenate(pair, 1) for pair in ((empty, half), (half, empty))]
            both.append(jnp.concatenate(full, 0).astype(bf16))
        for s in range(ref.shape[0]):

            @pl.when(swapped_ref[s] == 0)
            def _():
                ref[s] = both[0]

            @pl.when(swapped_ref[s] != 0)
            def _():
                ref[s] = both[1]


def position_tables(swapped, rel_rows, rel_cols):
    one = jax.ShapeDtypeStruct((swapped.shape[0], LANES, LANES), bf16)
    return pl.pallas_call(
        tables_kernel,
        grid_spec=pltpu.PrefetchScalarGridSpec(
            num_scalar_prefetch=1,
            grid=(1,),
            in_specs=[pl.BlockSpec(rel_rows.shape, lambda s, w: (0, 0))] * 2,
            out_specs=[pl.BlockSpec(one.shape, lambda s, w: (0, 0, 0))] * 2,
        ),
        out_shape=[one, one],
        cost_estimate=cost(0),
        name="position_tables",
    )(swapped, rel_rows, rel_cols)


def lane_in(shape, start, count):
    lane = lax.broadcasted_iota(jnp.int32, shape, 1) % HEAD
    return (lane >= start) & (lane < start + count)


def query_fields(q2, table):
    turned = dot_nn(q2, table)
    parts = []
    shape = (PITCH, LANES)
    in_rows = lane_in(shape, ROWFIELD, WIN)
    in_cols = lane_in(shape, COLFIELD, WIN)
    for a in range(q2.shape[0] // PITCH):
        t = turned[PITCH * a : PITCH * (a + 1)]
        r = pltpu.roll(t, (a - WIN + 1) % LANES, 1)
        c = pltpu.roll(t, LANES - (COLTABLE + 2 * WIN - 2 - (WIN - 1) - COLFIELD), 1, stride=1, stride_axis=0)
        parts.append(jnp.where(in_rows, r, jnp.where(in_cols, c, 0.0)))
    full = jnp.concatenate(parts, 0)
    high = full.astype(bf16).astype(f32)
    low = pltpu.roll(full - high, LOWFIELD, 1)
    one = jnp.where(lane_in(full.shape, MASKLANE, 1), 1.0, 0.0)
    return (high + low + one).astype(bf16)


def field_tables(fields):
    parts = []
    shape = (PITCH, LANES)
    in_rows = lane_in(shape, ROWFIELD, WIN)
    in_cols = lane_in(shape, COLFIELD, WIN)
    for a in range(fields.shape[0] // PITCH):
        t = fields[PITCH * a : PITCH * (a + 1)]
        r = jnp.where(in_rows, t, 0.0)
        c = jnp.where(in_cols, t, 0.0)
        r = pltpu.roll(r, a, 1) if a else r
        c = pltpu.roll(c, COLTABLE - COLFIELD, 1, stride=1, stride_axis=0)
        parts.append(r + c)
    return jnp.concatenate(parts, 0)


def first_half(shape, axis):
    return lax.broadcasted_iota(jnp.int32, shape, axis) < HEAD


def padded_rows(block, fill):
    if block.shape[0] == KEYS:
        return block
    rest = (KEYS - block.shape[0], LANES)
    return jnp.concatenate([block, jnp.broadcast_to(fill, rest).astype(block.dtype)], 0)


def pick(mask, head, one, two):
    return jnp.where(mask, one, two) if head == 0 else jnp.where(mask, two, one)


def slot_groups(slots):
    order = list(range(len(slots)))
    return [order[k : k + GROUP] for k in range(0, len(order), GROUP)]


def attend_kernel(slots, q_ref, k_ref, v_ref, vb_ref, tab_ref, att_ref, lse_ref):
    kf = key_fields(False)
    leftk = first_half((KEYS, LANES), 1)
    one = jnp.ones((KEYS, LANES), bf16)
    for group in slot_groups(slots):
        work = []
        for s in group:
            row, count, lane0 = slots[s]
            rows = pl.ds(row, count)
            q2 = q_ref[rows, :]
            k2 = padded_rows(k_ref[rows, :] * bf16(HEAD ** -0.5), jnp.zeros((1, LANES), bf16))
            v2 = padded_rows(v_ref[rows, :], vb_ref[0:1, :])
            x2 = query_fields(q2, tab_ref[s])
            left = first_half((count, LANES), 1)
            for e in range(2):
                work.append((s, e, pick(left, e, q2, x2), pick(leftk, e, k2, kf), pick(leftk, e, v2, one)))
        st = [dot_nt(ka, qa) for _, _, qa, ka, _ in work]
        peak = [jnp.max(v, axis=0, keepdims=True) for v in st]
        pt = [jnp.exp(v - p).astype(bf16) for v, p in zip(st, peak)]
        ot = [dot_tn(w[4], p) for w, p in zip(work, pt)]
        outs = []
        for (s, e, *_), p, o in zip(work, peak, ot):
            _, count, lane0 = slots[s]
            mass = o[HEAD : HEAD + 1] if e == 0 else o[0:1]
            lse_ref[0, e : e + 1, lane0 : lane0 + count] = p + jnp.log(mass)
            outs.append(o * (1.0 / mass))
        for k, s in enumerate(group):
            row, count, _ = slots[s]
            both = jnp.where(first_half((LANES, count), 0), outs[2 * k], outs[2 * k + 1])
            att_ref[pl.ds(row, count), :] = both.T.astype(bf16)


def attend_back_kernel(
    slots, q_ref, k_ref, v_ref, do_ref, lse_ref, vb_ref, tab_ref, tabb_ref,
    dqkv_ref, dtab_ref, dvb_ref,
):
    kf = key_fields(False)
    kb = key_fields(True)
    extra = jnp.zeros((1, LANES), f32)

    @pl.when(pl.program_id(0) == 0)
    def _():
        dtab_ref[...] = jnp.zeros_like(dtab_ref)

    leftk = first_half((KEYS, LANES), 1)
    zero = jnp.zeros((KEYS, LANES), bf16)
    for group in slot_groups(slots):
        work = []
        for s in group:
            row, count, lane0 = slots[s]
            rows = pl.ds(row, count)
            q2 = q_ref[rows, :]
            do2 = do_ref[rows, :]
            k2 = padded_rows(k_ref[rows, :] * bf16(HEAD ** -0.5), jnp.zeros((1, LANES), bf16))
            v2 = padded_rows(v_ref[rows, :], vb_ref[0:1, :])
            x2 = query_fields(q2, tab_ref[s])
            left = first_half((count, LANES), 1)
            for e in range(2):
                work.append((s, e, pick(left, e, q2, x2), k2, v2, do2))
        st = [dot_nt(pick(leftk, e, k2, kf), qa) for _, e, qa, k2, _, _ in work]
        dpt = [dot_nt(pick(leftk, e, v2, zero), do2) for _, e, _, _, v2, do2 in work]
        pt = []
        for (s, e, *_), v in zip(work, st):
            _, count, lane0 = slots[s]
            pt.append(jnp.exp(v - lse_ref[0, e : e + 1, lane0 : lane0 + count]))
        mean = [jnp.sum(p * d, axis=0, keepdims=True) for p, d in zip(pt, dpt)]
        dst = [(p * (d - m)).astype(bf16) for p, d, m in zip(pt, dpt, mean)]
        dv = [dot_nn(p.astype(bf16), w[5]) for p, w in zip(pt, work)]
        dk = [dot_nn(d, w[2]) for d, w in zip(dst, work)]
        dq = [dot_tn(d, pick(leftk, w[1], w[3], kb)) for d, w in zip(dst, work)]
        for k, s in enumerate(group):
            row, count, _ = slots[s]
            rows = pl.ds(row, count)
            left = first_half((count, LANES), 1)
            one, two = 2 * k, 2 * k + 1
            dt = field_tables(jnp.where(left, dq[two], dq[one]))
            high = dt.astype(bf16)
            low = (dt - high.astype(f32)).astype(bf16)
            tabb = tabb_ref[s]
            dq2 = jnp.where(left, dq[one], dq[two]) + dot_nt(high, tabb) + dot_nt(low, tabb)
            dk2 = jnp.where(leftk, dk[one], dk[two]) * (HEAD ** -0.5)
            dv2 = jnp.where(leftk, dv[one], dv[two])
            dqkv_ref[0, rows, :] = dq2.astype(bf16)
            dqkv_ref[1, rows, :] = dk2[:count].astype(bf16)
            dqkv_ref[2, rows, :] = dv2[:count].astype(bf16)
            if count < KEYS:
                extra = extra + jnp.sum(dv2[count:], axis=0, keepdims=True)
            q2 = q_ref[rows, :]
            dtab_ref[s] += dot_tn(q2, high) + dot_tn(q2, low)
    dvb_ref[0] = jnp.broadcast_to(extra, (8, LANES))


def slot_places(counts):
    places, row, lane = [], 0, 0
    for count in counts:
        places.append((row, count, lane))
        row += count
        lane += -(-count // LANES) * LANES
    return tuple(places), row, lane


def attend(projected, bias_v, tables, counts, first, count):
    slots, rows, lanes = slot_places(counts)
    width = projected.shape[1] // 3
    pairs = width // LANES
    col = lambda off: pl.BlockSpec((rows, LANES), lambda p: (0, off * pairs + first + p))
    return pl.pallas_call(
        lambda *refs: attend_kernel(slots, *refs),
        grid=(count,),
        in_specs=[
            col(0), col(1), col(2),
            pl.BlockSpec((8, LANES), lambda p: (0, first + p)),
            pl.BlockSpec((len(counts), LANES, LANES), lambda p: (0, 0, 0)),
        ],
        out_specs=[
            pl.BlockSpec((rows, LANES), lambda p: (0, p)),
            pl.BlockSpec((1, 8, lanes), lambda p: (p, 0, 0)),
        ],
        out_shape=[
            jax.ShapeDtypeStruct((rows, count * LANES), bf16),
            jax.ShapeDtypeStruct((count, 8, lanes), f32),
        ],
        compiler_params=pltpu.CompilerParams(vmem_limit_bytes=48 << 20),
        cost_estimate=pl.CostEstimate(flops=COST, bytes_accessed=1024, transcendentals=0),
        name="attend",
    )(projected, projected, projected, bias_v, tables)


def attend_back(projected, upstream, lse, bias_v, tables, tables_back, counts, first):
    count = lse.shape[0]
    slots, rows, lanes = slot_places(counts)
    width = projected.shape[1] // 3
    pairs = width // LANES
    col = lambda off: pl.BlockSpec((rows, LANES), lambda p: (0, off * pairs + first + p))
    n = len(counts)
    return pl.pallas_call(
        lambda *refs: attend_back_kernel(slots, *refs),
        grid=(count,),
        in_specs=[
            col(0), col(1), col(2), col(0),
            pl.BlockSpec((1, 8, lanes), lambda p: (p, 0, 0)),
            pl.BlockSpec((8, LANES), lambda p: (0, first + p)),
            pl.BlockSpec((n, LANES, LANES), lambda p: (0, 0, 0)),
            pl.BlockSpec((n, LANES, LANES), lambda p: (0, 0, 0)),
        ],
        out_specs=[
            pl.BlockSpec((3, rows, LANES), lambda p: (0, 0, p)),
            pl.BlockSpec((n, LANES, LANES), lambda p: (0, 0, 0)),
            pl.BlockSpec((1, 8, LANES), lambda p: (p, 0, 0)),
        ],
        out_shape=[
            jax.ShapeDtypeStruct((3, rows, count * LANES), bf16),
            jax.ShapeDtypeStruct((n, LANES, LANES), f32),
            jax.ShapeDtypeStruct((count, 8, LANES), f32),
        ],
        compiler_params=pltpu.CompilerParams(vmem_limit_bytes=48 << 20),
        cost_estimate=pl.CostEstimate(flops=COST, bytes_accessed=1024, transcendentals=0),
        name="attend_back",
    )(projected, projected, projected, upstream, lse, bias_v, tables, tables_back)


def sides(index):
    return WIN * index, min(WIN * index + WIN, GRID)


class Plan:
    def __init__(self, rows, cols, images):
        self.rows, self.cols, self.images = rows, cols, images
        self.devices = rows * cols
        self.tile_rows, self.tile_cols = GRID // rows, GRID // cols
        self.tokens = images * self.tile_rows * self.tile_cols
        kinds = ([], [], [])
        for n in range(images):
            for i in range(NWIN):
                for j in range(NWIN):
                    kinds[(i == NWIN - 1) + (j == NWIN - 1)].append((n, i, j))
        self.caps = tuple(-(-len(kind) // self.devices) for kind in kinds)
        self.parts = {w: self._sources(w) for kind in kinds for w in kind}
        owner = self._assign(kinds)
        self.counts = (KEYS,) * self.caps[0] + (EDGE * PITCH,) * (self.caps[1] + self.caps[2])
        _, self.window_rows, _ = slot_places(self.counts)
        self._tables(kinds, owner)

    def _distance(self, one, two):
        r, c = divmod(one, self.cols)
        q, e = divmod(two, self.cols)
        return abs(c - e) + abs(r // 2 - q // 2) + (0.125 if r % 2 != q % 2 else 0.0)

    def _sources(self, window):
        _, i, j = window
        (r0, r1), (c0, c1) = sides(i), sides(j)
        tr, tc = self.tile_rows, self.tile_cols
        found = {}
        for r in range(r0 // tr, (r1 - 1) // tr + 1):
            for c in range(c0 // tc, (c1 - 1) // tc + 1):
                high = min(r1, (r + 1) * tr) - max(r0, r * tr)
                wide = min(c1, (c + 1) * tc) - max(c0, c * tc)
                found[r * self.cols + c] = high * wide
        return found

    def _rounds(self, owner):
        pairs = {}
        for window, dev in owner.items():
            for source, amount in self.parts[window].items():
                if source != dev:
                    pairs[source, dev] = pairs.get((source, dev), 0) + amount
        rounds = []
        for pair, amount in sorted(pairs.items(), key=lambda p: (-p[1], p[0])):
            for senders, takers, members in rounds:
                if pair[0] not in senders and pair[1] not in takers:
                    break
            else:
                senders, takers, members = set(), set(), []
                rounds.append((senders, takers, members))
            senders.add(pair[0])
            takers.add(pair[1])
            members.append(pair)
        return pairs, [members for _, _, members in rounds]

    def _cost(self, owner):
        pairs, rounds = self._rounds(owner)
        moved = sum(amount * self._distance(*pair) for pair, amount in pairs.items())
        return moved / 4 + sum(64 + max(pairs[p] for p in members) for members in rounds)

    def _assign(self, kinds):
        owner = {}
        room = {}
        for kind, windows in enumerate(kinds):
            room[kind] = [self.caps[kind]] * self.devices
            for window in sorted(windows, key=lambda w: (-(w[1] + w[2]), w)):
                far = lambda d: sum(t * self._distance(s, d) for s, t in self.parts[window].items())
                dev = min((d for d in range(self.devices) if room[kind][d]), key=lambda d: (far(d), d))
                owner[window] = dev
                room[kind][dev] -= 1
        best = self._cost(owner)
        for _ in range(4):
            before = best
            for kind in (1, 2, 0):
                for one in kinds[kind]:
                    for dev in range(self.devices):
                        if dev == owner[one]:
                            continue
                        trials = []
                        if room[kind][dev]:
                            trials.append({**owner, one: dev})
                        for two in kinds[kind]:
                            if owner[two] == dev:
                                trials.append({**owner, one: dev, two: owner[one]})
                        for trial in trials:
                            price = self._cost(trial)
                            if price < best - 1e-9:
                                if sum(trial[w] != owner[w] for w in kinds[kind]) == 1:
                                    room[kind][owner[one]] += 1
                                    room[kind][dev] -= 1
                                owner, best = trial, price
                                break
            if best >= before:
                break
        return owner

    def _tables(self, kinds, owner):
        places, _, _ = slot_places(self.counts)
        starts = (0, self.caps[0], self.caps[0] + self.caps[1])
        self.swapped = np.zeros((self.devices, len(self.counts)), np.int32)
        taken = {}
        moves = {}
        for kind, windows in enumerate(kinds):
            for window in windows:
                n, i, j = window
                dev = owner[window]
                slot = starts[kind] + taken.get((dev, kind), 0)
                taken[dev, kind] = taken.get((dev, kind), 0) + 1
                swap = kind == 1 and j == NWIN - 1
                self.swapped[dev, slot] = swap
                (r0, r1), (c0, c1) = sides(i), sides(j)
                for r in range(r0, r1):
                    for c in range(c0, c1):
                        a, b = (c - c0, r - r0) if swap else (r - r0, c - c0)
                        row = places[slot][0] + PITCH * a + b
                        source = (r // self.tile_rows) * self.cols + c // self.tile_cols
                        token = (n * self.tile_rows + r % self.tile_rows) * self.tile_cols
                        token += c % self.tile_cols
                        moves.setdefault((source, dev), []).append((token, row))
        _, rounds = self._rounds(owner)
        self.perms = rounds
        self.sizes = [-(-max(len(moves[p]) for p in members) // PITCH) * PITCH for members in rounds]
        total = sum(self.sizes)
        self.pack = np.full((self.devices, total), -1, np.int32)
        self.take = np.full((self.devices, self.window_rows), -1, np.int32)
        self.pack_back = np.full((self.devices, total), -1, np.int32)
        self.take_back = np.full((self.devices, self.tokens), -1, np.int32)
        for dev in range(self.devices):
            for token, row in moves.get((dev, dev), ()):
                self.take[dev, row] = token
                self.take_back[dev, token] = row
        at = 0
        for members, size in zip(rounds, self.sizes):
            for source, dev in members:
                for k, (token, row) in enumerate(moves[source, dev]):
                    self.pack[source, at + k] = token
                    self.take[dev, row] = self.tokens + at + k
                    self.pack_back[dev, at + k] = row
                    self.take_back[source, token] = self.window_rows + at + k
            at += size


def chosen(index, start, count):
    spot = lax.broadcasted_iota(jnp.int32, (count, index.shape[1]), 0) + start
    return jnp.where(spot == index, 1.0, 0.0).astype(bf16)


def pack_kernel(sizes, index_ref, *refs):
    token_refs, out_refs = refs[: len(refs) - len(sizes)], refs[len(refs) - len(sizes) :]
    at = 0
    for size, out_ref in zip(sizes, out_refs):
        hot = chosen(index_ref[0:1, at : at + size], 0, token_refs[0].shape[0])
        for k, ref in enumerate(token_refs):
            width = ref.shape[1]
            moved = dot_tn(hot, ref[...].astype(bf16)).astype(bf16)
            out_ref[:, width * k : width * (k + 1)] = moved
        at += size


def pack(index, tokens, sizes):
    width = sum(t.shape[1] for t in tokens)
    return pl.pallas_call(
        lambda *refs: pack_kernel(sizes, *refs),
        out_shape=[jax.ShapeDtypeStruct((size, width), bf16) for size in sizes],
        compiler_params=pltpu.CompilerParams(vmem_limit_bytes=40 << 20),
        cost_estimate=cost(0),
        name="pack",
    )(index[None], *tokens)


def take_kernel(count, masked, index_ref, *refs):
    local_refs, arrived, out_refs = refs[:count], refs[count : -count - masked], refs[-count - masked :]
    index = index_ref[...]
    at = local_refs[0].shape[0]
    hot = chosen(index, 0, at)
    totals = []
    for ref in local_refs:
        local = ref[...]
        total = dot_tn(hot, local.astype(bf16))
        if local.dtype == f32:
            total = total + dot_tn(hot, (local - local.astype(bf16).astype(f32)).astype(bf16))
        totals.append(total)
    for ref in arrived:
        hot = chosen(index, at, ref.shape[0])
        width = ref.shape[1] // count
        totals = [
            t + dot_tn(hot, ref[:, width * k : width * (k + 1)]) for k, t in enumerate(totals)
        ]
        at += ref.shape[0]
    for ref, total in zip(out_refs, totals):
        ref[...] = total.astype(ref.dtype)
    if masked:
        row = jnp.where(index >= 0, 1.0, 0.0)
        out_refs[-1][...] = jnp.broadcast_to(row, (LANES, row.shape[1])).T


def take(index, locals_, arrived, masked=False):
    shapes = [((index.shape[0], local.shape[1]), local.dtype) for local in locals_]
    if masked:
        shapes.append(((index.shape[0], LANES), f32))
    return pl.pallas_call(
        lambda *refs: take_kernel(len(locals_), int(masked), *refs),
        out_shape=[jax.ShapeDtypeStruct(*shape) for shape in shapes],
        compiler_params=pltpu.CompilerParams(vmem_limit_bytes=40 << 20),
        cost_estimate=cost(0),
        name="take",
    )(index[None], *locals_, *arrived)


class Mover:
    def __init__(self, plan):
        self.plan = plan
        here = lax.axis_index("row") * plan.cols + lax.axis_index("col")
        mine = lambda table: lax.dynamic_index_in_dim(jnp.asarray(table), here, 0, keepdims=False)
        self.index = {name: mine(getattr(plan, name)) for name in ("pack", "take", "pack_back", "take_back")}
        self.swapped = mine(plan.swapped)

    def pack(self, *tokens):
        return pack(self.index["pack"], tokens, self.plan.sizes)

    def send(self, packed):
        return [lax.ppermute(s, ("row", "col"), perm) for s, perm in zip(packed, self.plan.perms)]

    def receive(self, *tokens, arrived, masked=False):
        return take(self.index["take"], tokens, arrived, masked)

    def pack_back(self, *rows):
        return pack(self.index["pack_back"], rows, self.plan.sizes)

    def send_back(self, packed):
        back = [[(two, one) for one, two in perm] for perm in self.plan.perms]
        return [lax.ppermute(s, ("row", "col"), perm) for s, perm in zip(packed, back)]

    def receive_back(self, *rows, arrived):
        return take(self.index["take_back"], rows, arrived)


AXES = ("dp", "row", "col")
TORUS = (2, 4, 4)


def order(*values):
    return lax.optimization_barrier(values)


def over_dp(v):
    return lax.ppermute(v, "dp", [(0, 1), (1, 0)])


def over_y(v):
    return lax.ppermute(v, "row", [(r, (r + 2) % 4) for r in range(4)])


def over_both(v):
    return lax.ppermute(v, ("dp", "row"), [(k, (k // 4 + 1) % 2 * 4 + (k % 4 + 2) % 4) for k in range(8)])


def over_core(v):
    return lax.ppermute(v, "row", [(r, r ^ 1) for r in range(4)])


def over_col(v, steps):
    return lax.ppermute(v, "col", [(c, (c + steps) % 4) for c in range(4)])


def block_at(flip_dp, flip_y, flip_core):
    dp, row = lax.axis_index("dp"), lax.axis_index("row")
    return (
        ((dp + flip_dp) % 2) * 4 + ((row // 2 + flip_y) % 2) * 2 + (row % 2 + flip_core) % 2
    )


KINDS = ((0, 0), (1, 0), (0, 1), (1, 1))


def column_kernel(store, *refs):
    seen, out_ref = refs[:4], refs[4]
    place = lax.axis_index("col")
    for j in range(4):
        for k in range(4):

            @pl.when((place - j) % 4 == k)
            def _():
                store(out_ref, j, seen[k])


def in_column(shard, store, shape):
    seen = [shard] + [over_col(shard, k) for k in (1, 2, 3)]
    return pl.pallas_call(
        lambda *refs: column_kernel(store, *refs),
        out_shape=jax.ShapeDtypeStruct(shape, bf16),
        cost_estimate=cost(0),
        name="in_column",
    )(*seen)


SMALL = 8


def shards_kernel(qkv_ref, up_ref, down_ref, proj_ref, *refs):
    first_ref, planes_ref = refs[-2:]
    rows, width = proj_ref.shape
    for k in range(3):
        first_ref[rows * k : rows * (k + 1), :] = qkv_ref[:, width * k : width * (k + 1)]
    first_ref[3 * rows :, :] = jnp.zeros((SMALL, width), bf16)
    for k, ref in enumerate(refs[:-2]):
        first_ref[3 * rows + k : 3 * rows + k + 1, 0 : ref.shape[1]] = ref[...]
    for k in range(4):
        planes_ref[0, k] = up_ref[:, width * k : width * (k + 1)]
        planes_ref[0, 4 + k] = down_ref[rows * k : rows * (k + 1), :]
    planes_ref[0, 8] = proj_ref[...]


def sent_shards(qkv_weight, up_weight, down_weight, proj_weight, small):
    rows, width = proj_weight.shape
    return pl.pallas_call(
        shards_kernel,
        out_shape=[
            jax.ShapeDtypeStruct((3 * rows + SMALL, width), bf16),
            jax.ShapeDtypeStruct((1, 9, rows, width), bf16),
        ],
        cost_estimate=cost(0),
        name="sent_shards",
    )(qkv_weight, up_weight, down_weight, proj_weight, *[v[None] for v in small])


def first_weights(shard):
    rows, width = (shard.shape[0] - SMALL) // 3, shard.shape[1]
    (shard,) = yield (shard,)

    def store(ref, j, shard):
        for plane in range(3):
            at = rows * (4 * plane + j)
            ref[at : at + rows, :] = shard[rows * plane : rows * (plane + 1), :]
        at = 12 * rows + SMALL * j
        ref[at : at + SMALL, :] = shard[3 * rows :, :]

    own = in_column(shard, store, (12 * rows + 4 * SMALL, width))
    (own,) = yield (own,)
    pieces = [own, over_dp(own), over_y(own), over_both(own)]
    pieces = yield pieces
    pieces = [*pieces, *[over_core(p) for p in pieces]]
    yield pieces


PAIR = 48


def put_rows(ref, at, value):
    high = value.astype(bf16)
    count = value.shape[0]
    ref[at : at + count, :] = high
    ref[at + count : at + 2 * count, :] = (value - high.astype(f32)).astype(bf16)


def both_rows(ref, at):
    half = PAIR // 2
    return ref[at : at + half, :].astype(f32) + ref[at + half : at + 2 * half, :].astype(f32)


def core_kernel(planes, small, mine_ref, came_ref, *refs):
    own_ref, sent_refs = refs[2 * small], refs[2 * small + 1 : 2 * small + 4]
    rows = mine_ref.shape[1]
    for plane in range(planes):
        at = rows * plane
        for k in range(4):
            total = mine_ref[4 * plane + k].astype(f32) + came_ref[4 * plane + k].astype(f32)
            if k:
                sent_refs[k - 1][at : at + rows, :] = total.astype(bf16)
            else:
                own_ref[at : at + rows, :] = total
    if small:
        total = refs[0][...] + refs[1][...]
        refs[-1][...] = total
        for ref in sent_refs:
            put_rows(ref, rows * planes, total)


def chips_kernel(planes, small, own_ref, dp_ref, y_ref, both_ref, *refs):
    mine_ref, sent_refs, column = refs[small], refs[small + 1 : small + 4], refs[-1]
    count = own_ref.shape[0] // planes // 4
    total = own_ref[...]
    for ref in (dp_ref, y_ref, both_ref):
        total = total + ref[: own_ref.shape[0], :].astype(f32)
    column[...] = total
    place = lax.axis_index("col")
    for k in range(4):
        for plane in range(planes):
            at = pl.multiple_of(4 * count * plane + (place + k) % 4 * count, count)
            rows = column[pl.ds(at, count), :]
            if k:
                sent_refs[k - 1][count * plane : count * (plane + 1), :] = rows.astype(bf16)
            else:
                mine_ref[plane] = rows
    if small:
        total = refs[0][...]
        for ref in (dp_ref, y_ref, both_ref):
            total = total + both_rows(ref, own_ref.shape[0])
        refs[-2][...] = total
        for ref in sent_refs:
            put_rows(ref, count * planes, total)


def column_sum_kernel(planes, small, mine_ref, *refs):
    came = refs[:3]
    out_refs = refs[3 + small :]
    count, width = mine_ref.shape[1:]
    for plane in range(planes):
        total = mine_ref[plane]
        for ref in came:
            total = total + ref[count * plane : count * (plane + 1), :].astype(f32)
        wide = out_refs[0].shape[1] // width
        if plane < wide:
            out_refs[0][:, width * plane : width * (plane + 1)] = total
        else:
            out_refs[1][...] = total
    if small:
        total = refs[3][...]
        for ref in came:
            total = total + both_rows(ref, count * planes)
        out_refs[-1][...] = total


def scatter_sum(mine, other, planes, whole=False):
    rows, width = mine.shape[1:]
    params = pltpu.CompilerParams(vmem_limit_bytes=40 << 20)
    shape = lambda kind, *dims: jax.ShapeDtypeStruct(dims, kind)
    (other,) = yield (other,)
    came = over_core(other)
    came, *given = yield (came,)
    small = len(given) // 2
    extra = PAIR * small
    sums = [shape(f32, PAIR // 2, width)] * small
    own, *rest = pl.pallas_call(
        lambda *refs: core_kernel(planes, small, *refs),
        out_shape=[shape(f32, planes * rows, width)]
        + [shape(bf16, planes * rows + extra, width)] * 3
        + sums,
        compiler_params=params,
        cost_estimate=cost(0),
        name="core_sum",
    )(mine, came, *given)
    own, *rest = yield (own, *rest)
    given = rest[3:]
    units = 1 if whole else planes
    count = planes * rows // units // 4
    came = yield (over_dp(rest[0]), over_y(rest[1]), over_both(rest[2]))
    mine, *rest = pl.pallas_call(
        lambda *refs: chips_kernel(units, small, *refs),
        out_shape=[shape(f32, units, count, width)]
        + [shape(bf16, units * count + extra, width)] * 3
        + sums,
        scratch_shapes=[pltpu.VMEM((planes * rows, width), f32)],
        compiler_params=params,
        cost_estimate=cost(0),
        name="chips_sum",
    )(own, *came, *given)
    mine, *rest = yield (mine, *rest)
    given = rest[3:]
    came = yield [over_col(v, k) for k, v in zip((1, 2, 3), rest)]
    wide = min(units, 4)
    yield pl.pallas_call(
        lambda *refs: column_sum_kernel(units, small, *refs),
        out_shape=[shape(f32, count, wide * width)]
        + [shape(f32, count, width)] * (units - wide)
        + sums,
        compiler_params=params,
        cost_estimate=cost(0),
        name="column_sum",
    )(mine, *came, *given)


def column_pair(v, steps):
    return lax.ppermute(v, "col", [(k, k ^ steps) for k in range(4)])


def half_kernel(bit, arrays, *refs):
    given, (mine_ref, sent_ref, kept) = refs[:arrays], refs[arrays:]
    total = given[0][...]
    for ref in given[1:]:
        total = total + ref[...].astype(f32)
    kept[...] = total
    place = lax.axis_index("col")
    half = place // 2 if bit == 2 else place % 2
    size = kept.shape[0] // 2
    mine_ref[...] = kept[pl.ds(pl.multiple_of(half * size, 8), size), :]
    sent_ref[...] = kept[pl.ds(pl.multiple_of((1 - half) * size, 8), size), :].astype(bf16)


def last_kernel(mine_ref, came_ref, out_ref):
    out_ref[...] = mine_ref[...] + came_ref[...].astype(f32)


def halves_sum(mine, other):
    shard, width = mine.shape[1:]
    rows = 4 * shard
    params = pltpu.CompilerParams(vmem_limit_bytes=40 << 20)
    shape = lambda kind, *dims: jax.ShapeDtypeStruct(dims, kind)
    (other,) = yield (other,)
    (came,) = yield (over_core(other),)
    sums = pl.pallas_call(
        lambda *refs: core_kernel(4, 0, *refs),
        out_shape=[shape(f32, rows, width)] + [shape(bf16, rows, width)] * 3,
        compiler_params=params,
        cost_estimate=cost(0),
        name="core_sum",
    )(mine, came)
    own, *rest = yield sums
    came = yield (over_dp(rest[0]), over_y(rest[1]), over_both(rest[2]))
    given = (own, *came)
    for bit in (2, 1):
        mine, sent = pl.pallas_call(
            lambda *refs: half_kernel(bit, len(given), *refs),
            out_shape=[shape(f32, rows // 2, width), shape(bf16, rows // 2, width)],
            scratch_shapes=[pltpu.VMEM((rows, width), f32)],
            compiler_params=params,
            cost_estimate=cost(0),
            name="half_sum",
        )(*given)
        rows //= 2
        mine, sent = yield (mine, sent)
        (came,) = yield (column_pair(sent, bit),)
        given = (mine, came)
    yield (
        pl.pallas_call(
            last_kernel,
            out_shape=shape(f32, rows, width),
            cost_estimate=cost(0),
            name="last_sum",
        )(*given),
    )


class Steps:
    def __init__(self, steps):
        self.steps = steps
        self.arrays = tuple(next(steps))

    def __call__(self, *values, more=()):
        values, arrays, more = lax.optimization_barrier((values, self.arrays, tuple(more)))
        self.arrays = tuple(self.steps.send((*arrays, *more)))
        return values if len(values) != 1 else values[0]


def on_torus():
    return tuple(lax.axis_size(a) for a in AXES) == TORUS


def device_number():
    return (lax.axis_index("dp") * lax.axis_size("row") + lax.axis_index("row")) * lax.axis_size(
        "col"
    ) + lax.axis_index("col")


def gather_at_once(*shards):
    return tuple(lax.all_gather(s, AXES, axis=0, tiled=True) for s in shards)


def sum_at_once(grad):
    return lax.psum_scatter(grad, AXES, scatter_dimension=0, tiled=True)


SPREAD = 0.3275911
TAIL_COEFFICIENTS = (0.1850680112838745, 0.18050004541873932, 0.20733030140399933, 0.020621487870812416, 0.46248844265937805, -0.41615772247314453, 0.5027683973312378, -0.14261901378631592)


def normal_parts(u):
    z = jnp.abs(u) * (2.0 ** -0.5)
    t = 1.0 / (1.0 + SPREAD * z)
    bell = jnp.exp(-0.5 * u * u)
    total = jnp.full_like(t, TAIL_COEFFICIENTS[-1])
    for coefficient in TAIL_COEFFICIENTS[-2::-1]:
        total = total * t + coefficient
    tail = 0.5 * total * t * bell
    return jnp.where(u < 0, tail, 1.0 - tail), bell * (2.0 * math.pi) ** -0.5


def normalize(values):
    center = values - jnp.mean(values, axis=-1, keepdims=True)
    inverse = lax.rsqrt(jnp.mean(center * center, axis=-1, keepdims=True) + epsilon)
    return center * inverse, inverse


def norm_back(upstream, normed, inverse, gain):
    scaled = upstream * gain
    inner = jnp.mean(scaled, axis=-1, keepdims=True)
    cross = jnp.mean(scaled * normed, axis=-1, keepdims=True)
    result = inverse * (scaled - inner - normed * cross)
    sums = [jnp.sum(v, axis=0, keepdims=True) for v in (upstream * normed, upstream)]
    return result, sums


def store_blocks(grad, kept, refs, first):
    rows = grad.shape[0] // 8
    if kept is not None:
        kept[...] = grad.astype(bf16)
    for core, ref in enumerate(refs):
        for k, kind in enumerate(KINDS):
            if kept is None:
                at = rows * (4 * core + k)
                ref[first + k] = grad[at : at + rows].astype(bf16)
            else:
                at = pl.multiple_of(block_at(*kind, core) * rows, rows)
                ref[first + k] = kept[pl.ds(at, rows), :]


def stacked_rows(rows):
    spare = jnp.zeros((8 - len(rows), rows[0].shape[1]), f32)
    return jnp.concatenate([*rows, spare], 0)


def spread(count, width):
    return jnp.asarray(np.arange(width)[None] % count == np.arange(LANES)[:, None], bf16)


QV, PROJ_ADD, GAIN_ONE, SHIFT_ONE, GAIN_TWO, SHIFT_TWO, UP_ADD, DOWN_ADD = range(8)
HELD = (48, 24, 24, 24, 24, 24, 96, 24)


def row(ref, k):
    return ref[k : k + 1, :]


def vectors_kernel(*refs):
    pieces, spreads = refs[:8], refs[8:11]
    vecs_ref, up_add_ref, bias_ref, bias_v_ref = refs[11:]
    rows = jnp.concatenate([piece[:, 0:LANES] for piece in pieces], 0)
    whole = []
    for count, spread_ref in zip((24, 48, 96), spreads):
        wide = dot_nn(rows, spread_ref[...])
        total = jnp.zeros((SMALL, wide.shape[1]), f32)
        group = lax.broadcasted_iota(jnp.int32, total.shape, 1) // count
        for k in range(8):
            block = block_at(*KINDS[k % 4], k // 4)
            for col in range(4):
                at = SMALL * (4 * k + col)
                total = total + jnp.where(group == 4 * block + col, wide[at : at + SMALL], 0.0)
        whole.append(total)
    vecs_ref[...] = whole[0]
    up_add_ref[...] = whole[2]
    qv = whole[1][QV : QV + 1]
    width = vecs_ref.shape[1]
    bias_ref[...] = jnp.concatenate([qv[:, :width], jnp.zeros((1, width), f32), qv[:, width:]], 1)
    bias_v_ref[...] = jnp.broadcast_to(qv[:, width:], bias_v_ref.shape).astype(bf16)


def vectors(pieces):
    rows, width = pieces[0].shape
    spreads = [spread(count, 32 * count) for count in (24, 48, 96)]
    tail = pl.BlockSpec((4 * SMALL, width), lambda s: (rows // (4 * SMALL) - 1, 0))
    shapes = [((SMALL, width), f32), ((SMALL, 4 * width), f32), ((1, 3 * width), f32), ((8, width), bf16)]
    return pl.pallas_call(
        vectors_kernel,
        grid=(1,),
        in_specs=[tail] * 8 + [whole_spec(s) for s in spreads],
        out_specs=[pl.BlockSpec(shape, lambda s: (0, 0)) for shape, _ in shapes],
        out_shape=[jax.ShapeDtypeStruct(*shape) for shape in shapes],
        cost_estimate=cost(0),
        name="vectors",
    )(*pieces, *spreads)


def gathered_vectors(small):
    whole = [v.astype(f32) for v in gather_at_once(*small)]
    width = whole[PROJ_ADD].shape[0]
    none = jnp.zeros((width,), f32)
    vecs = jnp.stack([v if v.shape[0] == width else none for v in whole])
    up_add = jnp.broadcast_to(whole[UP_ADD][None], (SMALL, 4 * width))
    query, value = whole[QV][:width], whole[QV][width:]
    bias = jnp.concatenate([query, none, value])[None]
    return vecs, up_add, bias, jnp.broadcast_to(value[None], (8, width)).astype(bf16)


def assemble(target, pieces):
    for k, piece in enumerate(pieces):
        if piece is None:
            continue
        rows = piece.shape[-2]
        at = pl.multiple_of(block_at(*KINDS[k % 4], k // 4) * rows, rows)
        target[pl.ds(at, rows), :] = piece[...].reshape(rows, piece.shape[-1])


def qkv_ahead_kernel(x_ref, real_ref, vecs_ref, bias_ref, *refs):
    weight_refs, (hidden_ref, out_ref, w_ref) = refs[:-3], refs[-3:]

    @pl.when(pl.program_id(0) == 0)
    def _():
        plain, _ = normalize(x_ref[...].astype(f32))
        hidden = plain * row(vecs_ref, GAIN_ONE) + row(vecs_ref, SHIFT_ONE)
        hidden = hidden * real_ref[:, 0:1]
        hidden_ref[...] = hidden.astype(bf16)

    if len(weight_refs) == 1:
        w_ref[...] = weight_refs[0][...]
    else:
        assemble(w_ref, weight_refs)
    out_ref[...] = (dot_nn(hidden_ref[...], w_ref[...]) + bias_ref[...]).astype(bf16)


def join_rows(target, source, planes):
    rows = source.shape[2]
    at = 0
    for device in range(source.shape[0]):
        for plane in range(planes):
            target[at : at + rows, :] = source[device, plane]
            at += rows


def up_kernel(pieced, x_ref, a_ref, g_ref, vecs_ref, up_add_ref, w_ref, p_ref, *refs):
    middle_ref, second_ref, active_ref, slope_ref, proj_ref, mine_ref, other_ref, kept, up_ref = refs
    step = pl.program_id(0)

    @pl.when(step == 0)
    def _():
        if pieced:
            join_rows(proj_ref, p_ref, 1)
        else:
            proj_ref[...] = p_ref[...]
        middle = x_ref[...].astype(f32) + row(vecs_ref, PROJ_ADD)
        middle = middle + dot_nn(a_ref[...], proj_ref[...])
        plain, _ = normalize(middle)
        middle_ref[...] = middle
        second = plain * row(vecs_ref, GAIN_TWO) + row(vecs_ref, SHIFT_TWO)
        second_ref[...] = second.astype(bf16)

    if pieced:
        join_rows(up_ref, w_ref, 1)
    else:
        up_ref[...] = w_ref[...]
    width = up_ref.shape[1]
    chunks = [slice(at, at + width // 3) for at in range(0, width, width // 3)]
    second, g = second_ref[...], g_ref[...]
    add = row(up_add_ref, UP_ADD)
    inner = {0: dot_nn(second, up_ref[:, chunks[0]]) + add[:, chunks[0]]}
    for k, cut in enumerate(chunks):
        if k + 1 < len(chunks):
            inner[k + 1] = dot_nn(second, up_ref[:, chunks[k + 1]]) + add[:, chunks[k + 1]]
        below, density = normal_parts(inner[k])
        active = (inner[k] * below).astype(bf16)
        active_ref[:, cut] = active
        slope_ref[:, cut] = (below + inner[k] * density).astype(slope_ref.dtype)
        kept[cut, :] = dot_tn(active, g).astype(bf16)
    rows = mine_ref.shape[1]
    kind, first = step, 0
    if pieced:
        dp, rank = lax.axis_index("dp"), lax.axis_index("row")
        kind = (step // 2 + dp) % 2 + 2 * ((step + rank // 2) % 2)
        first = rank % 2
    for plane in range(4):
        for away, ref in enumerate((mine_ref, other_ref)):
            at = pl.multiple_of((first + away) % 2 * 4 * rows + rows * plane, rows)
            ref[4 * plane + kind] = kept[pl.ds(at, rows), :]


def mlp_back_kernel(
    pieced, active_ref, slope_ref, middle_ref, g_ref, vecs_ref, down_ref, up_ref, second_ref, a_ref,
    proj_ref, out_ref, mine_ref, other_ref, middle_grad_ref, attended_grad_ref, up_add_grad_ref,
    sums_ref, total, back, kept, turned, *weights,
):
    step = pl.program_id(0)
    last = pl.num_programs(0) - 1

    def store(grad):
        store_blocks(grad, kept if pieced else None, (mine_ref, other_ref), 0)

    @pl.when(step == 0)
    def _():
        total[...] = middle_ref[...] + row(vecs_ref, DOWN_ADD)
        back[...] = jnp.zeros_like(back)
        turned[...] = second_ref[...].T

    @pl.when(step < last)
    def _():
        if pieced:
            join_rows(weights[0], down_ref, 4)
            join_rows(weights[1], up_ref, 1)
            down, up = weights[0][...], weights[1][...]
        else:
            down, up = down_ref[...], up_ref[...]
        inner_grad = dot_nt(g_ref[...], down) * slope_ref[...].astype(f32)
        inner_grad = inner_grad.astype(bf16)
        up_add_grad_ref[...] = jnp.broadcast_to(
            jnp.sum(inner_grad.astype(f32), axis=0, keepdims=True), up_add_grad_ref.shape
        )
        total[...] += dot_nn(active_ref[...], down)
        back[...] += dot_nt(inner_grad, up)
        store(dot_nn(turned[...], inner_grad))

    @pl.when(step == last)
    def _():
        out_ref[...] = total[...].astype(bf16)
        plain, inverse = normalize(middle_ref[...])
        flow = g_ref[...].astype(f32)
        part, sums = norm_back(back[...], plain, inverse, row(vecs_ref, GAIN_TWO))
        middle_grad = flow + part
        middle_grad_ref[...] = middle_grad
        branch = middle_grad.astype(bf16)
        attended_grad_ref[...] = dot_nt(branch, proj_ref[...]).astype(bf16)
        store(dot_tn(a_ref[...], branch))
        column = lambda v: jnp.sum(v, axis=0, keepdims=True)
        sums_ref[...] = stacked_rows([*sums, column(branch.astype(f32)), column(flow)])


def qkv_back_kernel(
    pieced, swapped_ref, hidden_ref, d0_ref, d1_ref, w_ref, middle_grad_ref, x_ref, real_ref,
    vecs_ref, e0_ref, e1_ref, two_ref, up_ref, t0_ref, t1_ref,
    mine_ref, other_ref, images_grad_ref, small_ref, total, columns, kept, turned,
):
    step = pl.program_id(0)

    @pl.when(step == 0)
    def _():
        total[...] = jnp.zeros_like(total)
        turned[...] = hidden_ref[...].T

    back = jnp.concatenate([ref[0] for ref in (d0_ref, d1_ref)], 1)
    total[...] += dot_nt(back, w_ref[...])
    grad = dot_nn(turned[...], back)
    store_blocks(grad, kept if pieced else None, (mine_ref, other_ref), 0)
    columns[step] = jnp.broadcast_to(
        jnp.sum(back.astype(f32), axis=0, keepdims=True), columns.shape[1:]
    )

    @pl.when(step == pl.num_programs(0) - 1)
    def _():
        hidden_grad = total[...].astype(bf16).astype(f32) * real_ref[:, 0:1]
        plain, inverse = normalize(x_ref[...].astype(f32))
        part, sums = norm_back(hidden_grad, plain, inverse, row(vecs_ref, GAIN_ONE))
        images_grad_ref[...] = middle_grad_ref[...] + part
        small_sums(
            swapped_ref, columns, (e0_ref, e1_ref), two_ref, sums, up_ref,
            (t0_ref, t1_ref), small_ref,
        )


def whole_spec(array):
    return pl.BlockSpec(array.shape, lambda s: (0,) * array.ndim)


def across(rows, width):
    return pl.BlockSpec((rows, width), lambda s: (0, s))


BIG = pltpu.CompilerParams(vmem_limit_bytes=56 << 20)


def qkv_ahead(x, real, vecs, bias, weights):
    rows, width = x.shape
    shard = width // 8
    if len(weights) == 1:
        specs = [across(width, width)]
    else:
        specs = [pl.BlockSpec((shard, width), lambda s: (s, 0))] * 8
    return pl.pallas_call(
        qkv_ahead_kernel,
        grid=(3,),
        in_specs=[
            whole_spec(x), whole_spec(real), whole_spec(vecs), across(1, width), *specs,
        ],
        out_specs=[whole_spec(x), across(rows, width), across(width, width)],
        out_shape=[
            jax.ShapeDtypeStruct((rows, width), bf16),
            jax.ShapeDtypeStruct((rows, 3 * width), bf16),
            jax.ShapeDtypeStruct((width, 3 * width), bf16),
        ],
        compiler_params=BIG,
        cost_estimate=cost(5 * 10**9),
        name="qkv_ahead",
    )(x, real, vecs, bias, *weights)


def up_ahead(x, attended, g, vecs, up_add, weights):
    rows, width = x.shape
    pieced = len(weights) == 1
    if pieced:
        (planes,) = weights
        one = (planes.shape[0], 1, *planes.shape[2:])
        specs = [pl.BlockSpec(one, lambda s: (0, s, 0, 0)), pl.BlockSpec(one, lambda s: (0, 8, 0, 0))]
        weights = planes, planes
    else:
        specs = [across(width, width), whole_spec(weights[1])]
    shape = jax.ShapeDtypeStruct
    grad = shape((16, width // 8, width), bf16)
    outs = [
        (whole_spec(x), shape((rows, width), f32)),
        (whole_spec(x), shape((rows, width), bf16)),
        (across(rows, width), shape((rows, 4 * width), bf16)),
        (across(rows, width), shape((rows, 4 * width), bf16)),
        (pl.BlockSpec((width, width), lambda s: (0, 0)), shape((width, width), bf16)),
        (whole_spec(grad), grad),
        (whole_spec(grad), grad),
    ]
    return pl.pallas_call(
        lambda *refs: up_kernel(pieced, *refs),
        grid=(4,),
        in_specs=[
            whole_spec(x), whole_spec(attended), whole_spec(g), whole_spec(vecs), across(8, width),
            *specs,
        ],
        out_specs=[spec for spec, _ in outs],
        out_shape=[out for _, out in outs],
        scratch_shapes=[pltpu.VMEM((width, width), bf16), pltpu.VMEM((width, width), bf16)],
        compiler_params=BIG,
        cost_estimate=cost(0),
        name="up_ahead",
    )(x, attended, g, vecs, up_add, *weights)


def mlp_back(active, slope, middle, g, vecs, weights, second, attended, proj):
    rows, width = second.shape
    shard = width // 8
    shape = jax.ShapeDtypeStruct
    upto = lambda s: jnp.minimum(s, 3)
    along = lambda count: pl.BlockSpec((count, width), lambda s: (0, upto(s)))
    pieced = len(weights) == 1
    scratch = [
        pltpu.VMEM((rows, width), f32), pltpu.VMEM((rows, width), f32),
        pltpu.VMEM((width, width), bf16), pltpu.VMEM((width, rows), bf16),
    ]
    if pieced:
        (planes,) = weights
        devices, _, *tile = planes.shape
        specs = [
            pl.BlockSpec((devices // 4, 4, *tile), lambda s: (upto(s), 1, 0, 0)),
            pl.BlockSpec((devices, 1, *tile), lambda s: (0, upto(s), 0, 0)),
        ]
        weights = planes, planes
        scratch += [pltpu.VMEM((width, width), bf16)] * 2
    else:
        specs = [pl.BlockSpec((width, width), lambda s: (upto(s), 0)), along(width)]
    sums = shape((8, width), f32)
    block = pl.BlockSpec((4, shard, width), lambda s: (s, 0, 0))
    blocks = shape((4 * 5, shard, width), bf16)
    still = lambda a: pl.BlockSpec(a.shape, lambda s: (0,) * a.ndim, pipeline_mode=pl.Buffered(1))
    outs = [
        (whole_spec(second), shape((rows, width), bf16)),
        (block, blocks),
        (block, blocks),
        (whole_spec(second), shape((rows, width), f32)),
        (whole_spec(second), shape((rows, width), bf16)),
        (along(8), shape((8, 4 * width), f32)),
        (whole_spec(sums), sums),
    ]
    return pl.pallas_call(
        lambda *refs: mlp_back_kernel(pieced, *refs),
        grid=(5,),
        in_specs=[
            along(rows), along(rows), still(middle), still(g), whole_spec(vecs), *specs,
            still(second), still(attended), still(proj),
        ],
        out_specs=[spec for spec, _ in outs],
        out_shape=[out for _, out in outs],
        scratch_shapes=scratch,
        compiler_params=BIG,
        cost_estimate=cost(0),
        name="mlp_back",
    )(active, slope, middle, g, vecs, *weights, second, attended, proj)


def qkv_back(hidden, pieces, weight, middle_grad, x, real, vecs, swapped, small, pieced):
    rows, width = x.shape
    shard = width // 8
    extra, two, up, tables = small
    whole = lambda a: pl.BlockSpec(a.shape, lambda s, w: (0,) * len(a.shape))
    planes = jax.ShapeDtypeStruct((12, shard, width), bf16)
    block = pl.BlockSpec((4, shard, width), lambda s, w: (s, 0, 0))
    outs = [jax.ShapeDtypeStruct((rows, width), f32), jax.ShapeDtypeStruct((SUM_ROWS, width), f32)]
    return pl.pallas_call(
        lambda *refs: qkv_back_kernel(pieced, *refs),
        grid_spec=pltpu.PrefetchScalarGridSpec(
            num_scalar_prefetch=1,
            grid=(3,),
            in_specs=[
                whole(hidden),
                *[pl.BlockSpec((1, *p.shape[1:]), lambda s, w: (s, 0, 0)) for p in pieces],
                pl.BlockSpec((width, width), lambda s, w: (0, s)),
                *[whole(a) for a in (middle_grad, x, real, vecs, *extra, two, up, *tables)],
            ],
            out_specs=[block, block, *[whole(out) for out in outs]],
            scratch_shapes=[
                pltpu.VMEM((rows, width), f32),
                pltpu.VMEM((3, 8, width), f32),
                pltpu.VMEM((width, width), bf16),
                pltpu.VMEM((width, rows), bf16),
            ],
        ),
        out_shape=[planes, planes, *outs],
        compiler_params=BIG,
        cost_estimate=cost(0),
        name="qkv_back",
    )(swapped, hidden, *pieces, weight, middle_grad, x, real, vecs, *extra, two, up, *tables)


SUM_ROWS = 24
SUM_AT = dict(query=0, value=1, proj=2, pre=3, mid=5, up=7, down=11, tables=16)


def small_sums(swapped_ref, column_ref, extra_refs, two_ref, one, up_ref, table_refs, out_ref):
    width = out_ref.shape[1]
    out_ref[...] = jnp.zeros_like(out_ref)

    def put(name, value, more=0):
        at = SUM_AT[name] + more
        out_ref[at : at + 1, :] = value

    put("query", column_ref[0, 0:1, :])
    extra = jnp.concatenate([ref[p, 0:1, :] for ref in extra_refs for p in range(ref.shape[0])], 1)
    put("value", column_ref[2, 0:1, :] + extra)
    put("proj", two_ref[2:3, :])
    for k in range(2):
        put("pre", one[k], k)
        put("mid", two_ref[k : k + 1, :], k)
    for k in range(4):
        put("up", up_ref[0:1, width * k : width * (k + 1)], k)
    put("down", two_ref[3:4, :])
    count = 32
    sums = [jnp.zeros((count, HEAD), f32) for _ in range(2)]
    for s in range(table_refs[0].shape[0]):
        grad = table_refs[0][s]
        for ref in table_refs[1:]:
            grad = grad + ref[s]
        both = (grad[:HEAD, HEAD:] + grad[HEAD:, :HEAD]).T
        parts = (both[:count], both[COLTABLE : COLTABLE + count])
        swap = swapped_ref[s] != 0
        sums[0] = sums[0] + jnp.where(swap, parts[1], parts[0])
        sums[1] = sums[1] + jnp.where(swap, parts[0], parts[1])
    tables = jnp.concatenate(sums, 1)
    at = SUM_AT["tables"]
    for k in range(4):
        out_ref[at : at + 8, LANES * k : LANES * (k + 1)] = tables[8 * k : 8 * k + 8]


def split_sums(total):
    count = lax.axis_size("dp") * lax.axis_size("row") * lax.axis_size("col")
    width = total.shape[1]

    def share(name, more=0, rows=1):
        at = SUM_AT[name] + more
        size = rows * width // count
        return lax.dynamic_slice(total[at : at + rows].reshape(-1), (device_number() * size,), (size,))

    at = SUM_AT["tables"]
    tables = jnp.concatenate([total[at : at + 8, LANES * k : LANES * (k + 1)] for k in range(4)], 0)
    tables = tables[: 2 * WIN - 1]
    vectors = (
        share("query", 0, 2), share("proj"), share("pre"), share("pre", 1), share("mid"),
        share("mid", 1), share("up", 0, 4), share("down"),
    )
    return vectors, (tables[:, :HEAD], tables[:, HEAD:])


def body(
    images, qkv_weight, qv_bias, proj_weight, proj_bias, pre_gain, pre_shift, mid_gain, mid_shift,
    up_weight, up_bias, down_weight, down_bias, rel_rows, rel_cols, cotangent,
):
    width = images.shape[-1]
    torus = on_torus()
    plan = plan_for(lax.axis_size("row"), lax.axis_size("col"), images.shape[0] * images.shape[1])
    move = Mover(plan)
    counts = plan.counts
    groups = ((0, 4), (4, 2))
    small = (qv_bias, proj_bias, pre_gain, pre_shift, mid_gain, mid_shift, up_bias, down_bias)
    pixels, cot = images.reshape(-1, width), cotangent.reshape(-1, width)
    swapped = move.swapped

    if torus:
        shard, planes = sent_shards(qkv_weight, up_weight, down_weight, proj_weight, small)
        first_steps = Steps(first_weights(shard))
        first_steps()
        (planes,) = gather_at_once(planes)
        weights = (planes,)
        sent = move.send(move.pack(pixels, cot))
        rel_rows, rel_cols = first_steps(rel_rows, rel_cols)
        tables, tables_back = position_tables(swapped, rel_rows, rel_cols)
        sent, tables = first_steps(sent, tables)
        x, g, real = move.receive(pixels, cot, arrived=sent, masked=True)
        qkv = first_steps.arrays
        vecs, up_add, bias, bias_v = vectors(qkv)
    else:
        sent = move.send(move.pack(pixels, cot))
        x, g, real = move.receive(pixels, cot, arrived=sent, masked=True)
        whole_qkv, *weights = gather_at_once(qkv_weight, up_weight, proj_weight, down_weight)
        qkv = (whole_qkv,)
        tables, tables_back = position_tables(swapped, rel_rows, rel_cols)
        vecs, up_add, bias, bias_v = gathered_vectors(small)

    hidden, projected, qkv = qkv_ahead(x, real, vecs, bias, qkv)
    attended, logsum = attend(projected, bias_v, tables, counts, 0, 6)
    middle, second, active, slope, proj, mine, other = up_ahead(
        x, attended, g, vecs, up_add, weights[:2] if len(weights) == 3 else weights
    )
    idle = lambda *values: values if len(values) != 1 else values[0]
    down_steps = up_sum = idle
    if torus:
        down_steps = Steps(halves_sum(mine, other))
    else:
        blocks = [v.reshape(4, 4, -1, width).swapaxes(0, 1) for v in (mine, other)]
        down_grad = jnp.stack(blocks, 1).reshape(-1, width)
    middle, second, active, slope = down_steps(middle, second, active, slope)
    middle, second, active, slope = down_steps(middle, second, active, slope)
    middle, second, active, slope = down_steps(middle, second, active, slope)
    result, *outs = mlp_back(
        active, slope, middle, g, vecs, (weights[2], weights[0]) if len(weights) == 3 else weights, second,
        attended, proj,
    )
    mine, other, middle_grad, attended_grad, up_add_grad, sums_two = down_steps(*outs)
    if torus:
        up_sum = Steps(scatter_sum(mine, other, 5))
    else:
        blocks = jnp.concatenate([mine.reshape(5, 4, -1, width), other.reshape(5, 4, -1, width)], 1)
        blocks = blocks.reshape(5, width, width)
        up_grad, proj_grad = jnp.swapaxes(blocks[:4], 0, 1).reshape(width, -1), blocks[4]
    attended_grad = up_sum(attended_grad)
    attended_grad = down_steps(attended_grad)
    attended_grad = up_sum(attended_grad)
    attended_grad = up_sum(attended_grad)
    pieces, table_grads, extra = [], [], []
    for first, count in groups:
        one, two, three = attend_back(
            projected, attended_grad, logsum[first : first + count], bias_v, tables, tables_back,
            counts, first,
        )
        pieces.append(one)
        table_grads.append(two)
        extra.append(three)
        attended_grad, pieces[-1] = order(attended_grad, one)
        if first == 0:
            attended_grad = down_steps(attended_grad)
            attended_grad = down_steps(attended_grad)
    if torus:
        pieces = up_sum(*pieces)
        pieces = up_sum(*pieces)
    small = extra, sums_two, up_add_grad, table_grads
    mine, other, images_grad, sums = qkv_back(
        hidden, pieces, qkv, middle_grad, x, real, vecs, swapped, small, torus
    )
    if torus:
        mine, other, images_grad, sums = up_sum(mine, other, images_grad, sums)
        mine, other, images_grad, sums = down_steps(mine, other, images_grad, sums)
        up_grad, proj_grad = up_sum.arrays
        (down_grad,) = down_steps.arrays
        qkv_sum = Steps(scatter_sum(mine, other, 3))
        images_grad, sums = qkv_sum(images_grad, sums)
        images_grad = qkv_sum(images_grad, more=(sums, over_core(sums)))
        images_grad = qkv_sum(images_grad)
        result, images_grad, up_grad, proj_grad, down_grad = order(
            result, images_grad, up_grad, proj_grad, down_grad
        )
        sent = move.send_back(move.pack_back(result, images_grad))
        result = qkv_sum(result)
        result = qkv_sum(result)
        out, images_grad = move.receive_back(result, images_grad, arrived=sent)
        out = qkv_sum(out)
        qkv_weight_grad, sums = qkv_sum.arrays
    else:
        blocks = jnp.concatenate(
            [mine.reshape(3, 4, -1, width), other.reshape(3, 4, -1, width)], 1
        ).reshape(3, width, width)
        qkv_weight_grad = jnp.swapaxes(blocks, 0, 1).reshape(width, -1)
        sent = move.send_back(move.pack_back(result, images_grad))
        out, images_grad = move.receive_back(result, images_grad, arrived=sent)
        sums = lax.psum(sums, AXES)
        qkv_weight_grad, proj_grad, up_grad, down_grad = [
            sum_at_once(g.astype(f32)) for g in (qkv_weight_grad, proj_grad, up_grad, down_grad)
        ]
    mine, full = split_sums(sums)
    return (
        out.reshape(images.shape),
        images_grad.reshape(images.shape),
        qkv_weight_grad,
        mine[0],
        proj_grad,
        mine[1],
        mine[2],
        mine[3],
        mine[4],
        mine[5],
        up_grad,
        mine[6],
        down_grad,
        mine[7],
        full[0],
        full[1],
    )


PLANS = {}


def plan_for(rows, cols, images):
    key = (rows, cols, images)
    if key not in PLANS:
        PLANS[key] = Plan(*key)
    return PLANS[key]


def solution(mesh):
    tokens = P(None, "dp", "row", "col", None)
    rows = P(AXES, None)
    vector = P(AXES)
    placed = (
        tokens, rows, vector, rows, vector, vector, vector, vector, vector,
        rows, vector, rows, vector, P(), P(), tokens,
    )
    given = (tokens, tokens, rows, vector, rows, vector, vector, vector, vector, vector,
             rows, vector, rows, vector, P(), P())
    return jax.shard_map(body, mesh=mesh, in_specs=placed, out_specs=given, check_vma=False)
```

```python
import math

import jax
import jax.numpy as jnp
import numpy as np
from jax import lax
from jax.experimental import pallas as pl
from jax.experimental.pallas import tpu as pltpu
from jax.sharding import PartitionSpec as P

HEAD = 64
WIN = 14
GRID = 64
NWIN = 5
PITCH = 16
KEYS = WIN * PITCH
LANES = 128
ROWFIELD, COLFIELD, LOWFIELD, MASKLANE = 0, 14, 28, 56
COLTABLE = 32
NEG = -1e30
GROUP = 4
COST = 1024
EDGE = GRID - WIN * (NWIN - 1)
epsilon = 1e-06
bf16 = jnp.bfloat16
f32 = jnp.float32


def cost(flops):
    return pl.CostEstimate(flops=COST, bytes_accessed=1024, transcendentals=0)


def dot_nn(a, b):
    return lax.dot_general(a, b, (((1,), (0,)), ((), ())), preferred_element_type=f32)


def dot_nt(a, b):
    return lax.dot_general(a, b, (((1,), (1,)), ((), ())), preferred_element_type=f32)


def dot_tn(a, b):
    return lax.dot_general(a, b, (((0,), (0,)), ((), ())), preferred_element_type=f32)


def key_fields(reverse):
    shape = (KEYS, LANES)
    t = lax.broadcasted_iota(jnp.int32, shape, 0)
    a, b = t // PITCH, t % PITCH
    lane = lax.broadcasted_iota(jnp.int32, shape, 1) % HEAD
    if reverse:
        one = (lane == ROWFIELD + WIN - 1 - a) | (lane == COLFIELD + WIN - 1 - b)
        return jnp.where(one & (b < WIN), 1.0, 0.0).astype(bf16)
    one = (lane == ROWFIELD + a) | (lane == LOWFIELD + ROWFIELD + a)
    one = one | (lane == COLFIELD + b) | (lane == LOWFIELD + COLFIELD + b)
    out = jnp.where(one & (b < WIN), 1.0, 0.0)
    return jnp.where((lane == MASKLANE) & (b >= WIN), NEG, out).astype(bf16)


def tables_kernel(swapped_ref, rows_ref, cols_ref, ahead_ref, back_ref):
    shape = (2 * WIN - 1, HEAD)
    index = lax.broadcasted_iota(jnp.int32, shape, 0)
    lane = lax.broadcasted_iota(jnp.int32, shape, 1)
    empty = jnp.zeros((HEAD, HEAD), f32)
    for ref, place in ((ahead_ref, 2 * WIN - 2 - index), (back_ref, index)):
        spots = [jnp.where(lane == place + start, 1.0, 0.0).astype(bf16) for start in (0, COLTABLE)]
        both = []
        for one, two in ((rows_ref, cols_ref), (cols_ref, rows_ref)):
            half = dot_tn(one[...], spots[0]) + dot_tn(two[...], spots[1])
            full = [jnp.concatenate(pair, 1) for pair in ((empty, half), (half, empty))]
            both.append(jnp.concatenate(full, 0).astype(bf16))
        for s in range(ref.shape[0]):

            @pl.when(swapped_ref[s] == 0)
            def _():
                ref[s] = both[0]

            @pl.when(swapped_ref[s] != 0)
            def _():
                ref[s] = both[1]


def position_tables(swapped, rel_rows, rel_cols):
    one = jax.ShapeDtypeStruct((swapped.shape[0], LANES, LANES), bf16)
    return pl.pallas_call(
        tables_kernel,
        grid_spec=pltpu.PrefetchScalarGridSpec(
            num_scalar_prefetch=1,
            grid=(1,),
            in_specs=[pl.BlockSpec(rel_rows.shape, lambda s, w: (0, 0))] * 2,
            out_specs=[pl.BlockSpec(one.shape, lambda s, w: (0, 0, 0))] * 2,
        ),
        out_shape=[one, one],
        cost_estimate=cost(0),
        name="position_tables",
    )(swapped, rel_rows, rel_cols)


def lane_in(shape, start, count):
    lane = lax.broadcasted_iota(jnp.int32, shape, 1) % HEAD
    return (lane >= start) & (lane < start + count)


def query_fields(q2, table):
    turned = dot_nn(q2, table)
    parts = []
    shape = (PITCH, LANES)
    in_rows = lane_in(shape, ROWFIELD, WIN)
    in_cols = lane_in(shape, COLFIELD, WIN)
    for a in range(q2.shape[0] // PITCH):
        t = turned[PITCH * a : PITCH * (a + 1)]
        r = pltpu.roll(t, (a - WIN + 1) % LANES, 1)
        c = pltpu.roll(t, LANES - (COLTABLE + 2 * WIN - 2 - (WIN - 1) - COLFIELD), 1, stride=1, stride_axis=0)
        parts.append(jnp.where(in_rows, r, jnp.where(in_cols, c, 0.0)))
    full = jnp.concatenate(parts, 0)
    high = full.astype(bf16).astype(f32)
    low = pltpu.roll(full - high, LOWFIELD, 1)
    one = jnp.where(lane_in(full.shape, MASKLANE, 1), 1.0, 0.0)
    return (high + low + one).astype(bf16)


def field_tables(fields):
    parts = []
    shape = (PITCH, LANES)
    in_rows = lane_in(shape, ROWFIELD, WIN)
    in_cols = lane_in(shape, COLFIELD, WIN)
    for a in range(fields.shape[0] // PITCH):
        t = fields[PITCH * a : PITCH * (a + 1)]
        r = jnp.where(in_rows, t, 0.0)
        c = jnp.where(in_cols, t, 0.0)
        r = pltpu.roll(r, a, 1) if a else r
        c = pltpu.roll(c, COLTABLE - COLFIELD, 1, stride=1, stride_axis=0)
        parts.append(r + c)
    return jnp.concatenate(parts, 0)


def first_half(shape, axis):
    return lax.broadcasted_iota(jnp.int32, shape, axis) < HEAD


def padded_rows(block, fill):
    if block.shape[0] == KEYS:
        return block
    rest = (KEYS - block.shape[0], LANES)
    return jnp.concatenate([block, jnp.broadcast_to(fill, rest).astype(block.dtype)], 0)


def pick(mask, head, one, two):
    return jnp.where(mask, one, two) if head == 0 else jnp.where(mask, two, one)


def slot_groups(slots):
    order = list(range(len(slots)))
    return [order[k : k + GROUP] for k in range(0, len(order), GROUP)]


def attend_kernel(slots, q_ref, k_ref, v_ref, vb_ref, tab_ref, att_ref, lse_ref):
    kf = key_fields(False)
    leftk = first_half((KEYS, LANES), 1)
    one = jnp.ones((KEYS, LANES), bf16)
    for group in slot_groups(slots):
        work = []
        for s in group:
            row, count, lane0 = slots[s]
            rows = pl.ds(row, count)
            q2 = q_ref[rows, :]
            k2 = padded_rows(k_ref[rows, :] * bf16(HEAD ** -0.5), jnp.zeros((1, LANES), bf16))
            v2 = padded_rows(v_ref[rows, :], vb_ref[0:1, :])
            x2 = query_fields(q2, tab_ref[s])
            left = first_half((count, LANES), 1)
            for e in range(2):
                work.append((s, e, pick(left, e, q2, x2), pick(leftk, e, k2, kf), pick(leftk, e, v2, one)))
        st = [dot_nt(ka, qa) for _, _, qa, ka, _ in work]
        peak = [jnp.max(v, axis=0, keepdims=True) for v in st]
        pt = [jnp.exp(v - p).astype(bf16) for v, p in zip(st, peak)]
        ot = [dot_tn(w[4], p) for w, p in zip(work, pt)]
        outs = []
        for (s, e, *_), p, o in zip(work, peak, ot):
            _, count, lane0 = slots[s]
            mass = o[HEAD : HEAD + 1] if e == 0 else o[0:1]
            lse_ref[0, e : e + 1, lane0 : lane0 + count] = p + jnp.log(mass)
            outs.append(o * (1.0 / mass))
        for k, s in enumerate(group):
            row, count, _ = slots[s]
            both = jnp.where(first_half((LANES, count), 0), outs[2 * k], outs[2 * k + 1])
            att_ref[pl.ds(row, count), :] = both.T.astype(bf16)


def attend_back_kernel(
    slots, q_ref, k_ref, v_ref, do_ref, lse_ref, vb_ref, tab_ref, tabb_ref,
    dqkv_ref, dtab_ref, dvb_ref,
):
    kf = key_fields(False)
    kb = key_fields(True)
    extra = jnp.zeros((1, LANES), f32)

    @pl.when(pl.program_id(0) == 0)
    def _():
        dtab_ref[...] = jnp.zeros_like(dtab_ref)

    leftk = first_half((KEYS, LANES), 1)
    zero = jnp.zeros((KEYS, LANES), bf16)
    for group in slot_groups(slots):
        work = []
        for s in group:
            row, count, lane0 = slots[s]
            rows = pl.ds(row, count)
            q2 = q_ref[rows, :]
            do2 = do_ref[rows, :]
            k2 = padded_rows(k_ref[rows, :] * bf16(HEAD ** -0.5), jnp.zeros((1, LANES), bf16))
            v2 = padded_rows(v_ref[rows, :], vb_ref[0:1, :])
            x2 = query_fields(q2, tab_ref[s])
            left = first_half((count, LANES), 1)
            for e in range(2):
                work.append((s, e, pick(left, e, q2, x2), k2, v2, do2))
        st = [dot_nt(pick(leftk, e, k2, kf), qa) for _, e, qa, k2, _, _ in work]
        dpt = [dot_nt(pick(leftk, e, v2, zero), do2) for _, e, _, _, v2, do2 in work]
        pt = []
        for (s, e, *_), v in zip(work, st):
            _, count, lane0 = slots[s]
            pt.append(jnp.exp(v - lse_ref[0, e : e + 1, lane0 : lane0 + count]))
        mean = [jnp.sum(p * d, axis=0, keepdims=True) for p, d in zip(pt, dpt)]
        dst = [(p * (d - m)).astype(bf16) for p, d, m in zip(pt, dpt, mean)]
        dv = [dot_nn(p.astype(bf16), w[5]) for p, w in zip(pt, work)]
        dk = [dot_nn(d, w[2]) for d, w in zip(dst, work)]
        dq = [dot_tn(d, pick(leftk, w[1], w[3], kb)) for d, w in zip(dst, work)]
        for k, s in enumerate(group):
            row, count, _ = slots[s]
            rows = pl.ds(row, count)
            left = first_half((count, LANES), 1)
            one, two = 2 * k, 2 * k + 1
            dt = field_tables(jnp.where(left, dq[two], dq[one]))
            high = dt.astype(bf16)
            low = (dt - high.astype(f32)).astype(bf16)
            tabb = tabb_ref[s]
            dq2 = jnp.where(left, dq[one], dq[two]) + dot_nt(high, tabb) + dot_nt(low, tabb)
            dk2 = jnp.where(leftk, dk[one], dk[two]) * (HEAD ** -0.5)
            dv2 = jnp.where(leftk, dv[one], dv[two])
            dqkv_ref[0, rows, :] = dq2.astype(bf16)
            dqkv_ref[1, rows, :] = dk2[:count].astype(bf16)
            dqkv_ref[2, rows, :] = dv2[:count].astype(bf16)
            if count < KEYS:
                extra = extra + jnp.sum(dv2[count:], axis=0, keepdims=True)
            q2 = q_ref[rows, :]
            dtab_ref[s] += dot_tn(q2, high) + dot_tn(q2, low)
    dvb_ref[0] = jnp.broadcast_to(extra, (8, LANES))


def slot_places(counts):
    places, row, lane = [], 0, 0
    for count in counts:
        places.append((row, count, lane))
        row += count
        lane += -(-count // LANES) * LANES
    return tuple(places), row, lane


def attend(projected, bias_v, tables, counts, first, count):
    slots, rows, lanes = slot_places(counts)
    width = projected.shape[1] // 3
    pairs = width // LANES
    col = lambda off: pl.BlockSpec((rows, LANES), lambda p: (0, off * pairs + first + p))
    return pl.pallas_call(
        lambda *refs: attend_kernel(slots, *refs),
        grid=(count,),
        in_specs=[
            col(0), col(1), col(2),
            pl.BlockSpec((8, LANES), lambda p: (0, first + p)),
            pl.BlockSpec((len(counts), LANES, LANES), lambda p: (0, 0, 0)),
        ],
        out_specs=[
            pl.BlockSpec((rows, LANES), lambda p: (0, p)),
            pl.BlockSpec((1, 8, lanes), lambda p: (p, 0, 0)),
        ],
        out_shape=[
            jax.ShapeDtypeStruct((rows, count * LANES), bf16),
            jax.ShapeDtypeStruct((count, 8, lanes), f32),
        ],
        compiler_params=pltpu.CompilerParams(vmem_limit_bytes=48 << 20),
        cost_estimate=pl.CostEstimate(flops=COST, bytes_accessed=1024, transcendentals=0),
        name="attend",
    )(projected, projected, projected, bias_v, tables)


def attend_back(projected, upstream, lse, bias_v, tables, tables_back, counts, first):
    count = lse.shape[0]
    slots, rows, lanes = slot_places(counts)
    width = projected.shape[1] // 3
    pairs = width // LANES
    col = lambda off: pl.BlockSpec((rows, LANES), lambda p: (0, off * pairs + first + p))
    n = len(counts)
    return pl.pallas_call(
        lambda *refs: attend_back_kernel(slots, *refs),
        grid=(count,),
        in_specs=[
            col(0), col(1), col(2), col(0),
            pl.BlockSpec((1, 8, lanes), lambda p: (p, 0, 0)),
            pl.BlockSpec((8, LANES), lambda p: (0, first + p)),
            pl.BlockSpec((n, LANES, LANES), lambda p: (0, 0, 0)),
            pl.BlockSpec((n, LANES, LANES), lambda p: (0, 0, 0)),
        ],
        out_specs=[
            pl.BlockSpec((3, rows, LANES), lambda p: (0, 0, p)),
            pl.BlockSpec((n, LANES, LANES), lambda p: (0, 0, 0)),
            pl.BlockSpec((1, 8, LANES), lambda p: (p, 0, 0)),
        ],
        out_shape=[
            jax.ShapeDtypeStruct((3, rows, count * LANES), bf16),
            jax.ShapeDtypeStruct((n, LANES, LANES), f32),
            jax.ShapeDtypeStruct((count, 8, LANES), f32),
        ],
        compiler_params=pltpu.CompilerParams(vmem_limit_bytes=48 << 20),
        cost_estimate=pl.CostEstimate(flops=COST, bytes_accessed=1024, transcendentals=0),
        name="attend_back",
    )(projected, projected, projected, upstream, lse, bias_v, tables, tables_back)


def sides(index):
    return WIN * index, min(WIN * index + WIN, GRID)


class Plan:
    def __init__(self, rows, cols, images):
        self.rows, self.cols, self.images = rows, cols, images
        self.devices = rows * cols
        self.tile_rows, self.tile_cols = GRID // rows, GRID // cols
        self.tokens = images * self.tile_rows * self.tile_cols
        kinds = ([], [], [])
        for n in range(images):
            for i in range(NWIN):
                for j in range(NWIN):
                    kinds[(i == NWIN - 1) + (j == NWIN - 1)].append((n, i, j))
        self.caps = tuple(-(-len(kind) // self.devices) for kind in kinds)
        self.parts = {w: self._sources(w) for kind in kinds for w in kind}
        owner = self._assign(kinds)
        self.counts = (KEYS,) * self.caps[0] + (EDGE * PITCH,) * (self.caps[1] + self.caps[2])
        _, self.window_rows, _ = slot_places(self.counts)
        self._tables(kinds, owner)

    def _distance(self, one, two):
        r, c = divmod(one, self.cols)
        q, e = divmod(two, self.cols)
        return abs(c - e) + abs(r // 2 - q // 2) + (0.125 if r % 2 != q % 2 else 0.0)

    def _sources(self, window):
        _, i, j = window
        (r0, r1), (c0, c1) = sides(i), sides(j)
        tr, tc = self.tile_rows, self.tile_cols
        found = {}
        for r in range(r0 // tr, (r1 - 1) // tr + 1):
            for c in range(c0 // tc, (c1 - 1) // tc + 1):
                high = min(r1, (r + 1) * tr) - max(r0, r * tr)
                wide = min(c1, (c + 1) * tc) - max(c0, c * tc)
                found[r * self.cols + c] = high * wide
        return found

    def _rounds(self, owner):
        pairs = {}
        for window, dev in owner.items():
            for source, amount in self.parts[window].items():
                if source != dev:
                    pairs[source, dev] = pairs.get((source, dev), 0) + amount
        rounds = []
        for pair, amount in sorted(pairs.items(), key=lambda p: (-p[1], p[0])):
            for senders, takers, members in rounds:
                if pair[0] not in senders and pair[1] not in takers:
                    break
            else:
                senders, takers, members = set(), set(), []
                rounds.append((senders, takers, members))
            senders.add(pair[0])
            takers.add(pair[1])
            members.append(pair)
        return pairs, [members for _, _, members in rounds]

    def _cost(self, owner):
        pairs, rounds = self._rounds(owner)
        moved = sum(amount * self._distance(*pair) for pair, amount in pairs.items())
        return moved / 4 + sum(64 + max(pairs[p] for p in members) for members in rounds)

    def _assign(self, kinds):
        owner = {}
        room = {}
        for kind, windows in enumerate(kinds):
            room[kind] = [self.caps[kind]] * self.devices
            for window in sorted(windows, key=lambda w: (-(w[1] + w[2]), w)):
                far = lambda d: sum(t * self._distance(s, d) for s, t in self.parts[window].items())
                dev = min((d for d in range(self.devices) if room[kind][d]), key=lambda d: (far(d), d))
                owner[window] = dev
                room[kind][dev] -= 1
        best = self._cost(owner)
        for _ in range(4):
            before = best
            for kind in (1, 2, 0):
                for one in kinds[kind]:
                    for dev in range(self.devices):
                        if dev == owner[one]:
                            continue
                        trials = []
                        if room[kind][dev]:
                            trials.append({**owner, one: dev})
                        for two in kinds[kind]:
                            if owner[two] == dev:
                                trials.append({**owner, one: dev, two: owner[one]})
                        for trial in trials:
                            price = self._cost(trial)
                            if price < best - 1e-9:
                                if sum(trial[w] != owner[w] for w in kinds[kind]) == 1:
                                    room[kind][owner[one]] += 1
                                    room[kind][dev] -= 1
                                owner, best = trial, price
                                break
            if best >= before:
                break
        return owner

    def _tables(self, kinds, owner):
        places, _, _ = slot_places(self.counts)
        starts = (0, self.caps[0], self.caps[0] + self.caps[1])
        self.swapped = np.zeros((self.devices, len(self.counts)), np.int32)
        taken = {}
        moves = {}
        for kind, windows in enumerate(kinds):
            for window in windows:
                n, i, j = window
                dev = owner[window]
                slot = starts[kind] + taken.get((dev, kind), 0)
                taken[dev, kind] = taken.get((dev, kind), 0) + 1
                swap = kind == 1 and j == NWIN - 1
                self.swapped[dev, slot] = swap
                (r0, r1), (c0, c1) = sides(i), sides(j)
                for r in range(r0, r1):
                    for c in range(c0, c1):
                        a, b = (c - c0, r - r0) if swap else (r - r0, c - c0)
                        row = places[slot][0] + PITCH * a + b
                        source = (r // self.tile_rows) * self.cols + c // self.tile_cols
                        token = (n * self.tile_rows + r % self.tile_rows) * self.tile_cols
                        token += c % self.tile_cols
                        moves.setdefault((source, dev), []).append((token, row))
        _, rounds = self._rounds(owner)
        self.perms = rounds
        self.sizes = [-(-max(len(moves[p]) for p in members) // PITCH) * PITCH for members in rounds]
        total = sum(self.sizes)
        self.pack = np.full((self.devices, total), -1, np.int32)
        self.take = np.full((self.devices, self.window_rows), -1, np.int32)
        self.pack_back = np.full((self.devices, total), -1, np.int32)
        self.take_back = np.full((self.devices, self.tokens), -1, np.int32)
        for dev in range(self.devices):
            for token, row in moves.get((dev, dev), ()):
                self.take[dev, row] = token
                self.take_back[dev, token] = row
        at = 0
        for members, size in zip(rounds, self.sizes):
            for source, dev in members:
                for k, (token, row) in enumerate(moves[source, dev]):
                    self.pack[source, at + k] = token
                    self.take[dev, row] = self.tokens + at + k
                    self.pack_back[dev, at + k] = row
                    self.take_back[source, token] = self.window_rows + at + k
            at += size


def chosen(index, start, count):
    spot = lax.broadcasted_iota(jnp.int32, (count, index.shape[1]), 0) + start
    return jnp.where(spot == index, 1.0, 0.0).astype(bf16)


def pack_kernel(sizes, index_ref, *refs):
    token_refs, out_refs = refs[: len(refs) - len(sizes)], refs[len(refs) - len(sizes) :]
    at = 0
    for size, out_ref in zip(sizes, out_refs):
        hot = chosen(index_ref[0:1, at : at + size], 0, token_refs[0].shape[0])
        for k, ref in enumerate(token_refs):
            width = ref.shape[1]
            moved = dot_tn(hot, ref[...].astype(bf16)).astype(bf16)
            out_ref[:, width * k : width * (k + 1)] = moved
        at += size


def pack(index, tokens, sizes):
    width = sum(t.shape[1] for t in tokens)
    return pl.pallas_call(
        lambda *refs: pack_kernel(sizes, *refs),
        out_shape=[jax.ShapeDtypeStruct((size, width), bf16) for size in sizes],
        compiler_params=pltpu.CompilerParams(vmem_limit_bytes=40 << 20),
        cost_estimate=cost(0),
        name="pack",
    )(index[None], *tokens)


def take_kernel(count, masked, index_ref, *refs):
    local_refs, arrived, out_refs = refs[:count], refs[count : -count - masked], refs[-count - masked :]
    index = index_ref[...]
    at = local_refs[0].shape[0]
    hot = chosen(index, 0, at)
    totals = []
    for ref in local_refs:
        local = ref[...]
        total = dot_tn(hot, local.astype(bf16))
        if local.dtype == f32:
            total = total + dot_tn(hot, (local - local.astype(bf16).astype(f32)).astype(bf16))
        totals.append(total)
    for ref in arrived:
        hot = chosen(index, at, ref.shape[0])
        width = ref.shape[1] // count
        totals = [
            t + dot_tn(hot, ref[:, width * k : width * (k + 1)]) for k, t in enumerate(totals)
        ]
        at += ref.shape[0]
    for ref, total in zip(out_refs, totals):
        ref[...] = total.astype(ref.dtype)
    if masked:
        row = jnp.where(index >= 0, 1.0, 0.0)
        out_refs[-1][...] = jnp.broadcast_to(row, (LANES, row.shape[1])).T


def take(index, locals_, arrived, masked=False):
    shapes = [((index.shape[0], local.shape[1]), local.dtype) for local in locals_]
    if masked:
        shapes.append(((index.shape[0], LANES), f32))
    return pl.pallas_call(
        lambda *refs: take_kernel(len(locals_), int(masked), *refs),
        out_shape=[jax.ShapeDtypeStruct(*shape) for shape in shapes],
        compiler_params=pltpu.CompilerParams(vmem_limit_bytes=40 << 20),
        cost_estimate=cost(0),
        name="take",
    )(index[None], *locals_, *arrived)


class Mover:
    def __init__(self, plan):
        self.plan = plan
        here = lax.axis_index("row") * plan.cols + lax.axis_index("col")
        mine = lambda table: lax.dynamic_index_in_dim(jnp.asarray(table), here, 0, keepdims=False)
        self.index = {name: mine(getattr(plan, name)) for name in ("pack", "take", "pack_back", "take_back")}
        self.swapped = mine(plan.swapped)

    def pack(self, *tokens):
        return pack(self.index["pack"], tokens, self.plan.sizes)

    def send(self, packed):
        return [lax.ppermute(s, ("row", "col"), perm) for s, perm in zip(packed, self.plan.perms)]

    def receive(self, *tokens, arrived, masked=False):
        return take(self.index["take"], tokens, arrived, masked)

    def pack_back(self, *rows):
        return pack(self.index["pack_back"], rows, self.plan.sizes)

    def send_back(self, packed):
        back = [[(two, one) for one, two in perm] for perm in self.plan.perms]
        return [lax.ppermute(s, ("row", "col"), perm) for s, perm in zip(packed, back)]

    def receive_back(self, *rows, arrived):
        return take(self.index["take_back"], rows, arrived)


AXES = ("dp", "row", "col")
TORUS = (2, 4, 4)


def order(*values):
    return lax.optimization_barrier(values)


def over_dp(v):
    return lax.ppermute(v, "dp", [(0, 1), (1, 0)])


def over_y(v):
    return lax.ppermute(v, "row", [(r, (r + 2) % 4) for r in range(4)])


def over_both(v):
    return lax.ppermute(v, ("dp", "row"), [(k, (k // 4 + 1) % 2 * 4 + (k % 4 + 2) % 4) for k in range(8)])


def over_core(v):
    return lax.ppermute(v, "row", [(r, r ^ 1) for r in range(4)])


def over_col(v, steps):
    return lax.ppermute(v, "col", [(c, (c + steps) % 4) for c in range(4)])


def block_at(flip_dp, flip_y, flip_core):
    dp, row = lax.axis_index("dp"), lax.axis_index("row")
    return (
        ((dp + flip_dp) % 2) * 4 + ((row // 2 + flip_y) % 2) * 2 + (row % 2 + flip_core) % 2
    )


KINDS = ((0, 0), (1, 0), (0, 1), (1, 1))


def column_kernel(store, *refs):
    seen, out_ref = refs[:4], refs[4]
    place = lax.axis_index("col")
    for j in range(4):
        for k in range(4):

            @pl.when((place - j) % 4 == k)
            def _():
                store(out_ref, j, seen[k])


def in_column(shard, store, shape):
    seen = [shard] + [over_col(shard, k) for k in (1, 2, 3)]
    return pl.pallas_call(
        lambda *refs: column_kernel(store, *refs),
        out_shape=jax.ShapeDtypeStruct(shape, bf16),
        cost_estimate=cost(0),
        name="in_column",
    )(*seen)


SMALL = 8


def shards_kernel(qkv_ref, up_ref, down_ref, proj_ref, *refs):
    first_ref, planes_ref = refs[-2:]
    rows, width = proj_ref.shape
    for k in range(3):
        first_ref[rows * k : rows * (k + 1), :] = qkv_ref[:, width * k : width * (k + 1)]
    first_ref[3 * rows :, :] = jnp.zeros((SMALL, width), bf16)
    for k, ref in enumerate(refs[:-2]):
        first_ref[3 * rows + k : 3 * rows + k + 1, 0 : ref.shape[1]] = ref[...]
    for k in range(4):
        planes_ref[0, k] = up_ref[:, width * k : width * (k + 1)]
        planes_ref[0, 4 + k] = down_ref[rows * k : rows * (k + 1), :]
    planes_ref[0, 8] = proj_ref[...]


def sent_shards(qkv_weight, up_weight, down_weight, proj_weight, small):
    rows, width = proj_weight.shape
    return pl.pallas_call(
        shards_kernel,
        out_shape=[
            jax.ShapeDtypeStruct((3 * rows + SMALL, width), bf16),
            jax.ShapeDtypeStruct((1, 9, rows, width), bf16),
        ],
        cost_estimate=cost(0),
        name="sent_shards",
    )(qkv_weight, up_weight, down_weight, proj_weight, *[v[None] for v in small])


def first_weights(shard):
    rows, width = (shard.shape[0] - SMALL) // 3, shard.shape[1]
    (shard,) = yield (shard,)

    def store(ref, j, shard):
        for plane in range(3):
            at = rows * (4 * plane + j)
            ref[at : at + rows, :] = shard[rows * plane : rows * (plane + 1), :]
        at = 12 * rows + SMALL * j
        ref[at : at + SMALL, :] = shard[3 * rows :, :]

    own = in_column(shard, store, (12 * rows + 4 * SMALL, width))
    (own,) = yield (own,)
    pieces = [own, over_dp(own), over_y(own), over_both(own)]
    pieces = yield pieces
    pieces = [*pieces, *[over_core(p) for p in pieces]]
    yield pieces


PAIR = 48


def put_rows(ref, at, value):
    high = value.astype(bf16)
    count = value.shape[0]
    ref[at : at + count, :] = high
    ref[at + count : at + 2 * count, :] = (value - high.astype(f32)).astype(bf16)


def both_rows(ref, at):
    half = PAIR // 2
    return ref[at : at + half, :].astype(f32) + ref[at + half : at + 2 * half, :].astype(f32)


def core_kernel(planes, small, mine_ref, came_ref, *refs):
    own_ref, sent_refs = refs[2 * small], refs[2 * small + 1 : 2 * small + 4]
    rows = mine_ref.shape[1]
    for plane in range(planes):
        at = rows * plane
        for k in range(4):
            total = mine_ref[4 * plane + k].astype(f32) + came_ref[4 * plane + k].astype(f32)
            if k:
                sent_refs[k - 1][at : at + rows, :] = total.astype(bf16)
            else:
                own_ref[at : at + rows, :] = total
    if small:
        total = refs[0][...] + refs[1][...]
        refs[-1][...] = total
        for ref in sent_refs:
            put_rows(ref, rows * planes, total)


def chips_kernel(planes, small, own_ref, dp_ref, y_ref, both_ref, *refs):
    mine_ref, sent_refs, column = refs[small], refs[small + 1 : small + 4], refs[-1]
    count = own_ref.shape[0] // planes // 4
    total = own_ref[...]
    for ref in (dp_ref, y_ref, both_ref):
        total = total + ref[: own_ref.shape[0], :].astype(f32)
    column[...] = total
    place = lax.axis_index("col")
    for k in range(4):
        for plane in range(planes):
            at = pl.multiple_of(4 * count * plane + (place + k) % 4 * count, count)
            rows = column[pl.ds(at, count), :]
            if k:
                sent_refs[k - 1][count * plane : count * (plane + 1), :] = rows.astype(bf16)
            else:
                mine_ref[plane] = rows
    if small:
        total = refs[0][...]
        for ref in (dp_ref, y_ref, both_ref):
            total = total + both_rows(ref, own_ref.shape[0])
        refs[-2][...] = total
        for ref in sent_refs:
            put_rows(ref, count * planes, total)


def column_sum_kernel(planes, small, mine_ref, *refs):
    came = refs[:3]
    out_refs = refs[3 + small :]
    count, width = mine_ref.shape[1:]
    for plane in range(planes):
        total = mine_ref[plane]
        for ref in came:
            total = total + ref[count * plane : count * (plane + 1), :].astype(f32)
        wide = out_refs[0].shape[1] // width
        if plane < wide:
            out_refs[0][:, width * plane : width * (plane + 1)] = total
        else:
            out_refs[1][...] = total
    if small:
        total = refs[3][...]
        for ref in came:
            total = total + both_rows(ref, count * planes)
        out_refs[-1][...] = total


def scatter_sum(mine, other, planes, whole=False):
    rows, width = mine.shape[1:]
    params = pltpu.CompilerParams(vmem_limit_bytes=40 << 20)
    shape = lambda kind, *dims: jax.ShapeDtypeStruct(dims, kind)
    (other,) = yield (other,)
    came = over_core(other)
    came, *given = yield (came,)
    small = len(given) // 2
    extra = PAIR * small
    sums = [shape(f32, PAIR // 2, width)] * small
    own, *rest = pl.pallas_call(
        lambda *refs: core_kernel(planes, small, *refs),
        out_shape=[shape(f32, planes * rows, width)]
        + [shape(bf16, planes * rows + extra, width)] * 3
        + sums,
        compiler_params=params,
        cost_estimate=cost(0),
        name="core_sum",
    )(mine, came, *given)
    own, *rest = yield (own, *rest)
    given = rest[3:]
    units = 1 if whole else planes
    count = planes * rows // units // 4
    came = yield (over_dp(rest[0]), over_y(rest[1]), over_both(rest[2]))
    mine, *rest = pl.pallas_call(
        lambda *refs: chips_kernel(units, small, *refs),
        out_shape=[shape(f32, units, count, width)]
        + [shape(bf16, units * count + extra, width)] * 3
        + sums,
        scratch_shapes=[pltpu.VMEM((planes * rows, width), f32)],
        compiler_params=params,
        cost_estimate=cost(0),
        name="chips_sum",
    )(own, *came, *given)
    mine, *rest = yield (mine, *rest)
    given = rest[3:]
    came = yield [over_col(v, k) for k, v in zip((1, 2, 3), rest)]
    wide = min(units, 4)
    yield pl.pallas_call(
        lambda *refs: column_sum_kernel(units, small, *refs),
        out_shape=[shape(f32, count, wide * width)]
        + [shape(f32, count, width)] * (units - wide)
        + sums,
        compiler_params=params,
        cost_estimate=cost(0),
        name="column_sum",
    )(mine, *came, *given)


def column_pair(v, steps):
    return lax.ppermute(v, "col", [(k, k ^ steps) for k in range(4)])


def half_kernel(bit, arrays, *refs):
    given, (mine_ref, sent_ref, kept) = refs[:arrays], refs[arrays:]
    total = given[0][...]
    for ref in given[1:]:
        total = total + ref[...].astype(f32)
    kept[...] = total
    place = lax.axis_index("col")
    half = place // 2 if bit == 2 else place % 2
    size = kept.shape[0] // 2
    mine_ref[...] = kept[pl.ds(pl.multiple_of(half * size, 8), size), :]
    sent_ref[...] = kept[pl.ds(pl.multiple_of((1 - half) * size, 8), size), :].astype(bf16)


def last_kernel(mine_ref, came_ref, out_ref):
    out_ref[...] = mine_ref[...] + came_ref[...].astype(f32)


def halves_sum(mine, other):
    shard, width = mine.shape[1:]
    rows = 4 * shard
    params = pltpu.CompilerParams(vmem_limit_bytes=40 << 20)
    shape = lambda kind, *dims: jax.ShapeDtypeStruct(dims, kind)
    (other,) = yield (other,)
    (came,) = yield (over_core(other),)
    sums = pl.pallas_call(
        lambda *refs: core_kernel(4, 0, *refs),
        out_shape=[shape(f32, rows, width)] + [shape(bf16, rows, width)] * 3,
        compiler_params=params,
        cost_estimate=cost(0),
        name="core_sum",
    )(mine, came)
    own, *rest = yield sums
    came = yield (over_dp(rest[0]), over_y(rest[1]), over_both(rest[2]))
    given = (own, *came)
    for bit in (2, 1):
        mine, sent = pl.pallas_call(
            lambda *refs: half_kernel(bit, len(given), *refs),
            out_shape=[shape(f32, rows // 2, width), shape(bf16, rows // 2, width)],
            scratch_shapes=[pltpu.VMEM((rows, width), f32)],
            compiler_params=params,
            cost_estimate=cost(0),
            name="half_sum",
        )(*given)
        rows //= 2
        mine, sent = yield (mine, sent)
        (came,) = yield (column_pair(sent, bit),)
        given = (mine, came)
    yield (
        pl.pallas_call(
            last_kernel,
            out_shape=shape(f32, rows, width),
            cost_estimate=cost(0),
            name="last_sum",
        )(*given),
    )


class Steps:
    def __init__(self, steps):
        self.steps = steps
        self.arrays = tuple(next(steps))

    def __call__(self, *values, more=()):
        values, arrays, more = lax.optimization_barrier((values, self.arrays, tuple(more)))
        self.arrays = tuple(self.steps.send((*arrays, *more)))
        return values if len(values) != 1 else values[0]


def on_torus():
    return tuple(lax.axis_size(a) for a in AXES) == TORUS


def device_number():
    return (lax.axis_index("dp") * lax.axis_size("row") + lax.axis_index("row")) * lax.axis_size(
        "col"
    ) + lax.axis_index("col")


def gather_at_once(*shards):
    return tuple(lax.all_gather(s, AXES, axis=0, tiled=True) for s in shards)


def sum_at_once(grad):
    return lax.psum_scatter(grad, AXES, scatter_dimension=0, tiled=True)


SPREAD = 0.3275911
TAIL_COEFFICIENTS = (0.1850680112838745, 0.18050004541873932, 0.20733030140399933, 0.020621487870812416, 0.46248844265937805, -0.41615772247314453, 0.5027683973312378, -0.14261901378631592)


def normal_parts(u):
    t = 1.0 / (1.0 + (SPREAD * 2.0 ** -0.5) * jnp.abs(u))
    bell = jnp.exp2(u * u * (-0.5 / math.log(2.0)))
    total = jnp.full_like(t, 0.5 * TAIL_COEFFICIENTS[-1])
    for coefficient in TAIL_COEFFICIENTS[-2::-1]:
        total = total * t + 0.5 * coefficient
    tail = total * (t * bell)
    return jnp.where(u < 0, tail, 1.0 - tail), bell * (2.0 * math.pi) ** -0.5


def normalize(values):
    center = values - jnp.mean(values, axis=-1, keepdims=True)
    inverse = lax.rsqrt(jnp.mean(center * center, axis=-1, keepdims=True) + epsilon)
    return center * inverse, inverse


def norm_back(upstream, normed, inverse, gain):
    scaled = upstream * gain
    inner = jnp.mean(scaled, axis=-1, keepdims=True)
    cross = jnp.mean(scaled * normed, axis=-1, keepdims=True)
    result = inverse * (scaled - inner - normed * cross)
    sums = [jnp.sum(v, axis=0, keepdims=True) for v in (upstream * normed, upstream)]
    return result, sums


def store_blocks(grad, kept, refs, first):
    rows = grad.shape[0] // 8
    if kept is not None:
        kept[...] = grad.astype(bf16)
    for core, ref in enumerate(refs):
        for k, kind in enumerate(KINDS):
            if kept is None:
                at = rows * (4 * core + k)
                ref[first + k] = grad[at : at + rows].astype(bf16)
            else:
                at = pl.multiple_of(block_at(*kind, core) * rows, rows)
                ref[first + k] = kept[pl.ds(at, rows), :]


def stacked_rows(rows):
    spare = jnp.zeros((8 - len(rows), rows[0].shape[1]), f32)
    return jnp.concatenate([*rows, spare], 0)


def spread(count, width):
    return jnp.asarray(np.arange(width)[None] % count == np.arange(LANES)[:, None], bf16)


QV, PROJ_ADD, GAIN_ONE, SHIFT_ONE, GAIN_TWO, SHIFT_TWO, UP_ADD, DOWN_ADD = range(8)
HELD = (48, 24, 24, 24, 24, 24, 96, 24)


def row(ref, k):
    return ref[k : k + 1, :]


def vectors_kernel(*refs):
    pieces, spreads = refs[:8], refs[8:11]
    vecs_ref, up_add_ref, bias_ref, bias_v_ref = refs[11:]
    rows = jnp.concatenate([piece[:, 0:LANES] for piece in pieces], 0)
    whole = []
    for count, spread_ref in zip((24, 48, 96), spreads):
        wide = dot_nn(rows, spread_ref[...])
        total = jnp.zeros((SMALL, wide.shape[1]), f32)
        group = lax.broadcasted_iota(jnp.int32, total.shape, 1) // count
        for k in range(8):
            block = block_at(*KINDS[k % 4], k // 4)
            for col in range(4):
                at = SMALL * (4 * k + col)
                total = total + jnp.where(group == 4 * block + col, wide[at : at + SMALL], 0.0)
        whole.append(total)
    vecs_ref[...] = whole[0]
    up_add_ref[...] = whole[2]
    qv = whole[1][QV : QV + 1]
    width = vecs_ref.shape[1]
    bias_ref[...] = jnp.concatenate([qv[:, :width], jnp.zeros((1, width), f32), qv[:, width:]], 1)
    bias_v_ref[...] = jnp.broadcast_to(qv[:, width:], bias_v_ref.shape).astype(bf16)


def vectors(pieces):
    rows, width = pieces[0].shape
    spreads = [spread(count, 32 * count) for count in (24, 48, 96)]
    tail = pl.BlockSpec((4 * SMALL, width), lambda s: (rows // (4 * SMALL) - 1, 0))
    shapes = [((SMALL, width), f32), ((SMALL, 4 * width), f32), ((1, 3 * width), f32), ((8, width), bf16)]
    return pl.pallas_call(
        vectors_kernel,
        grid=(1,),
        in_specs=[tail] * 8 + [whole_spec(s) for s in spreads],
        out_specs=[pl.BlockSpec(shape, lambda s: (0, 0)) for shape, _ in shapes],
        out_shape=[jax.ShapeDtypeStruct(*shape) for shape in shapes],
        cost_estimate=cost(0),
        name="vectors",
    )(*pieces, *spreads)


def gathered_vectors(small):
    whole = [v.astype(f32) for v in gather_at_once(*small)]
    width = whole[PROJ_ADD].shape[0]
    none = jnp.zeros((width,), f32)
    vecs = jnp.stack([v if v.shape[0] == width else none for v in whole])
    up_add = jnp.broadcast_to(whole[UP_ADD][None], (SMALL, 4 * width))
    query, value = whole[QV][:width], whole[QV][width:]
    bias = jnp.concatenate([query, none, value])[None]
    return vecs, up_add, bias, jnp.broadcast_to(value[None], (8, width)).astype(bf16)


def assemble(target, pieces):
    for k, piece in enumerate(pieces):
        if piece is None:
            continue
        rows = piece.shape[-2]
        at = pl.multiple_of(block_at(*KINDS[k % 4], k // 4) * rows, rows)
        target[pl.ds(at, rows), :] = piece[...].reshape(rows, piece.shape[-1])


def qkv_ahead_kernel(x_ref, real_ref, vecs_ref, bias_ref, *refs):
    weight_refs, (hidden_ref, out_ref, w_ref) = refs[:-3], refs[-3:]

    @pl.when(pl.program_id(0) == 0)
    def _():
        plain, _ = normalize(x_ref[...].astype(f32))
        hidden = plain * row(vecs_ref, GAIN_ONE) + row(vecs_ref, SHIFT_ONE)
        hidden = hidden * real_ref[:, 0:1]
        hidden_ref[...] = hidden.astype(bf16)

    if len(weight_refs) == 1:
        w_ref[...] = weight_refs[0][...]
    else:
        assemble(w_ref, weight_refs)
    out_ref[...] = (dot_nn(hidden_ref[...], w_ref[...]) + bias_ref[...]).astype(bf16)


def join_rows(target, source, planes):
    rows = source.shape[2]
    at = 0
    for device in range(source.shape[0]):
        for plane in range(planes):
            target[at : at + rows, :] = source[device, plane]
            at += rows


def up_kernel(pieced, x_ref, a_ref, g_ref, vecs_ref, up_add_ref, w_ref, p_ref, *refs):
    middle_ref, second_ref, active_ref, slope_ref, proj_ref, mine_ref, other_ref, kept, up_ref = refs
    step = pl.program_id(0)

    @pl.when(step == 0)
    def _():
        if pieced:
            join_rows(proj_ref, p_ref, 1)
        else:
            proj_ref[...] = p_ref[...]
        middle = x_ref[...].astype(f32) + row(vecs_ref, PROJ_ADD)
        middle = middle + dot_nn(a_ref[...], proj_ref[...])
        plain, _ = normalize(middle)
        middle_ref[...] = middle
        second = plain * row(vecs_ref, GAIN_TWO) + row(vecs_ref, SHIFT_TWO)
        second_ref[...] = second.astype(bf16)

    if pieced:
        join_rows(up_ref, w_ref, 1)
    else:
        up_ref[...] = w_ref[...]
    width = up_ref.shape[1]
    chunks = [slice(at, at + width // 3) for at in range(0, width, width // 3)]
    second, g = second_ref[...], g_ref[...]
    add = row(up_add_ref, UP_ADD)
    inner = {0: dot_nn(second, up_ref[:, chunks[0]]) + add[:, chunks[0]]}
    for k, cut in enumerate(chunks):
        if k + 1 < len(chunks):
            inner[k + 1] = dot_nn(second, up_ref[:, chunks[k + 1]]) + add[:, chunks[k + 1]]
        below, density = normal_parts(inner[k])
        active = (inner[k] * below).astype(bf16)
        active_ref[:, cut] = active
        slope_ref[:, cut] = (below + inner[k] * density).astype(slope_ref.dtype)
        kept[cut, :] = dot_tn(active, g).astype(bf16)
    rows = mine_ref.shape[1]
    kind, first = step, 0
    if pieced:
        dp, rank = lax.axis_index("dp"), lax.axis_index("row")
        kind = (step // 2 + dp) % 2 + 2 * ((step + rank // 2) % 2)
        first = rank % 2
    for plane in range(4):
        for away, ref in enumerate((mine_ref, other_ref)):
            at = pl.multiple_of((first + away) % 2 * 4 * rows + rows * plane, rows)
            ref[4 * plane + kind] = kept[pl.ds(at, rows), :]


def mlp_back_kernel(
    pieced, active_ref, slope_ref, middle_ref, g_ref, vecs_ref, down_ref, up_ref, second_ref, a_ref,
    proj_ref, out_ref, mine_ref, other_ref, middle_grad_ref, attended_grad_ref, up_add_grad_ref,
    sums_ref, total, back, kept, turned, *weights,
):
    step = pl.program_id(0)
    last = pl.num_programs(0) - 1

    def store(grad):
        store_blocks(grad, kept if pieced else None, (mine_ref, other_ref), 0)

    @pl.when(step == 0)
    def _():
        total[...] = middle_ref[...] + row(vecs_ref, DOWN_ADD)
        back[...] = jnp.zeros_like(back)
        turned[...] = second_ref[...].T

    @pl.when(step < last)
    def _():
        if pieced:
            join_rows(weights[0], down_ref, 4)
            join_rows(weights[1], up_ref, 1)
            down, up = weights[0][...], weights[1][...]
        else:
            down, up = down_ref[...], up_ref[...]
        inner_grad = dot_nt(g_ref[...], down) * slope_ref[...].astype(f32)
        inner_grad = inner_grad.astype(bf16)
        up_add_grad_ref[...] = jnp.broadcast_to(
            jnp.sum(inner_grad.astype(f32), axis=0, keepdims=True), up_add_grad_ref.shape
        )
        total[...] += dot_nn(active_ref[...], down)
        back[...] += dot_nt(inner_grad, up)
        store(dot_nn(turned[...], inner_grad))

    @pl.when(step == last)
    def _():
        out_ref[...] = total[...].astype(bf16)
        plain, inverse = normalize(middle_ref[...])
        flow = g_ref[...].astype(f32)
        part, sums = norm_back(back[...], plain, inverse, row(vecs_ref, GAIN_TWO))
        middle_grad = flow + part
        middle_grad_ref[...] = middle_grad
        branch = middle_grad.astype(bf16)
        attended_grad_ref[...] = dot_nt(branch, proj_ref[...]).astype(bf16)
        store(dot_tn(a_ref[...], branch))
        column = lambda v: jnp.sum(v, axis=0, keepdims=True)
        sums_ref[...] = stacked_rows([*sums, column(branch.astype(f32)), column(flow)])


def qkv_back_kernel(
    pieced, swapped_ref, hidden_ref, d0_ref, d1_ref, w_ref, middle_grad_ref, x_ref, real_ref,
    vecs_ref, e0_ref, e1_ref, two_ref, up_ref, t0_ref, t1_ref,
    mine_ref, other_ref, images_grad_ref, small_ref, total, columns, kept, turned,
):
    step = pl.program_id(0)

    @pl.when(step == 0)
    def _():
        total[...] = jnp.zeros_like(total)
        turned[...] = hidden_ref[...].T

    back = jnp.concatenate([ref[0] for ref in (d0_ref, d1_ref)], 1)
    total[...] += dot_nt(back, w_ref[...])
    grad = dot_nn(turned[...], back)
    store_blocks(grad, kept if pieced else None, (mine_ref, other_ref), 0)
    columns[step] = jnp.broadcast_to(
        jnp.sum(back.astype(f32), axis=0, keepdims=True), columns.shape[1:]
    )

    @pl.when(step == pl.num_programs(0) - 1)
    def _():
        hidden_grad = total[...].astype(bf16).astype(f32) * real_ref[:, 0:1]
        plain, inverse = normalize(x_ref[...].astype(f32))
        part, sums = norm_back(hidden_grad, plain, inverse, row(vecs_ref, GAIN_ONE))
        images_grad_ref[...] = middle_grad_ref[...] + part
        small_sums(
            swapped_ref, columns, (e0_ref, e1_ref), two_ref, sums, up_ref,
            (t0_ref, t1_ref), small_ref,
        )


def whole_spec(array):
    return pl.BlockSpec(array.shape, lambda s: (0,) * array.ndim)


def across(rows, width):
    return pl.BlockSpec((rows, width), lambda s: (0, s))


BIG = pltpu.CompilerParams(vmem_limit_bytes=56 << 20)


def qkv_ahead(x, real, vecs, bias, weights):
    rows, width = x.shape
    shard = width // 8
    if len(weights) == 1:
        specs = [across(width, width)]
    else:
        specs = [pl.BlockSpec((shard, width), lambda s: (s, 0))] * 8
    return pl.pallas_call(
        qkv_ahead_kernel,
        grid=(3,),
        in_specs=[
            whole_spec(x), whole_spec(real), whole_spec(vecs), across(1, width), *specs,
        ],
        out_specs=[whole_spec(x), across(rows, width), across(width, width)],
        out_shape=[
            jax.ShapeDtypeStruct((rows, width), bf16),
            jax.ShapeDtypeStruct((rows, 3 * width), bf16),
            jax.ShapeDtypeStruct((width, 3 * width), bf16),
        ],
        compiler_params=BIG,
        cost_estimate=cost(5 * 10**9),
        name="qkv_ahead",
    )(x, real, vecs, bias, *weights)


def up_ahead(x, attended, g, vecs, up_add, weights):
    rows, width = x.shape
    pieced = len(weights) == 1
    if pieced:
        (planes,) = weights
        one = (planes.shape[0], 1, *planes.shape[2:])
        specs = [pl.BlockSpec(one, lambda s: (0, s, 0, 0)), pl.BlockSpec(one, lambda s: (0, 8, 0, 0))]
        weights = planes, planes
    else:
        specs = [across(width, width), whole_spec(weights[1])]
    shape = jax.ShapeDtypeStruct
    grad = shape((16, width // 8, width), bf16)
    outs = [
        (whole_spec(x), shape((rows, width), f32)),
        (whole_spec(x), shape((rows, width), bf16)),
        (across(rows, width), shape((rows, 4 * width), bf16)),
        (across(rows, width), shape((rows, 4 * width), bf16)),
        (pl.BlockSpec((width, width), lambda s: (0, 0)), shape((width, width), bf16)),
        (whole_spec(grad), grad),
        (whole_spec(grad), grad),
    ]
    return pl.pallas_call(
        lambda *refs: up_kernel(pieced, *refs),
        grid=(4,),
        in_specs=[
            whole_spec(x), whole_spec(attended), whole_spec(g), whole_spec(vecs), across(8, width),
            *specs,
        ],
        out_specs=[spec for spec, _ in outs],
        out_shape=[out for _, out in outs],
        scratch_shapes=[pltpu.VMEM((width, width), bf16), pltpu.VMEM((width, width), bf16)],
        compiler_params=BIG,
        cost_estimate=cost(0),
        name="up_ahead",
    )(x, attended, g, vecs, up_add, *weights)


def mlp_back(active, slope, middle, g, vecs, weights, second, attended, proj):
    rows, width = second.shape
    shard = width // 8
    shape = jax.ShapeDtypeStruct
    upto = lambda s: jnp.minimum(s, 3)
    along = lambda count: pl.BlockSpec((count, width), lambda s: (0, upto(s)))
    pieced = len(weights) == 1
    scratch = [
        pltpu.VMEM((rows, width), f32), pltpu.VMEM((rows, width), f32),
        pltpu.VMEM((width, width), bf16), pltpu.VMEM((width, rows), bf16),
    ]
    if pieced:
        (planes,) = weights
        devices, _, *tile = planes.shape
        specs = [
            pl.BlockSpec((devices // 4, 4, *tile), lambda s: (upto(s), 1, 0, 0)),
            pl.BlockSpec((devices, 1, *tile), lambda s: (0, upto(s), 0, 0)),
        ]
        weights = planes, planes
        scratch += [pltpu.VMEM((width, width), bf16)] * 2
    else:
        specs = [pl.BlockSpec((width, width), lambda s: (upto(s), 0)), along(width)]
    sums = shape((8, width), f32)
    block = pl.BlockSpec((4, shard, width), lambda s: (s, 0, 0))
    blocks = shape((4 * 5, shard, width), bf16)
    still = lambda a: pl.BlockSpec(a.shape, lambda s: (0,) * a.ndim, pipeline_mode=pl.Buffered(1))
    outs = [
        (whole_spec(second), shape((rows, width), bf16)),
        (block, blocks),
        (block, blocks),
        (whole_spec(second), shape((rows, width), f32)),
        (whole_spec(second), shape((rows, width), bf16)),
        (along(8), shape((8, 4 * width), f32)),
        (whole_spec(sums), sums),
    ]
    return pl.pallas_call(
        lambda *refs: mlp_back_kernel(pieced, *refs),
        grid=(5,),
        in_specs=[
            along(rows), along(rows), still(middle), still(g), whole_spec(vecs), *specs,
            still(second), still(attended), still(proj),
        ],
        out_specs=[spec for spec, _ in outs],
        out_shape=[out for _, out in outs],
        scratch_shapes=scratch,
        compiler_params=BIG,
        cost_estimate=cost(0),
        name="mlp_back",
    )(active, slope, middle, g, vecs, *weights, second, attended, proj)


def qkv_back(hidden, pieces, weight, middle_grad, x, real, vecs, swapped, small, pieced):
    rows, width = x.shape
    shard = width // 8
    extra, two, up, tables = small
    whole = lambda a: pl.BlockSpec(a.shape, lambda s, w: (0,) * len(a.shape))
    planes = jax.ShapeDtypeStruct((12, shard, width), bf16)
    block = pl.BlockSpec((4, shard, width), lambda s, w: (s, 0, 0))
    outs = [jax.ShapeDtypeStruct((rows, width), f32), jax.ShapeDtypeStruct((SUM_ROWS, width), f32)]
    return pl.pallas_call(
        lambda *refs: qkv_back_kernel(pieced, *refs),
        grid_spec=pltpu.PrefetchScalarGridSpec(
            num_scalar_prefetch=1,
            grid=(3,),
            in_specs=[
                whole(hidden),
                *[pl.BlockSpec((1, *p.shape[1:]), lambda s, w: (s, 0, 0)) for p in pieces],
                pl.BlockSpec((width, width), lambda s, w: (0, s)),
                *[whole(a) for a in (middle_grad, x, real, vecs, *extra, two, up, *tables)],
            ],
            out_specs=[block, block, *[whole(out) for out in outs]],
            scratch_shapes=[
                pltpu.VMEM((rows, width), f32),
                pltpu.VMEM((3, 8, width), f32),
                pltpu.VMEM((width, width), bf16),
                pltpu.VMEM((width, rows), bf16),
            ],
        ),
        out_shape=[planes, planes, *outs],
        compiler_params=BIG,
        cost_estimate=cost(0),
        name="qkv_back",
    )(swapped, hidden, *pieces, weight, middle_grad, x, real, vecs, *extra, two, up, *tables)


SUM_ROWS = 24
SUM_AT = dict(query=0, value=1, proj=2, pre=3, mid=5, up=7, down=11, tables=16)


def small_sums(swapped_ref, column_ref, extra_refs, two_ref, one, up_ref, table_refs, out_ref):
    width = out_ref.shape[1]
    out_ref[...] = jnp.zeros_like(out_ref)

    def put(name, value, more=0):
        at = SUM_AT[name] + more
        out_ref[at : at + 1, :] = value

    put("query", column_ref[0, 0:1, :])
    extra = jnp.concatenate([ref[p, 0:1, :] for ref in extra_refs for p in range(ref.shape[0])], 1)
    put("value", column_ref[2, 0:1, :] + extra)
    put("proj", two_ref[2:3, :])
    for k in range(2):
        put("pre", one[k], k)
        put("mid", two_ref[k : k + 1, :], k)
    for k in range(4):
        put("up", up_ref[0:1, width * k : width * (k + 1)], k)
    put("down", two_ref[3:4, :])
    count = 32
    sums = [jnp.zeros((count, HEAD), f32) for _ in range(2)]
    for s in range(table_refs[0].shape[0]):
        grad = table_refs[0][s]
        for ref in table_refs[1:]:
            grad = grad + ref[s]
        both = (grad[:HEAD, HEAD:] + grad[HEAD:, :HEAD]).T
        parts = (both[:count], both[COLTABLE : COLTABLE + count])
        swap = swapped_ref[s] != 0
        sums[0] = sums[0] + jnp.where(swap, parts[1], parts[0])
        sums[1] = sums[1] + jnp.where(swap, parts[0], parts[1])
    tables = jnp.concatenate(sums, 1)
    at = SUM_AT["tables"]
    for k in range(4):
        out_ref[at : at + 8, LANES * k : LANES * (k + 1)] = tables[8 * k : 8 * k + 8]


def split_sums(total):
    count = lax.axis_size("dp") * lax.axis_size("row") * lax.axis_size("col")
    width = total.shape[1]

    def share(name, more=0, rows=1):
        at = SUM_AT[name] + more
        size = rows * width // count
        return lax.dynamic_slice(total[at : at + rows].reshape(-1), (device_number() * size,), (size,))

    at = SUM_AT["tables"]
    tables = jnp.concatenate([total[at : at + 8, LANES * k : LANES * (k + 1)] for k in range(4)], 0)
    tables = tables[: 2 * WIN - 1]
    vectors = (
        share("query", 0, 2), share("proj"), share("pre"), share("pre", 1), share("mid"),
        share("mid", 1), share("up", 0, 4), share("down"),
    )
    return vectors, (tables[:, :HEAD], tables[:, HEAD:])


def body(
    images, qkv_weight, qv_bias, proj_weight, proj_bias, pre_gain, pre_shift, mid_gain, mid_shift,
    up_weight, up_bias, down_weight, down_bias, rel_rows, rel_cols, cotangent,
):
    width = images.shape[-1]
    torus = on_torus()
    plan = plan_for(lax.axis_size("row"), lax.axis_size("col"), images.shape[0] * images.shape[1])
    move = Mover(plan)
    counts = plan.counts
    groups = ((0, 4), (4, 2))
    small = (qv_bias, proj_bias, pre_gain, pre_shift, mid_gain, mid_shift, up_bias, down_bias)
    pixels, cot = images.reshape(-1, width), cotangent.reshape(-1, width)
    swapped = move.swapped

    if torus:
        shard, planes = sent_shards(qkv_weight, up_weight, down_weight, proj_weight, small)
        first_steps = Steps(first_weights(shard))
        first_steps()
        (planes,) = gather_at_once(planes)
        weights = (planes,)
        sent = move.send(move.pack(pixels, cot))
        rel_rows, rel_cols = first_steps(rel_rows, rel_cols)
        tables, tables_back = position_tables(swapped, rel_rows, rel_cols)
        sent, tables = first_steps(sent, tables)
        x, g, real = move.receive(pixels, cot, arrived=sent, masked=True)
        qkv = first_steps.arrays
        vecs, up_add, bias, bias_v = vectors(qkv)
    else:
        sent = move.send(move.pack(pixels, cot))
        x, g, real = move.receive(pixels, cot, arrived=sent, masked=True)
        whole_qkv, *weights = gather_at_once(qkv_weight, up_weight, proj_weight, down_weight)
        qkv = (whole_qkv,)
        tables, tables_back = position_tables(swapped, rel_rows, rel_cols)
        vecs, up_add, bias, bias_v = gathered_vectors(small)

    hidden, projected, qkv = qkv_ahead(x, real, vecs, bias, qkv)
    attended, logsum = attend(projected, bias_v, tables, counts, 0, 6)
    middle, second, active, slope, proj, mine, other = up_ahead(
        x, attended, g, vecs, up_add, weights[:2] if len(weights) == 3 else weights
    )
    idle = lambda *values: values if len(values) != 1 else values[0]
    down_steps = up_sum = idle
    if torus:
        down_steps = Steps(halves_sum(mine, other))
    else:
        blocks = [v.reshape(4, 4, -1, width).swapaxes(0, 1) for v in (mine, other)]
        down_grad = jnp.stack(blocks, 1).reshape(-1, width)
    middle, second, active, slope = down_steps(middle, second, active, slope)
    middle, second, active, slope = down_steps(middle, second, active, slope)
    middle, second, active, slope = down_steps(middle, second, active, slope)
    result, *outs = mlp_back(
        active, slope, middle, g, vecs, (weights[2], weights[0]) if len(weights) == 3 else weights, second,
        attended, proj,
    )
    mine, other, middle_grad, attended_grad, up_add_grad, sums_two = down_steps(*outs)
    if torus:
        up_sum = Steps(scatter_sum(mine, other, 5))
    else:
        blocks = jnp.concatenate([mine.reshape(5, 4, -1, width), other.reshape(5, 4, -1, width)], 1)
        blocks = blocks.reshape(5, width, width)
        up_grad, proj_grad = jnp.swapaxes(blocks[:4], 0, 1).reshape(width, -1), blocks[4]
    attended_grad = up_sum(attended_grad)
    attended_grad = down_steps(attended_grad)
    attended_grad = up_sum(attended_grad)
    attended_grad = up_sum(attended_grad)
    pieces, table_grads, extra = [], [], []
    for first, count in groups:
        one, two, three = attend_back(
            projected, attended_grad, logsum[first : first + count], bias_v, tables, tables_back,
            counts, first,
        )
        pieces.append(one)
        table_grads.append(two)
        extra.append(three)
        attended_grad, pieces[-1] = order(attended_grad, one)
        if first == 0:
            attended_grad = down_steps(attended_grad)
            attended_grad = down_steps(attended_grad)
    if torus:
        pieces = up_sum(*pieces)
        pieces = up_sum(*pieces)
    small = extra, sums_two, up_add_grad, table_grads
    mine, other, images_grad, sums = qkv_back(
        hidden, pieces, qkv, middle_grad, x, real, vecs, swapped, small, torus
    )
    if torus:
        mine, other, images_grad, sums = up_sum(mine, other, images_grad, sums)
        mine, other, images_grad, sums = down_steps(mine, other, images_grad, sums)
        up_grad, proj_grad = up_sum.arrays
        (down_grad,) = down_steps.arrays
        qkv_sum = Steps(scatter_sum(mine, other, 3))
        images_grad, sums = qkv_sum(images_grad, sums)
        images_grad = qkv_sum(images_grad, more=(sums, over_core(sums)))
        images_grad = qkv_sum(images_grad)
        result, images_grad, up_grad, proj_grad, down_grad = order(
            result, images_grad, up_grad, proj_grad, down_grad
        )
        sent = move.send_back(move.pack_back(result, images_grad))
        result = qkv_sum(result)
        result = qkv_sum(result)
        out, images_grad = move.receive_back(result, images_grad, arrived=sent)
        out = qkv_sum(out)
        qkv_weight_grad, sums = qkv_sum.arrays
    else:
        blocks = jnp.concatenate(
            [mine.reshape(3, 4, -1, width), other.reshape(3, 4, -1, width)], 1
        ).reshape(3, width, width)
        qkv_weight_grad = jnp.swapaxes(blocks, 0, 1).reshape(width, -1)
        sent = move.send_back(move.pack_back(result, images_grad))
        out, images_grad = move.receive_back(result, images_grad, arrived=sent)
        sums = lax.psum(sums, AXES)
        qkv_weight_grad, proj_grad, up_grad, down_grad = [
            sum_at_once(g.astype(f32)) for g in (qkv_weight_grad, proj_grad, up_grad, down_grad)
        ]
    mine, full = split_sums(sums)
    return (
        out.reshape(images.shape),
        images_grad.reshape(images.shape),
        qkv_weight_grad,
        mine[0],
        proj_grad,
        mine[1],
        mine[2],
        mine[3],
        mine[4],
        mine[5],
        up_grad,
        mine[6],
        down_grad,
        mine[7],
        full[0],
        full[1],
    )


PLANS = {}


def plan_for(rows, cols, images):
    key = (rows, cols, images)
    if key not in PLANS:
        PLANS[key] = Plan(*key)
    return PLANS[key]


def solution(mesh):
    tokens = P(None, "dp", "row", "col", None)
    rows = P(AXES, None)
    vector = P(AXES)
    placed = (
        tokens, rows, vector, rows, vector, vector, vector, vector, vector,
        rows, vector, rows, vector, P(), P(), tokens,
    )
    given = (tokens, tokens, rows, vector, rows, vector, vector, vector, vector, vector,
             rows, vector, rows, vector, P(), P())
    return jax.shard_map(body, mesh=mesh, in_specs=placed, out_specs=given, check_vma=False)
```
